128 devices in a mesh: sph: 16 (over z, x_hi, core), fv: 8 (over x_lo, y).
Axes of the slice: x: 4 (x_hi: 2, x_lo: 2; x = x_hi * 2 + x_lo), y: 4, z: 4, core: 2. Of those that a mesh axis runs over, the one named last changes fastest.
Arguments:
- positions: float32 [3, 262144], P(None, ('sph', 'fv')), may hold values from -6 to 6
- particle_temp: float32 [262144], P(('sph', 'fv')), may hold values from -6 to 6
- volume: float32 [262144], P(('sph', 'fv')), may hold values from 0.001953125 to 0.0078125
- nbr_blocks: int32 [1024, 16], P(('sph', 'fv')), may hold values from 0 to 1023, as said below
- nbr_count: int32 [1024], P(('sph', 'fv')), may hold values from 1 to 16, as said below
- iface_part: int32 [131072], P(('sph', 'fv')), may hold values from 0 to 2047
- iface_owner: int32 [131072, 1], P(('sph', 'fv')), may hold values from 0 to 127; in each aligned block of 1024 rows (0 to 1023, 1024 to 2047, ...) at most 16 rows name the same one
- iface_cell: int32 [131072], P(('sph', 'fv')), may hold values from 0 to 8191
- substrate_temp: float32 [32, 512, 2048], P(None, 'sph', 'fv'), may hold values from -6 to 6
- conduct: float32 [32, 512, 2048], P(None, 'sph', 'fv'), may hold values from 0.5 to 1
- laser_cells: int32 [256], replicated, may hold values from 0 to 1048575
- laser_power: float32 [256], replicated, may hold values from 0.5 to 4
Outputs:
- particle_out: float32 [262144], P(('sph', 'fv'))
- substrate_out: float32 [32, 512, 2048], P(None, 'sph', 'fv')
The draws below stay inside these ranges and needn't reach their ends.
Inputs may be any that keep to these rules, and one draw needn't show every extreme that they name: `nbr_blocks`: row b lists global block numbers within 8 of b; its first nbr_count[b] entries are distinct and begin with b, the others equal b. `nbr_count`: blocks near the beam have up to 16 live slots, the others far fewer; some block has exactly 16. `iface_owner`: among the 1024 entries of one device at most 16 name the same owner, and in some device exactly 16 do.
All inputs are finite; a program needn't handle non-finite values.
Results may differ from the reference program's by a relative error of at most 0.0001.
Values sent between devices are 32-bit elements; how exact they have to be, the bound alone decides.
A program may use at most 128 MiB of HBM per device.

```python
import math
import jax
import jax.numpy as jnp
import numpy as np
from jax import lax

PB = 256
BLK_DEV = 8
KN = 16
IF_DEV = 1024
CX = 32
CY = 256
GZ = 32
SUB = 4
TRACK = 256
OWNERS = 128
CAP = 16
P_DEV = 2048
NBLK = 1024
NP = 262144
IFACE = 131072
GX = 512
GY = 2048
N_FV = 8


def neighbour_table(rng_key):
    window = 2 * BLK_DEV + 1
    beam_block = jax.random.randint(jax.random.fold_in(rng_key, 11), (), BLK_DEV, NBLK - BLK_DEV)
    keys_all = jax.random.split(jax.random.fold_in(rng_key, 12), NBLK)
    shuffled = jax.vmap(lambda one_key: jax.random.permutation(one_key, window))(keys_all).astype(jnp.int32)
    offsets = jnp.arange(window, dtype=jnp.int32) - BLK_DEV
    block_ids = jnp.arange(NBLK, dtype=jnp.int32)
    candidate = block_ids[:, None] + offsets[None, :]
    inside = (candidate >= 0) & (candidate < NBLK)
    scores = jnp.where(offsets[None, :] == 0, -1, jnp.where(inside, shuffled, window + shuffled))
    order_ids = jnp.argsort(scores, axis=1)
    chosen = jnp.take_along_axis(candidate, order_ids, 1)[:, :KN]
    usable = jnp.sum(inside.astype(jnp.int32), axis=1)
    quiet_count = jax.random.randint(jax.random.fold_in(rng_key, 13), (NBLK,), max(1, KN // 8), KN // 4 + 1)
    near_beam = jnp.abs(block_ids - beam_block) <= BLK_DEV // 2
    live_count = jnp.minimum(jnp.where(near_beam, KN, quiet_count), usable)
    slot_ids = jnp.arange(KN, dtype=jnp.int32)
    block_table = jnp.where(slot_ids[None, :] < live_count[:, None], chosen, block_ids[:, None])
    return (block_table.astype(jnp.int32), live_count.astype(jnp.int32))


def draw_nbr_blocks(key, part):
    return neighbour_table(key)[0]


def draw_nbr_count(key, part):
    return neighbour_table(key)[1]


def plant(array, rng, smallest, high):
    shape = array.shape
    spot = [jax.random.randint(jax.random.fold_in(rng, axis), (), 0, shape[axis]) for axis in range(len(shape))]
    array = array.at[tuple(spot)].set(smallest)
    longest = shape.index(max(shape))
    spot[longest] = (spot[longest] + 1) % shape[longest]
    return array.at[tuple(spot)].set(high)


def steps_of(key, shape, cuts, least, high):
    def one(axis_at, blocks):
        draws = jax.random.uniform(jax.random.fold_in(jax.random.fold_in(key, 6), axis_at), (blocks,), jnp.float32, least / len(cuts), high / len(cuts))
        return jnp.repeat(jnp.exp(draws), shape[axis_at] // blocks).reshape((-1,) + (1,) * (len(shape) - axis_at - 1))

    gain = one(*cuts[0])
    for cut in cuts[1:]:
        gain = gain * one(*cut)
    return gain


def shared_out(rng, own, number, rows, amount, top, most, slope):
    order = jax.random.permutation(rng, amount)
    crowded, ordinary = portions_of(amount, rows * top, most, slope, True), portions_of(amount, rows * top, most, slope, False)
    places = jnp.arange(amount)

    def named(tallies, turn):
        used = int((tallies > 0).sum())
        fixed = max(1, used // 4)
        passed = fixed + (places - fixed + turn * (used - fixed)) % max(1, amount - fixed)
        return jnp.zeros((amount,), jnp.int32).at[order[jnp.where(places < fixed, places, passed)]].set(jnp.asarray(tallies, jnp.int32))

    tallies = jnp.where(number % 4 == 0, named(crowded, number // 4), named(ordinary, number - number // 4 - 1))
    mixed = jax.random.permutation(jax.random.fold_in(own, 3), amount)
    donor, sink = mixed[0:amount // 2 * 2:2], mixed[1:amount // 2 * 2:2]
    room = jnp.minimum(tallies[donor] - 1, most - tallies[sink]) // 2
    room = jnp.where((donor == order[0]) | (sink == order[0]) | (tallies[sink] == 0), 0, jnp.maximum(room, 0))
    passed = jax.random.randint(jax.random.fold_in(own, 4), (amount // 2,), 0, 1 << 20) % (room + 1)
    tallies = tallies.at[donor].add(-passed).at[sink].add(passed)
    items = jnp.searchsorted(jnp.cumsum(tallies), jnp.arange(rows * top), side="right").astype(jnp.int32)
    grid = items.reshape(top, rows).T
    grid = grid[jax.random.permutation(jax.random.fold_in(own, 1), rows)]
    turn = jax.random.randint(jax.random.fold_in(own, 2), (rows, 1), 0, top)
    return jnp.take_along_axis(grid, (jnp.arange(top)[None, :] + turn) % top, axis=1)


def portions_of(amount, total, bound, skew, full):
    weights = [(1 << 20) // math.isqrt(grade ** skew) + 1 for grade in range(1, amount + 1)]
    largest = bound if full else min(bound, max(-(-total // amount), total * weights[0] // sum(weights)))
    least = 1 if total - largest >= amount - 1 else 0
    holding, spare = [largest] + [least] * (amount - 1), total - largest - least * (amount - 1)
    while spare > 0:
        free = [i for i in range(1, amount) if holding[i] < largest] or [i for i in range(1, amount) if holding[i] < bound]
        whole, remaining = sum([weights[i] for i in free]), spare
        for i in free:
            more = min(bound - holding[i], max(1, remaining * weights[i] // whole), spare)
            holding[i] = holding[i] + more
            spare = spare - more
    return np.array(holding)


def centred(key, shape, scale, most, shards=(), kind=jnp.bfloat16):
    level = steps_of(key, shape, shards, -0.22, 0.18) if shards else 1.0
    array = jax.random.normal(key, shape, jnp.float32) * scale * level
    return jnp.minimum(jnp.maximum(array, -most), most).astype(kind)


def setup_inputs(seed: int = 0) -> dict:
    splits = jax.random.split(jax.random.key(seed), 13)
    positions = centred(splits[0], (3, NP), 1.0, 6.0, ((1, 128),), jnp.float32)
    particle_temp = centred(splits[1], (NP,), 1.0, 6.0, ((0, 128),), jnp.float32)
    volume = jnp.clip(jnp.exp(math.log(0.0078125) - 1.3862944 * jax.random.uniform(splits[2], (NP,), jnp.float32) ** steps_of(splits[2], (NP,), ((0, 128),), -0.2, 0.2)), 0.001953125, 0.0078125)
    nbr_blocks = draw_nbr_blocks(jax.random.fold_in(splits[12], 71), 0)
    nbr_count = draw_nbr_count(jax.random.fold_in(splits[12], 71), 0)
    iface_part = plant(jax.random.randint(splits[5], (IFACE,), 0, P_DEV), jax.random.fold_in(splits[5], 1), 0, P_DEV - 1).astype(jnp.int32)
    iface_owner_keys = jax.random.split(jax.random.fold_in(splits[6], 1), IFACE // IF_DEV)
    iface_owner_turns = jax.random.permutation(jax.random.fold_in(splits[6], 3), IFACE // IF_DEV)
    iface_owner = jax.vmap(lambda own, number: shared_out(jax.random.fold_in(splits[6], 2), own, number, IF_DEV, OWNERS, 1, CAP, 2))(iface_owner_keys, iface_owner_turns).reshape((IFACE, 1))
    iface_cell = plant(jax.random.randint(splits[7], (IFACE,), 0, CX * CY), jax.random.fold_in(splits[7], 1), 0, (CX * CY) - 1).astype(jnp.int32)
    substrate_temp = centred(splits[8], (GZ, GX, GY), 1.0, 6.0, ((1, 16), (2, 8)), jnp.float32)
    conduct = jnp.clip(0.5 + 0.5 * jax.random.uniform(splits[9], (GZ, GX, GY), jnp.float32) ** steps_of(splits[9], (GZ, GX, GY), ((1, 16), (2, 8)), -0.2, 0.2), 0.5, 1.0)
    laser_cells = plant(jax.random.randint(splits[10], (TRACK,), 0, GX * GY), jax.random.fold_in(splits[10], 1), 0, (GX * GY) - 1).astype(jnp.int32)
    laser_power = jnp.clip(jnp.exp(jax.random.uniform(splits[11], (TRACK,), jnp.float32, math.log(0.5), math.log(4.0))), 0.5, 4.0)
    return {"positions": positions, "particle_temp": particle_temp, "volume": volume, "nbr_blocks": nbr_blocks, "nbr_count": nbr_count, "iface_part": iface_part, "iface_owner": iface_owner, "iface_cell": iface_cell, "substrate_temp": substrate_temp, "conduct": conduct, "laser_cells": laser_cells, "laser_power": laser_power}


KERNEL_SCALE = 0.5
SPH_STEP = 0.05
CONTACT_GAIN = 1.0
PARTICLE_SHARE = 0.5
SURFACE_GAIN = 0.5
LAMBDA_STEP = 0.1


def pair_heat(own_blocks, other_blocks):
    diff_x = own_blocks[:, 0, :, None] - other_blocks[:, 0, None, :]
    diff_y = own_blocks[:, 1, :, None] - other_blocks[:, 1, None, :]
    diff_z = own_blocks[:, 2, :, None] - other_blocks[:, 2, None, :]
    distance = diff_x * diff_x + diff_y * diff_y + diff_z * diff_z
    kernel = jnp.exp(-distance * KERNEL_SCALE) * (2.0 * KERNEL_SCALE)
    own_k = 1.0 + 0.5 * jnp.tanh(own_blocks[:, 3])
    other_k = 1.0 + 0.5 * jnp.tanh(other_blocks[:, 3])
    harmonic = 2.0 * own_k[:, :, None] * other_k[:, None, :] / (own_k[:, :, None] + other_k[:, None, :])
    change = other_blocks[:, 3, None, :] - own_blocks[:, 3, :, None]
    return jnp.sum(other_blocks[:, 4, None, :] * harmonic * change * kernel, axis=2)


def conduct_step(field, coef):
    conduct_now = coef * (1.0 + 0.5 * jnp.tanh(field))
    center = field[:, 1:-1, 1:-1]
    center_k = conduct_now[:, 1:-1, 1:-1]
    summed = jnp.zeros_like(center)
    lateral = ((field[:, 2:, 1:-1], conduct_now[:, 2:, 1:-1]), (field[:, :-2, 1:-1], conduct_now[:, :-2, 1:-1]),
               (field[:, 1:-1, 2:], conduct_now[:, 1:-1, 2:]), (field[:, 1:-1, :-2], conduct_now[:, 1:-1, :-2]))
    for side_u, side_k in lateral:
        summed = summed + 0.5 * (center_k + side_k) * (side_u - center)
    below = jnp.concatenate([center[1:], jnp.zeros_like(center[:1])], 0)
    below_k = jnp.concatenate([center_k[1:], center_k[-1:]], 0)
    summed = summed + 0.5 * (center_k + below_k) * (below - center)
    above = jnp.concatenate([center[:1], center[:-1]], 0)
    above_k = jnp.concatenate([center_k[:1], center_k[:-1]], 0)
    summed = summed + 0.5 * (center_k + above_k) * (above - center)
    return center + LAMBDA_STEP * summed


def pair_group(grouped):
    return pair_heat(grouped[0], grouped[1])


def reference(positions, particle_temp, volume, nbr_blocks, nbr_count, iface_part, iface_owner, iface_cell, substrate_temp, conduct, laser_cells, laser_power):
    packed = jnp.concatenate([positions, particle_temp[None], volume[None]], 0)
    blocks = packed.reshape(5, NBLK, PB).transpose(1, 0, 2)
    groups = NBLK // BLK_DEV

    def add_slot(slot, summed):
        column = lax.dynamic_index_in_dim(nbr_blocks, slot, 1, keepdims=False)
        other = jnp.take(blocks, column, axis=0)
        paired = lax.map(pair_group, (blocks.reshape(groups, BLK_DEV, 5, PB), other.reshape(groups, BLK_DEV, 5, PB)))
        live = slot < nbr_count
        return summed + jnp.where(live[:, None], paired.reshape(NBLK, PB), 0.0)

    heat_in = lax.fori_loop(0, KN, add_slot, jnp.zeros((NBLK, PB), jnp.float32)).reshape(NP)

    owner_dev = iface_owner[:, 0]
    grid_x = (owner_dev // N_FV) * CX + iface_cell // CY
    grid_y = (owner_dev % N_FV) * CY + iface_cell % CY
    flat_cell = (grid_x * GY + grid_y).astype(jnp.int32)
    ghost_temp = jnp.take(substrate_temp[0].reshape(GX * GY), flat_cell)
    particle_ids = ((jnp.arange(IFACE, dtype=jnp.int32) // IF_DEV) * P_DEV + iface_part).astype(jnp.int32)
    contact = CONTACT_GAIN * (jnp.take(particle_temp, particle_ids) - ghost_temp)
    cell_flux = jnp.zeros((GX * GY,), jnp.float32).at[flat_cell].add(contact)
    laser_heat = jnp.zeros((GX * GY,), jnp.float32).at[laser_cells].add(laser_power)
    top_layer = substrate_temp[0] + SURFACE_GAIN * (cell_flux + laser_heat).reshape(GX, GY)
    field = jnp.concatenate([top_layer[None], substrate_temp[1:]], 0)
    coef_pad = jnp.pad(conduct, ((0, 0), (1, 1), (1, 1)))
    for section in range(SUB):
        field = conduct_step(jnp.pad(field, ((0, 0), (1, 1), (1, 1))), coef_pad)
    particle_flux = jnp.zeros((NP,), jnp.float32).at[particle_ids].add(contact)
    particle_out = particle_temp + SPH_STEP * heat_in - PARTICLE_SHARE * particle_flux
    return particle_out, field
```

```python
import functools

import jax
import jax.numpy as jnp
from jax import lax
from jax.experimental import pallas as pl
from jax.experimental.pallas import tpu as pltpu
from jax.sharding import PartitionSpec as P

SUB = 4
KERNEL_SCALE = 0.5
SPH_STEP = 0.05
CONTACT_GAIN = 1.0
PARTICLE_SHARE = 0.5
SURFACE_GAIN = 0.5
LAMBDA_STEP = 0.1
NS, NF = 16, 8
CX, CY, GZ = 32, 256, 32
BX, BY = 40, 384
PB, NB, KN, CAP = 256, 8, 16, 16
PD, NE = 2048, 1024
MESH = pl.DeviceIdType.MESH
F32, BF = jnp.float32, jnp.bfloat16
LOG2E = 1.4426950408889634


def split3(x):
    a = x.astype(BF)
    r = x - a.astype(F32)
    b = r.astype(BF)
    c = (r - b.astype(F32)).astype(BF)
    return a, b, c


def dot(a, b, ca, cb):
    return lax.dot_general(a, b, (((ca,), (cb,)), ((), ())), preferred_element_type=F32)


def iota(shape, dim):
    return lax.broadcasted_iota(jnp.int32, shape, dim)


def hot(rows, row_index):
    return jnp.where(iota((rows, row_index.shape[1]), 0) == row_index, 1.0, 0.0)


def main_kernel(
    pos, temp1, temp16, vol, ipart, iown, icell, lcell, lpow, sub, cond,
    out, ext_out, pflux_out,
    U, C, surf, top, ty, pk_s, pk_r, send1, recv1, send2, recv2, rsend1, rret1, rsend2, rret2,
    pt, qt, ohp_lo, fz_ref, kring, pack, lsem, ssem, rsem,
):
    S = lax.axis_index("sph")
    F = lax.axis_index("fv")
    sn, sp = (S + 1) % NS, (S + NS - 1) % NS
    fn, fp = (F + 1) % NF, (F + NF - 1) % NF

    barrier = pltpu.get_barrier_semaphore()
    partners = [(S, (F + d) % NF) for d in range(1, NF)]
    partners += [((S + d) % NS, F) for d in range(1, NS)]
    partners += [(sn, fn), (sn, fp), (sp, fn), (sp, fp)]
    for who in partners:
        pl.semaphore_signal(barrier, inc=1, device_id=who, device_id_type=MESH)

    lc = [
        pltpu.make_async_copy(sub.at[0], surf, lsem.at[0]),
        pltpu.make_async_copy(sub.at[pl.ds(1, GZ - 1)], U.at[0, pl.ds(1, GZ - 1), pl.ds(0, CX), pl.ds(0, CY)], lsem.at[1]),
        pltpu.make_async_copy(cond, C.at[:, pl.ds(0, CX), pl.ds(0, CY)], lsem.at[2]),
    ]
    for c in lc:
        c.start()

    count = [0]

    def remote(src, dst, who):
        i = count[0]
        count[0] += 1
        c = pltpu.make_async_remote_copy(
            src_ref=src, dst_ref=dst, send_sem=ssem.at[i], recv_sem=rsem.at[i],
            device_id=who, device_id_type=MESH)
        c.start()
        return c

    pack[...] = jnp.concatenate([pos[...], temp1[...], vol[...], jnp.zeros((3, PD), F32)], 0)

    own = iown[...]
    row_of = (own % NF) * NS + own // NF
    part = ipart[...]
    php = hot(16, part // 128).astype(BF)
    plo = hot(128, part % 128)
    ohp_lo[...] = plo.astype(BF)
    t0, t1, t2 = split3(temp16[...])
    g = dot(t0, php, 0, 0) + dot(t1, php, 0, 0) + dot(t2, php, 0, 0)
    tval = jnp.sum(g * plo, axis=0, keepdims=True)
    po = hot(128, row_of)
    pb = po.astype(BF)
    pt[...] = pb
    tri = jnp.where(iota((256, 256), 0) < iota((256, 256), 1), 1.0, 0.0).astype(BF)
    ones = jnp.ones((256, 256), BF)
    run = jnp.zeros((128, 256), F32)
    ranks = []
    for k in range(NE // 256):
        pc = pb[:, k * 256:(k + 1) * 256]
        cum = dot(pc, tri, 1, 0) + run
        run = run + dot(pc, ones, 1, 0)
        ranks.append(jnp.sum(cum * po[:, k * 256:(k + 1) * 256], axis=0, keepdims=True))
    rank = jnp.concatenate(ranks, 1)
    q = jnp.where(iota((CAP, NE), 0).astype(F32) == rank, 1.0, 0.0)
    qt[...] = q
    c1 = icell[...] + 1
    chi = (c1 // 256 * 256).astype(F32)
    clo = (c1 % 256).astype(F32)
    v0, v1, v2 = split3(tval)
    zero = jnp.zeros((96, NE), BF)
    zq = jnp.zeros((CAP, NE), F32)

    def rows(a, b):
        return jnp.concatenate([jnp.concatenate([a, b], 0).astype(BF), zero], 0)

    send1[...] = (
        dot(pb, rows(q * chi, q * v0.astype(F32)), 1, 1)
        + dot(pb, rows(q * clo, q * v1.astype(F32)), 1, 1)
        + dot(pb, rows(zq, q * v2.astype(F32)), 1, 1)
    )

    pl.semaphore_wait(barrier, len(partners))

    ph1 = []
    for d in range(1, NF):
        f = (F + d) % NF
        ph1.append(remote(send1.at[pl.ds(pl.multiple_of(f * NS, NS), NS)], recv1.at[F], (S, f)))
    recv1[pl.ds(F, 1)] = send1[pl.ds(pl.multiple_of(F * NS, NS), NS)].reshape(1, NS, 128)

    nxt = ((S + (F + 1) // NF) % NS, fn)
    prv = ((S + NS - (NF - F) // NF) % NS, fp)
    pc = [remote(pack, ext_out.at[0], nxt), remote(pack, ext_out.at[2], prv)]
    ext_out[1] = pack[...]

    halo = []
    for src, dst, lo in ((sub, U.at[0], 1), (cond, C, 0)):
        n = GZ - lo
        halo.append(remote(src.at[pl.ds(lo, n), pl.ds(0, 4)], dst.at[pl.ds(lo, n), pl.ds(32, 4), pl.ds(0, CY)], (sp, F)))
        halo.append(remote(src.at[pl.ds(lo, n), pl.ds(28, 4)], dst.at[pl.ds(lo, n), pl.ds(36, 4), pl.ds(0, CY)], (sn, F)))

    for c in lc:
        c.wait()
    lane32 = iota((CX, 128), 1)
    for a in range(2):
        src = U.at[0] if a == 0 else C

        def pack_z(z, acc):
            left, right = acc
            hit = lane32 // 4 == z
            l = pltpu.roll(src[z, 0:CX, 0:128], 4 * z, 1)
            r = pltpu.roll(src[z, 0:CX, 128:256], (4 * z + 4) % 128, 1)
            return jnp.where(hit, l, left), jnp.where(hit, r, right)

        z0 = jnp.zeros((CX, 128), F32)
        left, right = lax.fori_loop(1 - a, GZ, pack_z, (z0, z0))
        pk_s[a, 0] = left
        pk_s[a, 1] = right
        halo += y_faces(remote, pk_s.at[a, 0], pk_s.at[a, 1], pk_r.at[a, 0], pk_r.at[a, 1], S, F, sn, sp, fn, fp)

    for c in ph1:
        c.wait_recv()
    send2[...] = jnp.swapaxes(recv1[...], 0, 1)
    ph2 = []
    for d in range(1, NS):
        s = (S + d) % NS
        ph2.append(remote(send2.at[s], recv2.at[S], (s, F)))
    recv2[pl.ds(S, 1)] = send2[pl.ds(S, 1)]

    for c in halo:
        c.wait_recv()
    row = iota((BX, BY), 0)
    lane = iota((BX, BY), 1)
    up = (S > 0).astype(F32)
    down = (S < NS - 1).astype(F32)
    lft = (F > 0).astype(F32)
    rgt = (F < NF - 1).astype(F32)
    rmask = jnp.where(row < 32, 1.0, jnp.where(row < 36, down, up))
    mask = rmask * jnp.where(lane < 256, 1.0, jnp.where(lane < 320, rgt, lft))
    xmask = mask[32:40, 0:256]
    ymask = mask[:, 256:384]
    near = iota((BX, 128), 1) < 64

    for a in range(2):
        dst = U.at[0] if a == 0 else C
        pr, plf = pk_r[a, 0], pk_r[a, 1]

        def unpack_z(z, _):
            dst[z, 32:40, 0:256] = dst[z, 32:40, 0:256] * xmask
            r = pltpu.roll(pr, (128 - 4 * z) % 128, 1)
            l = pltpu.roll(plf, (252 - 4 * z) % 128, 1)
            dst[z, :, 256:384] = jnp.where(near, r, l) * ymask
            return 0

        lax.fori_loop(1 - a, GZ, unpack_z, 0)

    for c in ph2:
        c.wait_recv()
    rt = jnp.transpose(recv2[...].reshape(128, 128))
    cf = jnp.concatenate([rt[s:s + 1, :] for s in range(CAP)], 1)
    tf = jnp.concatenate([rt[CAP + s:CAP + s + 1, :] for s in range(CAP)], 1)
    ci = cf.astype(jnp.int32) - 1
    live = ci >= 0
    hi = jnp.where(live, ci // 256, -1)
    lo = jnp.where(live, ci % 256, -1)
    s0, s1, s2 = split3(surf[...])
    lc_ = lcell[...]
    lx, ly = lc_ // (NF * CY), lc_ % (NF * CY)
    mine = (lx // CX == S) & (ly // CY == F)
    lhi = jnp.where(mine, lx % CX, -1)
    llo = jnp.where(mine, ly % CY, -1)
    lpower = jnp.where(mine, lpow[...], 0.0)
    fl = jnp.zeros((CX, CY), F32)

    def scatter(fl, ohi, olo, value):
        olo = olo.astype(BF)
        for v in split3(value):
            fl = fl + dot((ohi * v.astype(F32)).astype(BF), olo, 1, 1)
        return fl

    cons = []
    W = 512
    for k in range(2048 // W):
        sl = slice(k * W, (k + 1) * W)
        oh = hot(CX, hi[:, sl])
        ol = hot(CY, lo[:, sl])
        ob = oh.astype(BF)
        g = dot(s0, ob, 0, 0) + dot(s1, ob, 0, 0) + dot(s2, ob, 0, 0)
        ghost = jnp.sum(g * ol, axis=0, keepdims=True)
        con = jnp.where(live[:, sl], CONTACT_GAIN * (tf[:, sl] - ghost), 0.0)
        cons.append(con)
        fl = scatter(fl, oh, ol, con)
    fl = scatter(fl, hot(CX, lhi), hot(CY, llo), lpower)
    top[...] = surf[...] + SURFACE_GAIN * fl
    con = jnp.concatenate(cons, 1)

    th = [
        remote(top.at[pl.ds(0, 4)], U.at[0, 0, pl.ds(32, 4), pl.ds(0, CY)], (sp, F)),
        remote(top.at[pl.ds(28, 4)], U.at[0, 0, pl.ds(36, 4), pl.ds(0, CY)], (sn, F)),
    ]
    th += y_faces(remote, top.at[:, pl.ds(0, 128)], top.at[:, pl.ds(128, 128)], ty.at[0], ty.at[1], S, F, sn, sp, fn, fp)

    back = jnp.concatenate([con[:, s * 128:(s + 1) * 128] for s in range(CAP)] + [jnp.zeros((112, 128), F32)], 0)
    rsend1[...] = jnp.transpose(back).reshape(NS, NF, 128)
    rh1 = []
    for d in range(1, NS):
        s = (S + d) % NS
        rh1.append(remote(rsend1.at[s], rret1.at[S], (s, F)))
    rret1[pl.ds(S, 1)] = rsend1[pl.ds(S, 1)]

    U[0, 0, 0:CX, 0:CY] = top[...]
    for c in th:
        c.wait_recv()
    U[0, 0, 32:40, 0:256] = U[0, 0, 32:40, 0:256] * xmask
    U[0, 0, :, 256:384] = jnp.where(near, ty[0], ty[1]) * ymask

    lam = mask * (LAMBDA_STEP * 0.5)

    def conductivity(u, c):
        return c + (0.5 * c) * jnp.tanh(u)

    def lateral(u, k):
        ru = pltpu.roll(u, BY - 1, 1)
        rk = pltpu.roll(k, BY - 1, 1)
        fy = (k + rk) * (ru - u)
        net = fy - pltpu.roll(fy, 1, 1)
        ru = pltpu.roll(u, BX - 1, 0)
        rk = pltpu.roll(k, BX - 1, 0)
        fx = (k + rk) * (ru - u)
        return net + (fx - pltpu.roll(fx, 1, 0))

    for step in range(SUB):
        a, b = step % 2, 1 - step % 2
        last = step == SUB - 1

        def store(z, v):
            if last:
                out[z] = v[0:CX, 0:CY]
            else:
                U[b, z] = v

        kring[0] = conductivity(U[a, 0], C[0])
        fz_ref[...] = jnp.zeros((BX, BY), F32)

        def layer(z, _):
            u, k = U[a, z], kring[z % 2]
            un = U[a, z + 1]
            kn = conductivity(un, C[z + 1])
            kring[(z + 1) % 2] = kn
            fz = (k + kn) * (un - u)
            net = lateral(u, k) + (fz - fz_ref[...])
            fz_ref[...] = fz
            store(z, u + lam * net)
            return 0

        lax.fori_loop(0, GZ - 1, layer, 0)
        u, k = U[a, GZ - 1], kring[(GZ - 1) % 2]
        net = lateral(u, k) + ((k + k) * (0.0 - u) - fz_ref[...])
        store(GZ - 1, u + lam * net)

        if step == 1:
            for c in rh1:
                c.wait_recv()
            rsend2[...] = jnp.swapaxes(rret1[...], 0, 1)
            rh2 = []
            for d in range(1, NF):
                f = (F + d) % NF
                rh2.append(remote(rsend2.at[f], rret2.at[F], (S, f)))
            rret2[pl.ds(F, 1)] = rsend2[pl.ds(F, 1)]

    for c in rh2:
        c.wait_recv()
    x = jnp.zeros((128, NE), F32)
    for v in split3(rret2[...].reshape(128, 128)):
        x = x + dot(v, pt[...], 0, 0)
    cval = jnp.sum(x[0:CAP] * qt[...], axis=0, keepdims=True)
    php = hot(16, ipart[...] // 128)
    pf = jnp.zeros((16, 128), F32)
    for v in split3(cval):
        pf = pf + dot((php * v.astype(F32)).astype(BF), ohp_lo[...], 1, 1)
    pflux_out[...] = jnp.concatenate([pf[r:r + 1, :] for r in range(16)], 1)

    for c in pc:
        c.wait_recv()
    for c in ph1 + pc + halo + ph2 + th + rh1 + rh2:
        c.wait_send()


def y_faces(remote, left, right, into_right, into_left, S, F, sn, sp, fn, fp):
    return [
        remote(left, into_right.at[pl.ds(0, CX)], (S, fp)),
        remote(right, into_left.at[pl.ds(0, CX)], (S, fn)),
        remote(left.at[pl.ds(0, 4)], into_right.at[pl.ds(32, 4)], (sp, fp)),
        remote(left.at[pl.ds(28, 4)], into_right.at[pl.ds(36, 4)], (sn, fp)),
        remote(right.at[pl.ds(0, 4)], into_left.at[pl.ds(32, 4)], (sp, fn)),
        remote(right.at[pl.ds(28, 4)], into_left.at[pl.ds(36, 4)], (sn, fn)),
    ]


COPIES = 7 + 2 + 4 + 12 + 15 + 8 + 15 + 7


def main_call(pos, temp1, temp16, vol, ipart, iown, icell, lcell, lpow, sub, cond):
    vm = pl.BlockSpec(memory_space=pltpu.VMEM)
    hbm = pl.BlockSpec(memory_space=pl.ANY)
    s = lambda *shape: pltpu.VMEM(shape, F32)
    return pl.pallas_call(
        main_kernel,
        out_shape=[
            jax.ShapeDtypeStruct((GZ, CX, CY), F32),
            jax.ShapeDtypeStruct((3, 8, PD), F32),
            jax.ShapeDtypeStruct((1, PD), F32),
        ],
        in_specs=[vm] * 9 + [hbm] * 2,
        out_specs=[vm] * 3,
        scratch_shapes=[
            s(2, GZ, BX, BY), s(GZ, BX, BY), s(CX, CY), s(CX, CY), s(2, BX, 128),
            s(2, 2, CX, 128), s(2, 2, BX, 128),
            s(128, 128), s(NF, NS, 128), s(NS, NF, 128), s(NS, NF, 128),
            s(NS, NF, 128), s(NS, NF, 128), s(NF, NS, 128), s(NF, NS, 128),
            pltpu.VMEM((128, NE), BF), s(CAP, NE), pltpu.VMEM((128, NE), BF),
            s(BX, BY), s(2, BX, BY), s(8, PD),
            pltpu.SemaphoreType.DMA((3,)),
            pltpu.SemaphoreType.DMA((COPIES,)),
            pltpu.SemaphoreType.DMA((COPIES,)),
        ],
        compiler_params=pltpu.CompilerParams(
            collective_id=0, has_side_effects=True, vmem_limit_bytes=48 * 2**20),
        name="contact_and_conduct",
    )(pos, temp1, temp16, vol, ipart, iown, icell, lcell, lpow, sub, cond)


KP = 128


def heat_kernel(nbr, cnt, ext, pflux, out, jt, it, aj, tj):
    eye = jnp.where(iota((KP, KP), 0) == iota((KP, KP), 1), 1.0, 0.0).astype(BF)
    one3 = jnp.ones((3, PB), BF)
    scale = (LOG2E * 2.0 * KERNEL_SCALE) ** 0.5
    ones8 = jnp.ones((8, 128), BF)

    for t in range(3):
        def prep(b, _):
            blk = ext[t, :, pl.ds(pl.multiple_of(b * PB, PB), PB)]
            p = blk[0:3] * scale
            temp = blk[3:4]
            volume = blk[4:5]
            norm = -0.5 * jnp.sum(p * p, axis=0, keepdims=True)
            p0, p1, p2 = split3(p)
            nj = jnp.concatenate(split3(norm + jnp.log2(volume * (2.0 * KERNEL_SCALE))), 0)
            zj = jnp.zeros((KP - 33, PB), BF)
            jrow = jnp.concatenate([p0, p1, p2] * 3 + [one3, nj, zj], 0)
            jt[t * NB + b] = dot(jrow, eye, 0, 0).astype(BF)
            half = 0.5 / (1.0 + 0.5 * jnp.tanh(temp))
            zr = jnp.zeros((5, PB), BF)
            aj[t * NB + b] = dot(jnp.concatenate(list(split3(half)) + [zr], 0), ones8, 0, 0)
            tj[t * NB + b] = dot(jnp.concatenate(list(split3(temp)) + [zr], 0), ones8, 0, 0)
            if t == 1:
                ni = jnp.concatenate(split3(norm), 0)
                it[b] = jnp.concatenate([p0] * 3 + [p1] * 3 + [p2] * 3 + [ni, one3, zj], 0)
            return 0

        lax.fori_loop(0, NB, prep, 0)

    def block(b, _):
        at = pl.ds(pl.multiple_of(b * PB, PB), PB)
        temp = ext[1, 3:4, at]
        half = 0.5 / (1.0 + 0.5 * jnp.tanh(temp))

        def slot(s, acc):
            o = nbr[b, s]
            e = jnp.exp2(dot(jt[o], it[b], 1, 0))
            res = []
            for h in range(2):
                sl = slice(h * 128, (h + 1) * 128)
                v = e[:, sl] / (aj[o] + half[:, sl]) * (tj[o] - temp[:, sl])
                res.append(jnp.sum(v.reshape(PB // 8, 8, 128), axis=0))
            return acc + jnp.concatenate(res, 1)

        acc = lax.fori_loop(0, cnt[b], slot, jnp.zeros((8, PB), F32))
        heat = jnp.sum(acc, axis=0, keepdims=True)
        out[:, at] = temp + SPH_STEP * heat - PARTICLE_SHARE * pflux[:, at]
        return 0

    lax.fori_loop(0, NB, block, 0)


def heat_call(nbr, cnt, ext, pflux):
    vm = pl.BlockSpec(memory_space=pltpu.VMEM)
    sm = pl.BlockSpec(memory_space=pltpu.SMEM)
    return pl.pallas_call(
        heat_kernel,
        out_shape=jax.ShapeDtypeStruct((1, PD), F32),
        in_specs=[sm, sm, vm, vm],
        out_specs=vm,
        scratch_shapes=[
            pltpu.VMEM((3 * NB, PB, KP), BF), pltpu.VMEM((NB, KP, PB), BF),
            pltpu.VMEM((3 * NB, PB, 128), F32), pltpu.VMEM((3 * NB, PB, 128), F32),
        ],
        compiler_params=pltpu.CompilerParams(vmem_limit_bytes=32 * 2**20),
        name="pair_heat",
    )(nbr, cnt, ext, pflux)


def body(positions, particle_temp, volume, nbr_blocks, nbr_count, iface_part, iface_owner,
         iface_cell, substrate_temp, conduct, laser_cells, laser_power):
    device = lax.axis_index("sph") * NF + lax.axis_index("fv")
    nbr = nbr_blocks - (device - 1) * NB
    field, ext, pflux = main_call(
        positions, particle_temp.reshape(1, PD), particle_temp.reshape(16, 128), volume.reshape(1, PD),
        iface_part.reshape(1, NE), iface_owner.reshape(1, NE), iface_cell.reshape(1, NE),
        laser_cells.reshape(1, -1), laser_power.reshape(1, -1), substrate_temp, conduct)
    particle_out = heat_call(nbr, nbr_count, ext, pflux)
    return particle_out.reshape(PD), field


def solution(mesh):
    in_specs = (
        P(None, ("sph", "fv")),
        P(("sph", "fv")),
        P(("sph", "fv")),
        P(("sph", "fv"), None),
        P(("sph", "fv")),
        P(("sph", "fv")),
        P(("sph", "fv"), None),
        P(("sph", "fv")),
        P(None, "sph", "fv"),
        P(None, "sph", "fv"),
        P(),
        P(),
    )
    out_specs = (P(("sph", "fv")), P(None, "sph", "fv"))
    return jax.shard_map(body, mesh=mesh, in_specs=in_specs, out_specs=out_specs, check_vma=False)
```

```python
import functools

import jax
import jax.numpy as jnp
from jax import lax
from jax.experimental import pallas as pl
from jax.experimental.pallas import tpu as pltpu
from jax.sharding import PartitionSpec as P

SUB = 4
KERNEL_SCALE = 0.5
SPH_STEP = 0.05
CONTACT_GAIN = 1.0
PARTICLE_SHARE = 0.5
SURFACE_GAIN = 0.5
LAMBDA_STEP = 0.1
NS, NF = 16, 8
CX, CY, GZ = 32, 256, 32
BX = 40
PB, NB, KN, CAP = 256, 8, 16, 16
PD, NE = 2048, 1024
MESH = pl.DeviceIdType.MESH
F32, BF = jnp.float32, jnp.bfloat16
LOG2E = 1.4426950408889634


def split2(x):
    a = x.astype(BF)
    return a, (x - a.astype(F32)).astype(BF)


def dot(a, b, ca, cb):
    return lax.dot_general(a, b, (((ca,), (cb,)), ((), ())), preferred_element_type=F32)


def iota(shape, dim):
    return lax.broadcasted_iota(jnp.int32, shape, dim)


def hot(rows, row_index):
    return jnp.where(iota((rows, row_index.shape[1]), 0) == row_index, 1.0, 0.0)


def keep(rows, row_index, value):
    return jnp.where(iota((rows, row_index.shape[1]), 0) == row_index, value, 0.0)


def faces(remote, left, right, into_right, into_left, S, F, sn, sp, fn, fp):
    return [
        remote(left, into_right.at[pl.ds(0, CX)], (S, fp)),
        remote(right, into_left.at[pl.ds(0, CX)], (S, fn)),
        remote(left.at[pl.ds(0, 4)], into_right.at[pl.ds(32, 4)], (sp, fp)),
        remote(left.at[pl.ds(28, 4)], into_right.at[pl.ds(36, 4)], (sn, fp)),
        remote(right.at[pl.ds(0, 4)], into_left.at[pl.ds(32, 4)], (sp, fn)),
        remote(right.at[pl.ds(28, 4)], into_left.at[pl.ds(36, 4)], (sn, fn)),
    ]


GROUP = 4
HEAT_FIRST = 4


def main_kernel(
    nbr, cnt, pos, temp1, temp16, vol, ipart, iown, icell, lcell, lpow, sub, cond,
    out, pout,
    U, C, outv, su, sc, fs, surf, top, ty, pk_s, pk_r,
    send1, recv1, send2, recv2, rsend1, rret1, rsend2, rret2,
    pt, qt, ohp_lo, fz_ref, kc_ref, pack, ext, vt, wb, pair_r, jt, it, aj, heat, lsem, osem, ssem, rsem,
):
    S = lax.axis_index("sph")
    F = lax.axis_index("fv")
    sn, sp = (S + 1) % NS, (S + NS - 1) % NS
    fn, fp = (F + 1) % NF, (F + NF - 1) % NF

    barrier = pltpu.get_barrier_semaphore()
    partners = [(S, (F + d) % NF) for d in range(1, NF)]
    partners += [((S + d) % NS, F) for d in range(1, NS)]
    partners += [(sn, fn), (sn, fp), (sp, fn), (sp, fp)]
    for who in partners:
        pl.semaphore_signal(barrier, inc=1, device_id=who, device_id_type=MESH)

    lc = [
        pltpu.make_async_copy(sub.at[0], surf, lsem.at[0]),
        pltpu.make_async_copy(sub.at[pl.ds(1, GZ - 1)], U.at[0, pl.ds(1, GZ - 1), pl.ds(0, CX)], lsem.at[1]),
        pltpu.make_async_copy(cond, C.at[pl.ds(0, GZ), pl.ds(0, CX)], lsem.at[2]),
    ]
    for c in lc:
        c.start()

    count = [0]

    def remote(src, dst, who):
        i = count[0]
        count[0] += 1
        c = pltpu.make_async_remote_copy(
            src_ref=src, dst_ref=dst, send_sem=ssem.at[i], recv_sem=rsem.at[i],
            device_id=who, device_id_type=MESH)
        c.start()
        return c

    pack[...] = jnp.concatenate([pos[...], temp1[...], vol[...], jnp.zeros((3, PD), F32)], 0)

    own = iown[...]
    row_of = (own % NF) * NS + own // NF
    part = ipart[...]
    php = hot(16, part // 128).astype(BF)
    plo = hot(128, part % 128)
    ohp_lo[...] = plo.astype(BF)
    tval = sum(dot(t, php, 0, 0) for t in split2(temp16[...]))
    tval = jnp.sum(tval * plo, axis=0, keepdims=True)
    po = hot(128, row_of)
    pb = po.astype(BF)
    pt[...] = pb
    tri = jnp.where(iota((256, 256), 0) < iota((256, 256), 1), 1.0, 0.0).astype(BF)
    ones = jnp.ones((256, 256), BF)
    run = jnp.zeros((128, 256), F32)
    ranks = []
    for k in range(NE // 256):
        pc = pb[:, k * 256:(k + 1) * 256]
        cum = dot(pc, tri, 1, 0) + run
        run = run + dot(pc, ones, 1, 0)
        ranks.append(jnp.sum(cum * po[:, k * 256:(k + 1) * 256], axis=0, keepdims=True))
    rank = jnp.concatenate(ranks, 1)
    q = jnp.where(iota((CAP, NE), 0).astype(F32) == rank, 1.0, 0.0)
    qt[...] = q
    c1 = icell[...] + 1
    chi = (c1 // 256 * 256).astype(F32)
    clo = (c1 % 256).astype(F32)
    v0, v1 = split2(tval)
    zero = jnp.zeros((96, NE), BF)

    def rows(a, b):
        return jnp.concatenate([jnp.concatenate([a, b], 0).astype(BF), zero], 0)

    send1[...] = (
        dot(pb, rows(q * chi, q * v0.astype(F32)), 1, 1)
        + dot(pb, rows(q * clo, q * v1.astype(F32)), 1, 1)
    )

    pl.semaphore_wait(barrier, len(partners))

    ph1 = []
    for d in range(1, NF):
        f = (F + d) % NF
        ph1.append(remote(send1.at[pl.ds(pl.multiple_of(f * NS, NS), NS)], recv1.at[F], (S, f)))
    recv1[pl.ds(F, 1)] = send1[pl.ds(pl.multiple_of(F * NS, NS), NS)].reshape(1, NS, 128)

    nxt = ((S + (F + 1) // NF) % NS, fn)
    prv = ((S + NS - (NF - F) // NF) % NS, fp)
    pcs = [remote(pack, ext.at[0], nxt), remote(pack, ext.at[2], prv)]
    ext[1] = pack[...]

    halo = []
    for src, dst, lo in ((sub, U.at[0], 1), (cond, C, 0)):
        n = GZ - lo
        halo.append(remote(src.at[pl.ds(lo, n), pl.ds(0, 4)], dst.at[pl.ds(lo, n), pl.ds(32, 4)], (sp, F)))
        halo.append(remote(src.at[pl.ds(lo, n), pl.ds(28, 4)], dst.at[pl.ds(lo, n), pl.ds(36, 4)], (sn, F)))

    for c in lc:
        c.wait()
    U[0, GZ] = jnp.zeros((BX, CY), F32)
    U[1, GZ] = jnp.zeros((BX, CY), F32)
    C[GZ] = jnp.zeros((BX, CY), F32)
    lane = iota((CX, 128), 1)
    for a in range(2):
        src = U.at[0] if a == 0 else C
        for side in range(2):
            for half in range(2):
                acc = jnp.zeros((CX, 128), F32)
                for w in range(16):
                    x = src[half * 16 + w, 0:CX, side * 128:(side + 1) * 128]
                    acc = jnp.where(lane // 8 == w, pltpu.roll(x, (8 * w + 4) % 128, 1), acc)
                pk_s[a, side, :, half * 128:(half + 1) * 128] = acc
        halo += faces(remote, pk_s.at[a, 0], pk_s.at[a, 1], pk_r.at[a, 1], pk_r.at[a, 0], S, F, sn, sp, fn, fp)

    for c in ph1:
        c.wait_recv()
    send2[...] = jnp.swapaxes(recv1[...], 0, 1)
    ph2 = []
    for d in range(1, NS):
        s = (S + d) % NS
        ph2.append(remote(send2.at[s], recv2.at[S], (s, F)))
    recv2[pl.ds(S, 1)] = send2[pl.ds(S, 1)]

    for c in pcs:
        c.wait_recv()
    heat_prep(ext, vt, jt, it, aj)
    weight = live_weights(nbr, cnt, S * NF + F)
    sub8 = iota((NB, 128), 0)
    one8 = jnp.ones((NB, 128), BF)
    for b in range(NB):
        wb[b] = dot(jnp.where(sub8 == b, weight, 0.0).astype(BF), one8, 0, 0)
    heat_blocks(wb, pair_r, ext, vt, jt, it, aj, heat, 0, HEAT_FIRST)

    for c in ph2:
        c.wait_recv()
    rt = jnp.transpose(recv2[...].reshape(128, 128))
    cf = jnp.concatenate([rt[s:s + 1, :] for s in range(CAP)], 1)
    tf = jnp.concatenate([rt[CAP + s:CAP + s + 1, :] for s in range(CAP)], 1)
    ci = cf.astype(jnp.int32) - 1
    live = ci >= 0
    hi = jnp.where(live, ci // 256 + (ci % 256) // 128 * CX, -1)
    lo = jnp.where(live, ci % 128, -1)
    sf = surf[...]
    ss = jnp.concatenate(split2(jnp.concatenate([sf[:, 0:128], sf[:, 128:256]], 0)), 0)
    cons = []
    W = 512
    for k in range(2048 // W):
        sl = slice(k * W, (k + 1) * W)
        ob = hot(64, hi[:, sl]).astype(BF)
        g = dot(ss, jnp.concatenate([ob, ob], 0), 0, 0)
        ghost = jnp.sum(keep(128, lo[:, sl], g), axis=0, keepdims=True)
        cons.append(jnp.where(live[:, sl], CONTACT_GAIN * (tf[:, sl] - ghost), 0.0))
    lc_ = lcell[...]
    lx, ly = lc_ // (NF * CY), lc_ % (NF * CY)
    mine = (lx // CX == S) & (ly // CY == F)
    lhi = jnp.where(mine, lx % CX + (ly % CY) // 128 * CX, -1)
    llo = jnp.where(mine, ly % 128, -1)
    fl = jnp.zeros((128, 128), F32)
    parts = [(hi[:, k * W:(k + 1) * W], lo[:, k * W:(k + 1) * W], cons[k]) for k in range(2048 // W)]
    for h, l, value in parts + [(lhi, llo, lpow[...])]:
        ch = jnp.concatenate([keep(64, h, v.astype(F32)) for v in split2(value)], 0).astype(BF)
        fl = fl + dot(ch, hot(128, l).astype(BF), 1, 1)
    fl = fl[0:64] + fl[64:128]
    top[...] = sf + SURFACE_GAIN * jnp.concatenate([fl[0:32], fl[32:64]], 1)
    con = jnp.concatenate(cons, 1)

    th = [
        remote(top.at[pl.ds(0, 4)], U.at[0, 0, pl.ds(32, 4)], (sp, F)),
        remote(top.at[pl.ds(28, 4)], U.at[0, 0, pl.ds(36, 4)], (sn, F)),
    ]
    th += faces(remote, top.at[:, pl.ds(0, 128)], top.at[:, pl.ds(128, 128)], ty.at[1], ty.at[0], S, F, sn, sp, fn, fp)

    back = jnp.concatenate([con[:, s * 128:(s + 1) * 128] for s in range(CAP)] + [jnp.zeros((112, 128), F32)], 0)
    rsend1[...] = jnp.transpose(back).reshape(NS, NF, 128)
    rh1 = []
    for d in range(1, NS):
        s = (S + d) % NS
        rh1.append(remote(rsend1.at[s], rret1.at[S], (s, F)))
    rret1[pl.ds(S, 1)] = rsend1[pl.ds(S, 1)]

    heat_blocks(wb, pair_r, ext, vt, jt, it, aj, heat, HEAT_FIRST, NB)

    for c in halo:
        c.wait_recv()
    row = iota((BX, CY), 0)
    lane = iota((BX, CY), 1)
    up = (S > 0).astype(F32)
    down = (S < NS - 1).astype(F32)
    rmask = jnp.where(row < 32, 1.0, jnp.where(row < 36, down, up))
    smask = [
        rmask * jnp.where(lane % 8 < 4, (F > 0).astype(F32), 1.0),
        rmask * jnp.where(lane % 8 < 4, 1.0, (F < NF - 1).astype(F32)),
    ]
    xmask = rmask[32:40]

    @pl.when(S == 0)
    def _():
        U[0, 1:GZ, 36:40, :] = jnp.zeros((GZ - 1, 4, CY), F32)
        C[0:GZ, 36:40, :] = jnp.zeros((GZ, 4, CY), F32)

    @pl.when(S == NS - 1)
    def _():
        U[0, 1:GZ, 32:36, :] = jnp.zeros((GZ - 1, 4, CY), F32)
        C[0:GZ, 32:36, :] = jnp.zeros((GZ, 4, CY), F32)

    lane8 = iota((8, 128), 1)

    def own_strip(src, side):
        halves = []
        for half in range(2):
            acc = jnp.zeros((8, 128), F32)
            for w in range(16):
                x = src[half * 16 + w, 32:40, side * 128:(side + 1) * 128]
                acc = jnp.where(lane8 // 8 == w, pltpu.roll(x, (8 * w + 4) % 128, 1), acc)
            halves.append(acc)
        return jnp.concatenate(halves, 1)

    for c in th:
        c.wait_recv()
    U[0, 0, 0:CX] = top[...]
    U[0, 0, 32:40] = U[0, 0, 32:40] * xmask
    zero_z = lane < 8
    for a in range(2):
        src = U.at[0] if a == 0 else C
        for side in range(2):
            mine_ = jnp.concatenate([pk_s[a, side], own_strip(src, side)], 0)
            other = pk_r[a, side]
            first = (other, mine_) if side == 0 else (mine_, other)
            v = jnp.where(lane % 8 < 4, first[0], first[1])
            if a == 0:
                o = U[0, 0, :, side * 128:(side + 1) * 128]
                n_ = ty[side]
                l128 = iota((BX, 128), 1)
                if side == 0:
                    near = jnp.where(l128 < 64, o, n_)
                else:
                    near = jnp.where(l128 < 64, n_, o)
                near = pltpu.roll(near, 4, 1)
                v = jnp.where(zero_z, jnp.concatenate([near, near], 1), v)
                su[side] = v * smask[side]
            else:
                sc[side] = v * smask[side]

    G = LAMBDA_STEP * 0.5

    def conductivity(u, c):
        return c * (G + (0.5 * G) * jnp.tanh(u))

    def along_x(u, k):
        fx = (k + pltpu.roll(k, BX - 1, 0)) * (pltpu.roll(u, BX - 1, 0) - u)
        return fx - pltpu.roll(fx, 1, 0)

    lane1 = iota((BX, 128), 1)
    first_lane, last_lane = lane1 == 0, lane1 == 127
    for step in range(SUB):
        a, b = step % 2, 1 - step % 2
        last = step == SUB - 1
        for side in range(2):
            u, c = su[side], sc[side]
            k = conductivity(u, c)
            fy = (k + pltpu.roll(k, CY - 1, 1)) * (pltpu.roll(u, CY - 1, 1) - u)
            fs[side, 0] = fy[:, 0:128]
            fs[side, 1] = fy[:, 128:256]
            if not last:
                below = lane >= CY - 8
                un = jnp.where(below, 0.0, pltpu.roll(u, CY - 8, 1))
                kn = jnp.where(below, k, pltpu.roll(k, CY - 8, 1))
                fz = (k + kn) * (un - u)
                fup = jnp.where(lane < 8, 0.0, pltpu.roll(fz, 8, 1))
                net = (fy - pltpu.roll(fy, 1, 1)) + (fz - fup) + along_x(u, k)
                su[side] = (u + net) * smask[side]

        kc_ref[...] = conductivity(U[a, 0], C[0])
        fz_ref[...] = jnp.zeros((BX, CY), F32)

        def layers(n, _):
            z0 = n * GROUP
            k, fz0 = kc_ref[...], fz_ref[...]
            u = U[a, z0]
            for m in range(GROUP):
                z = z0 + m
                un = U[a, z + 1]
                kn = conductivity(un, C[z + 1])
                if m == GROUP - 1:
                    kf = jnp.where(z == GZ - 1, k, kn)
                else:
                    kf = kn
                fz = (k + kf) * (un - u)
                net = along_x(u, k) + (fz - fz0)
                w = z % 16
                kl, kr = k[:, 0:128], k[:, 128:256]
                ul, ur = u[:, 0:128], u[:, 128:256]
                skl, skr = pltpu.roll(kl, 127, 1), pltpu.roll(kr, 127, 1)
                sul, sur = pltpu.roll(ul, 127, 1), pltpu.roll(ur, 127, 1)
                fyl = (kl + jnp.where(last_lane, skr, skl)) * (jnp.where(last_lane, sur, sul) - ul)
                fyr = (kr + skr) * (sur - ur)
                fyr = jnp.where(last_lane, pltpu.roll(fs[1, z // 16], (124 + 128 - 8 * w) % 128, 1), fyr)
                bl, br = pltpu.roll(fyl, 1, 1), pltpu.roll(fyr, 1, 1)
                edge = pltpu.roll(fs[0, z // 16], (125 + 128 - 8 * w) % 128, 1)
                nl = fyl - jnp.where(first_lane, edge, bl)
                nr = fyr - jnp.where(first_lane, bl, br)
                new = u + (net + jnp.concatenate([nl, nr], 1))
                if last:
                    outv[z] = new[0:CX]
                else:
                    U[b, z, 0:CX] = new[0:CX]
                    U[b, z, 32:40] = new[32:40] * xmask
                u, k, fz0 = un, kn, fz
            kc_ref[...] = k
            fz_ref[...] = fz0
            if last:
                pltpu.make_async_copy(
                    outv.at[pl.ds(z0, GROUP)], out.at[pl.ds(z0, GROUP)], osem.at[n]).start()
            return 0

        lax.fori_loop(0, GZ // GROUP, layers, 0)

        if step == 1:
            for c in rh1:
                c.wait_recv()
            rsend2[...] = jnp.swapaxes(rret1[...], 0, 1)
            rh2 = []
            for d in range(1, NF):
                f = (F + d) % NF
                rh2.append(remote(rsend2.at[f], rret2.at[F], (S, f)))
            rret2[pl.ds(F, 1)] = rsend2[pl.ds(F, 1)]

    for c in rh2:
        c.wait_recv()
    rr = rret2[...].reshape(128, 128)[:, 0:CAP]
    x = sum(dot(v, pt[...], 0, 0) for v in split2(rr))
    cval = jnp.sum(x * qt[...], axis=0, keepdims=True)
    ph = ipart[...] // 128
    pf = sum(dot(keep(16, ph, v.astype(F32)).astype(BF), ohp_lo[...], 1, 1) for v in split2(cval))
    pflux = jnp.concatenate([pf[r:r + 1, :] for r in range(16)], 1)
    pout[...] = temp1[...] + SPH_STEP * heat[...] - PARTICLE_SHARE * pflux

    for n in range(GZ // GROUP):
        pltpu.make_async_copy(
            outv.at[pl.ds(n * GROUP, GROUP)], out.at[pl.ds(n * GROUP, GROUP)], osem.at[n]).wait()
    for c in ph1 + pcs + halo + ph2 + th + rh1 + rh2:
        c.wait_send()


KP = 80


def groups3(x):
    a = x.astype(BF).astype(F32)
    r = x - a
    b = r.astype(BF).astype(F32)
    return [a, b, r - b]


def heat_prep(ext, vt, jt, it, aj):
    scale = (LOG2E * 2.0 * KERNEL_SCALE) ** 0.5
    r32, c256 = iota((32, 256), 0), iota((32, 256), 1)
    rep = jnp.where((c256 < 72) & (c256 % 24 == r32), 1.0, 0.0)
    tail = jnp.where((c256 >= 128) & (r32 >= 24) & (r32 < 27), 1.0, 0.0)
    spread = (rep + tail).astype(BF)
    row = iota((8, PB), 0)
    for t in range(3):
        def prep(n, _):
            for m in range(4):
                b = n * 4 + m
                at = pl.ds(pl.multiple_of(b * PB, PB), PB)
                blk = ext[t, :, at]
                p = jnp.where(row < 3, blk * scale, 0.0)
                norm = -0.5 * jnp.sum(p * p, axis=0, keepdims=True)
                nj = norm + jnp.log2(blk[4:5] * (2.0 * KERNEL_SCALE))
                sj = groups3(jnp.where(row == 3, nj, jnp.where(row == 4, 1.0, p)))
                half = 0.5 / (1.0 + 0.5 * jnp.tanh(blk[3:4]))
                h0, h1, h2 = groups3(half)
                ah = jnp.where(row == 0, h0, jnp.where(row == 1, h1, jnp.where(row == 2, h2, 0.0)))
                both = dot(jnp.concatenate(sj + [ah], 0).astype(BF), spread, 0, 0)
                t0, t1, t2 = groups3(blk[3:4])
                vt[t * NB + b] = jnp.where(row == 0, t0, jnp.where(row == 1, t1, jnp.where(row == 2, t2, jnp.where(row == 3, 1.0, 0.0))))
                jt[t * NB + b] = both[:, 0:128].astype(BF)
                aj[t * NB + b] = both[:, 128:256]
                if t == 1:
                    i0, i1, i2 = groups3(jnp.where(row == 3, 1.0, jnp.where(row == 4, norm, p)))
                    z = jnp.zeros((128 - 72, PB), F32)
                    it[b] = jnp.concatenate([i0, i0, i0, i1, i1, i1, i2, i2, i2, z], 0).astype(BF)
            return 0

        lax.fori_loop(0, NB // 4, prep, 0)


WIN = 2 * NB + 1


def live_weights(nbr, cnt, device):
    local = nbr[...] - (device - 1) * NB
    eq = iota((NB, NB), 0) == iota((NB, NB), 1)
    count = jnp.sum(jnp.where(eq, jnp.broadcast_to(cnt[...], (NB, NB)).astype(F32), 0.0), axis=1, keepdims=True)
    w = jnp.zeros((NB, 128), F32)
    at = iota((NB, 128), 1)
    for s in range(KN):
        live = jnp.where(count > s, 1.0, 0.0)
        w = w + jnp.where(at == local[:, s:s + 1], live, 0.0)
    return w


def heat_blocks(wb, pair_r, ext, vt, jt, it, aj, heat, start, stop):
    def block(b, _):
        at = pl.ds(pl.multiple_of(b * PB, PB), PB)
        temp = ext[1, 3:4, at]
        half = 0.5 / (1.0 + 0.5 * jnp.tanh(temp))
        itb = it[b]
        for d in range(WIN):
            o = b + d
            e = dot(jt[o], itb, 1, 0)
            a = aj[o]
            for h in range(2):
                sl = slice(h * 128, (h + 1) * 128)
                s4 = (a + half[:, sl]).reshape(PB // 16, 2, 8, 128)
                s0, s1 = s4[:, 0], s4[:, 1]
                inv = 1.0 / (s0 * s1)
                f = jnp.stack([s1 * inv, s0 * inv], 1).reshape(PB, 128)
                pair_r[d * PB:(d + 1) * PB, sl] = (jnp.exp2(e[:, sl]) * f).astype(BF)
        left = []
        for d in range(WIN):
            w = wb[b, pl.ds(b + d, 1), :]
            v = vt[b + d]
            left.append(v * jnp.concatenate([w, w], 1))
        acc = dot(jnp.concatenate(left, 1).astype(BF), pair_r[...], 1, 0)
        heat[:, at] = acc[0:1] + acc[1:2] + acc[2:3] - temp * acc[3:4]
        return 0

    lax.fori_loop(start, stop, block, 0)


COPIES = 7 + 2 + 4 + 12 + 15 + 8 + 15 + 7


def main_call(nbr, cnt, *args):
    vm = pl.BlockSpec(memory_space=pltpu.VMEM)
    hbm = pl.BlockSpec(memory_space=pl.ANY)
    s = lambda *shape: pltpu.VMEM(shape, F32)
    return pl.pallas_call(
        main_kernel,
        out_shape=[
            jax.ShapeDtypeStruct((GZ, CX, CY), F32),
            jax.ShapeDtypeStruct((1, PD), F32),
        ],
        in_specs=[vm] * 11 + [hbm] * 2,
        out_specs=[hbm, vm],
        scratch_shapes=[
            s(2, GZ + 1, BX, CY), s(GZ + 1, BX, CY), s(GZ, CX, CY), s(2, BX, CY), s(2, BX, CY),
            s(2, 2, BX, 128), s(CX, CY), s(CX, CY), s(2, BX, 128),
            s(2, 2, CX, CY), s(2, 2, BX, CY),
            s(128, 128), s(NF, NS, 128), s(NS, NF, 128), s(NS, NF, 128),
            s(NS, NF, 128), s(NS, NF, 128), s(NF, NS, 128), s(NF, NS, 128),
            pltpu.VMEM((128, NE), BF), s(CAP, NE), pltpu.VMEM((128, NE), BF),
            s(BX, CY), s(BX, CY), s(8, PD), s(3, 8, PD), s(3 * NB, 8, PB), s(NB, 128, 128), pltpu.VMEM((WIN * PB, PB), BF),
            pltpu.VMEM((3 * NB, PB, 128), BF), pltpu.VMEM((NB, 128, PB), BF),
            s(3 * NB, PB, 128), s(1, PD),
            pltpu.SemaphoreType.DMA((3,)),
            pltpu.SemaphoreType.DMA((GZ // GROUP,)),
            pltpu.SemaphoreType.DMA((COPIES,)),
            pltpu.SemaphoreType.DMA((COPIES,)),
        ],
        compiler_params=pltpu.CompilerParams(
            collective_id=0, has_side_effects=True, vmem_limit_bytes=67_000_000),
        name="step",
    )(nbr, cnt, *args)


def body(positions, particle_temp, volume, nbr_blocks, nbr_count, iface_part, iface_owner,
         iface_cell, substrate_temp, conduct, laser_cells, laser_power):
    field, particle_out = main_call(
        nbr_blocks, nbr_count.reshape(1, NB), positions, particle_temp.reshape(1, PD), particle_temp.reshape(16, 128), volume.reshape(1, PD),
        iface_part.reshape(1, NE), iface_owner.reshape(1, NE), iface_cell.reshape(1, NE),
        laser_cells.reshape(1, -1), laser_power.reshape(1, -1), substrate_temp, conduct)
    return particle_out.reshape(PD), field


def solution(mesh):
    in_specs = (
        P(None, ("sph", "fv")),
        P(("sph", "fv")),
        P(("sph", "fv")),
        P(("sph", "fv"), None),
        P(("sph", "fv")),
        P(("sph", "fv")),
        P(("sph", "fv"), None),
        P(("sph", "fv")),
        P(None, "sph", "fv"),
        P(None, "sph", "fv"),
        P(),
        P(),
    )
    out_specs = (P(("sph", "fv")), P(None, "sph", "fv"))
    return jax.shard_map(body, mesh=mesh, in_specs=in_specs, out_specs=out_specs, check_vma=False)
```

```python
import functools

import jax
import jax.numpy as jnp
from jax import lax
from jax.experimental import pallas as pl
from jax.experimental.pallas import tpu as pltpu
from jax.sharding import PartitionSpec as P

SUB = 4
KERNEL_SCALE = 0.5
SPH_STEP = 0.05
CONTACT_GAIN = 1.0
PARTICLE_SHARE = 0.5
SURFACE_GAIN = 0.5
LAMBDA_STEP = 0.1
NS, NF = 16, 8
CX, CY, GZ = 32, 256, 32
BX = 40
PB, NB, KN, CAP = 256, 8, 16, 16
PD, NE = 2048, 1024
MESH = pl.DeviceIdType.MESH
F32, BF = jnp.float32, jnp.bfloat16
LOG2E = 1.4426950408889634


def split2(x):
    a = x.astype(BF)
    return a, (x - a.astype(F32)).astype(BF)


def dot(a, b, ca, cb):
    return lax.dot_general(a, b, (((ca,), (cb,)), ((), ())), preferred_element_type=F32)


def iota(shape, dim):
    return lax.broadcasted_iota(jnp.int32, shape, dim)


def hot(rows, row_index):
    return jnp.where(iota((rows, row_index.shape[1]), 0) == row_index, 1.0, 0.0)


def keep(rows, row_index, value):
    return jnp.where(iota((rows, row_index.shape[1]), 0) == row_index, value, 0.0)


def faces(remote, left, right, into_right, into_left, S, F, sn, sp, fn, fp):
    return [
        remote(left, into_right.at[pl.ds(0, CX)], (S, fp)),
        remote(right, into_left.at[pl.ds(0, CX)], (S, fn)),
        remote(left.at[pl.ds(0, 4)], into_right.at[pl.ds(32, 4)], (sp, fp)),
        remote(left.at[pl.ds(28, 4)], into_right.at[pl.ds(36, 4)], (sn, fp)),
        remote(right.at[pl.ds(0, 4)], into_left.at[pl.ds(32, 4)], (sp, fn)),
        remote(right.at[pl.ds(28, 4)], into_left.at[pl.ds(36, 4)], (sn, fn)),
    ]


GROUP = 4


def main_kernel(
    h_nbr, h_cnt, h_pos, h_temp1, h_temp16, h_vol, h_ipart, h_iown, h_icell, h_lcell, h_lpow, sub, cond,
    outv, pout,
    nbr, cnt, pos, temp1, temp16, vol, ipart, iown, icell, lcell, lpow,
    U, C, su, sc, fs, surf, top, ty, pk_s, pk_r,
    send1, recv1, send2, recv2, rsend1, rret1, rsend2, rret2,
    pt, qt, ohp_lo, fz_ref, kc_ref, pack, ext, vt, wb, pair_r, jt, it, aj, hrow, hacc, heat, lsem, ssem, rsem,
):
    S = lax.axis_index("sph")
    F = lax.axis_index("fv")
    sn, sp = (S + 1) % NS, (S + NS - 1) % NS
    fn, fp = (F + 1) % NF, (F + NF - 1) % NF

    barrier = pltpu.get_barrier_semaphore()
    partners = [(S, (F + d) % NF) for d in range(1, NF)]
    partners += [((S + d) % NS, F) for d in range(1, NS)]
    partners += [(sn, fn), (sn, fp), (sp, fn), (sp, fp)]
    for who in partners:
        pl.semaphore_signal(barrier, inc=1, device_id=who, device_id_type=MESH)

    small = [
        pltpu.make_async_copy(a, b, lsem.at[3 + n]) for n, (a, b) in enumerate((
            (h_ipart, ipart), (h_temp16, temp16), (h_iown, iown), (h_icell, icell), (h_pos, pos), (h_temp1, temp1),
            (h_vol, vol), (h_nbr, nbr), (h_cnt, cnt), (h_lcell, lcell), (h_lpow, lpow)))
    ]
    for c in small:
        c.start()

    lc = [
        pltpu.make_async_copy(sub.at[0], surf, lsem.at[0]),
        pltpu.make_async_copy(sub.at[pl.ds(1, GZ - 1)], U.at[0, pl.ds(1, GZ - 1), pl.ds(0, CX)], lsem.at[1]),
        pltpu.make_async_copy(cond, C.at[pl.ds(0, GZ), pl.ds(0, CX)], lsem.at[2]),
    ]
    for c in lc:
        c.start()

    count = [0]

    def remote(src, dst, who):
        i = count[0]
        count[0] += 1
        c = pltpu.make_async_remote_copy(
            src_ref=src, dst_ref=dst, send_sem=ssem.at[i], recv_sem=rsem.at[i],
            device_id=who, device_id_type=MESH)
        c.start()
        return c

    for c in small:
        c.wait()

    pack[...] = jnp.concatenate([pos[...], temp1[...], vol[...], jnp.zeros((3, PD), F32)], 0)

    own = iown[...]
    row_of = (own % NF) * NS + own // NF
    part = ipart[...]
    php = hot(16, part // 128).astype(BF)
    plo = hot(128, part % 128)
    ohp_lo[...] = plo.astype(BF)
    tval = sum(dot(t, php, 0, 0) for t in split2(temp16[...]))
    tval = jnp.sum(tval * plo, axis=0, keepdims=True)
    po = hot(128, row_of)
    pb = po.astype(BF)
    pt[...] = pb
    tri = jnp.where(iota((256, 256), 0) < iota((256, 256), 1), 1.0, 0.0).astype(BF)
    ones = jnp.ones((256, 256), BF)
    run = jnp.zeros((128, 256), F32)
    ranks = []
    for k in range(NE // 256):
        pc = pb[:, k * 256:(k + 1) * 256]
        cum = dot(pc, tri, 1, 0) + run
        run = run + dot(pc, ones, 1, 0)
        ranks.append(jnp.sum(cum * po[:, k * 256:(k + 1) * 256], axis=0, keepdims=True))
    rank = jnp.concatenate(ranks, 1)
    q = jnp.where(iota((CAP, NE), 0).astype(F32) == rank, 1.0, 0.0)
    qt[...] = q
    c1 = icell[...] + 1
    chi = (c1 // 256 * 256).astype(F32)
    clo = (c1 % 256).astype(F32)
    v0, v1 = split2(tval)
    zero = jnp.zeros((96, NE), BF)

    def rows(a, b):
        return jnp.concatenate([jnp.concatenate([a, b], 0).astype(BF), zero], 0)

    send1[...] = (
        dot(pb, rows(q * chi, q * v0.astype(F32)), 1, 1)
        + dot(pb, rows(q * clo, q * v1.astype(F32)), 1, 1)
    )

    pl.semaphore_wait(barrier, len(partners))

    ph1 = []
    for d in range(1, NF):
        f = (F + d) % NF
        ph1.append(remote(send1.at[pl.ds(pl.multiple_of(f * NS, NS), NS)], recv1.at[F], (S, f)))
    recv1[pl.ds(F, 1)] = send1[pl.ds(pl.multiple_of(F * NS, NS), NS)].reshape(1, NS, 128)

    nxt = ((S + (F + 1) // NF) % NS, fn)
    prv = ((S + NS - (NF - F) // NF) % NS, fp)
    pcs = [remote(pack, ext.at[0], nxt), remote(pack, ext.at[2], prv)]
    ext[1] = pack[...]

    halo = []
    for src, dst, lo in ((sub, U.at[0], 1), (cond, C, 0)):
        n = GZ - lo
        halo.append(remote(src.at[pl.ds(lo, n), pl.ds(0, 4)], dst.at[pl.ds(lo, n), pl.ds(32, 4)], (sp, F)))
        halo.append(remote(src.at[pl.ds(lo, n), pl.ds(28, 4)], dst.at[pl.ds(lo, n), pl.ds(36, 4)], (sn, F)))

    for c in lc:
        c.wait()
    U[0, GZ] = jnp.zeros((BX, CY), F32)
    U[1, GZ] = jnp.zeros((BX, CY), F32)
    C[GZ] = jnp.zeros((BX, CY), F32)
    def packed(src, lo, hi):
        n = hi - lo
        l = iota((n, 128), 1)
        halves = []
        for half in range(2):
            acc = jnp.zeros((n, 128), F32)
            for w in range(16):
                z = half * 16 + w
                x = jnp.where(l < 64, src[z, lo:hi, 0:128], src[z, lo:hi, 128:256])
                acc = jnp.where(l // 8 == w, pltpu.roll(x, (8 * w + 4) % 128, 1), acc)
            halves.append(acc)
        return jnp.concatenate(halves, 1)

    for a in range(2):
        pk_s[a] = packed(U.at[0] if a == 0 else C, 0, CX)
        halo += faces(remote, pk_s.at[a], pk_s.at[a], pk_r.at[a, 1], pk_r.at[a, 0], S, F, sn, sp, fn, fp)

    for c in ph1:
        c.wait_recv()
    send2[...] = jnp.swapaxes(recv1[...], 0, 1)
    ph2 = []
    for d in range(1, NS):
        s = (S + d) % NS
        ph2.append(remote(send2.at[s], recv2.at[S], (s, F)))
    recv2[pl.ds(S, 1)] = send2[pl.ds(S, 1)]

    for c in pcs:
        c.wait_recv()
    heat_prep(ext, vt, jt, it, aj, hrow)
    hacc[...] = jnp.zeros((NB, 8, PB), F32)
    weight = live_weights(nbr, cnt, S * NF + F)
    sub8 = iota((NB, 128), 0)
    one8 = jnp.ones((NB, 128), BF)
    for b in range(NB):
        wb[b] = dot(jnp.where(sub8 == b, weight, 0.0).astype(BF), one8, 0, 0)
    heat_blocks(wb, pair_r, vt, jt, it, aj, hrow, hacc, 0, NB // 2, 5)

    for c in ph2:
        c.wait_recv()
    rt = jnp.transpose(recv2[...].reshape(128, 128))
    cf = jnp.concatenate([rt[s:s + 1, :] for s in range(CAP)], 1)
    tf = jnp.concatenate([rt[CAP + s:CAP + s + 1, :] for s in range(CAP)], 1)
    ci = cf.astype(jnp.int32) - 1
    live = ci >= 0
    hi = jnp.where(live, ci // 256 + (ci % 256) // 128 * CX, -1)
    lo = jnp.where(live, ci % 128, -1)
    sf = surf[...]
    ss = jnp.concatenate(split2(jnp.concatenate([sf[:, 0:128], sf[:, 128:256]], 0)), 0)
    cons = []
    W = 512
    for k in range(2048 // W):
        sl = slice(k * W, (k + 1) * W)
        ob = hot(64, hi[:, sl]).astype(BF)
        g = dot(ss, jnp.concatenate([ob, ob], 0), 0, 0)
        ghost = jnp.sum(keep(128, lo[:, sl], g), axis=0, keepdims=True)
        cons.append(jnp.where(live[:, sl], CONTACT_GAIN * (tf[:, sl] - ghost), 0.0))
    lc_ = lcell[...]
    lx, ly = lc_ // (NF * CY), lc_ % (NF * CY)
    mine = (lx // CX == S) & (ly // CY == F)
    lhi = jnp.where(mine, lx % CX + (ly % CY) // 128 * CX, -1)
    llo = jnp.where(mine, ly % 128, -1)
    fl = jnp.zeros((128, 128), F32)
    parts = [(hi[:, k * W:(k + 1) * W], lo[:, k * W:(k + 1) * W], cons[k]) for k in range(2048 // W)]
    for h, l, value in parts + [(lhi, llo, lpow[...])]:
        ch = jnp.concatenate([keep(64, h, v.astype(F32)) for v in split2(value)], 0).astype(BF)
        fl = fl + dot(ch, hot(128, l).astype(BF), 1, 1)
    fl = fl[0:64] + fl[64:128]
    top[...] = sf + SURFACE_GAIN * jnp.concatenate([fl[0:32], fl[32:64]], 1)
    con = jnp.concatenate(cons, 1)

    th = [
        remote(top.at[pl.ds(0, 4)], U.at[0, 0, pl.ds(32, 4)], (sp, F)),
        remote(top.at[pl.ds(28, 4)], U.at[0, 0, pl.ds(36, 4)], (sn, F)),
    ]
    th += faces(remote, top.at[:, pl.ds(0, 128)], top.at[:, pl.ds(128, 128)], ty.at[1], ty.at[0], S, F, sn, sp, fn, fp)

    back = jnp.concatenate([con[:, s * 128:(s + 1) * 128] for s in range(CAP)] + [jnp.zeros((112, 128), F32)], 0)
    rsend1[...] = jnp.transpose(back).reshape(NS, NF, 128)
    rh1 = []
    for d in range(1, NS):
        s = (S + d) % NS
        rh1.append(remote(rsend1.at[s], rret1.at[S], (s, F)))
    rret1[pl.ds(S, 1)] = rsend1[pl.ds(S, 1)]

    heat_blocks(wb, pair_r, vt, jt, it, aj, hrow, hacc, NB // 2, NB, 4)
    for b in range(NB):
        h8 = hacc[b]
        warm, amount = h8[0:1] + h8[1:2] + h8[2:3], h8[3:4] + h8[4:5] + h8[5:6]
        heat[:, b * PB:(b + 1) * PB] = warm - ext[1, 3:4, b * PB:(b + 1) * PB] * amount

    for c in halo:
        c.wait_recv()
    row = iota((BX, CY), 0)
    lane = iota((BX, CY), 1)
    up = (S > 0).astype(F32)
    down = (S < NS - 1).astype(F32)
    rmask = jnp.where(row < 32, 1.0, jnp.where(row < 36, down, up))
    smask = [
        rmask * jnp.where(lane % 8 < 4, (F > 0).astype(F32), 1.0),
        rmask * jnp.where(lane % 8 < 4, 1.0, (F < NF - 1).astype(F32)),
    ]
    xmask = rmask[32:40]

    @pl.when(S == 0)
    def _():
        U[0, 1:GZ, 36:40, :] = jnp.zeros((GZ - 1, 4, CY), F32)
        C[0:GZ, 36:40, :] = jnp.zeros((GZ, 4, CY), F32)

    @pl.when(S == NS - 1)
    def _():
        U[0, 1:GZ, 32:36, :] = jnp.zeros((GZ - 1, 4, CY), F32)
        C[0:GZ, 32:36, :] = jnp.zeros((GZ, 4, CY), F32)

    for c in th:
        c.wait_recv()
    U[0, 0, 0:CX] = top[...]
    U[0, 0, 32:40] = U[0, 0, 32:40] * xmask
    zero_z = lane < 8
    l128 = iota((BX, 128), 1)
    for a in range(2):
        src = U.at[0] if a == 0 else C
        mine_ = jnp.concatenate([pk_s[a], packed(src, 32, 40)], 0)
        for side in range(2):
            first = (pk_r[a, side], mine_) if side == 0 else (mine_, pk_r[a, side])
            v = jnp.where(lane % 8 < 4, first[0], first[1])
            if a == 0:
                o = U[0, 0, :, side * 128:(side + 1) * 128]
                near = (o, ty[side]) if side == 0 else (ty[side], o)
                near = pltpu.roll(jnp.where(l128 < 64, near[0], near[1]), 4, 1)
                v = jnp.where(zero_z, jnp.concatenate([near, near], 1), v)
                su[side] = v * smask[side]
            else:
                sc[side] = v * smask[side]

    G = LAMBDA_STEP * 0.5

    def conductivity(u, c):
        return c * (G + (0.5 * G) * jnp.tanh(u))

    def along_x(u, k):
        fx = (k + pltpu.roll(k, BX - 1, 0)) * (pltpu.roll(u, BX - 1, 0) - u)
        return fx - pltpu.roll(fx, 1, 0)

    lane1 = iota((BX, 128), 1)
    first_lane, last_lane = lane1 == 0, lane1 == 127
    for step in range(SUB):
        a, b = step % 2, 1 - step % 2
        last = step == SUB - 1
        for side in range(2):
            u, c = su[side], sc[side]
            k = conductivity(u, c)
            fy = (k + pltpu.roll(k, CY - 1, 1)) * (pltpu.roll(u, CY - 1, 1) - u)
            if side == 0:
                face = pltpu.roll(fy, 1, 1)
            else:
                face = jnp.where(lane % 8 == 4, face, fy)
                fs[0] = face[:, 0:128]
                fs[1] = face[:, 128:256]
            if not last:
                below = lane >= CY - 8
                un = jnp.where(below, 0.0, pltpu.roll(u, CY - 8, 1))
                kn = jnp.where(below, k, pltpu.roll(k, CY - 8, 1))
                fz = (k + kn) * (un - u)
                fup = jnp.where(lane < 8, 0.0, pltpu.roll(fz, 8, 1))
                net = (fy - pltpu.roll(fy, 1, 1)) + (fz - fup) + along_x(u, k)
                su[side] = (u + net) * smask[side]

        kc_ref[...] = conductivity(U[a, 0], C[0])
        fz_ref[...] = jnp.zeros((BX, CY), F32)

        def layers(n, _):
            z0 = n * GROUP
            k, fz0 = kc_ref[...], fz_ref[...]
            u = U[a, z0]
            for m in range(GROUP):
                z = z0 + m
                un = U[a, z + 1]
                kn = conductivity(un, C[z + 1])
                if m == GROUP - 1:
                    kf = jnp.where(z == GZ - 1, k, kn)
                else:
                    kf = kn
                fz = (k + kf) * (un - u)
                net = along_x(u, k) + (fz - fz0)
                w = z % 16
                kl, kr = k[:, 0:128], k[:, 128:256]
                ul, ur = u[:, 0:128], u[:, 128:256]
                skl, skr = pltpu.roll(kl, 127, 1), pltpu.roll(kr, 127, 1)
                sul, sur = pltpu.roll(ul, 127, 1), pltpu.roll(ur, 127, 1)
                fyl = (kl + jnp.where(last_lane, skr, skl)) * (jnp.where(last_lane, sur, sul) - ul)
                fyr = (kr + skr) * (sur - ur)
                edge = pltpu.roll(fs[z // 16], (124 + 128 - 8 * w) % 128, 1)
                fyr = jnp.where(last_lane, edge, fyr)
                bl, br = pltpu.roll(fyl, 1, 1), pltpu.roll(fyr, 1, 1)
                nl = fyl - jnp.where(first_lane, edge, bl)
                nr = fyr - jnp.where(first_lane, bl, br)
                new = u + (net + jnp.concatenate([nl, nr], 1))
                if last:
                    outv[z] = new[0:CX]
                else:
                    U[b, z, 0:CX] = new[0:CX]
                    U[b, z, 32:40] = new[32:40] * xmask
                u, k, fz0 = un, kn, fz
            kc_ref[...] = k
            fz_ref[...] = fz0
            return 0

        lax.fori_loop(0, GZ // GROUP, layers, 0)

        if step == 1:
            for c in rh1:
                c.wait_recv()
            rsend2[...] = jnp.swapaxes(rret1[...], 0, 1)
            rh2 = []
            for d in range(1, NF):
                f = (F + d) % NF
                rh2.append(remote(rsend2.at[f], rret2.at[F], (S, f)))
            rret2[pl.ds(F, 1)] = rsend2[pl.ds(F, 1)]

    for c in rh2:
        c.wait_recv()
    rr = rret2[...].reshape(128, 128)[:, 0:CAP]
    x = sum(dot(v, pt[...], 0, 0) for v in split2(rr))
    cval = jnp.sum(x * qt[...], axis=0, keepdims=True)
    ph = ipart[...] // 128
    pf = sum(dot(keep(16, ph, v.astype(F32)).astype(BF), ohp_lo[...], 1, 1) for v in split2(cval))
    pflux = jnp.concatenate([pf[r:r + 1, :] for r in range(16)], 1)
    pout[...] = temp1[...] + SPH_STEP * heat[...] - PARTICLE_SHARE * pflux

    for c in ph1 + pcs + halo + ph2 + th + rh1 + rh2:
        c.wait_send()


UNROLL = 8


def groups3(x):
    a = x.astype(BF).astype(F32)
    r = x - a
    b = r.astype(BF).astype(F32)
    return [a, b, r - b]


def heat_prep(ext, vt, jt, it, aj, hrow):
    scale = (LOG2E * 2.0 * KERNEL_SCALE) ** 0.5
    r32, c256 = iota((32, 256), 0), iota((32, 256), 1)
    rep = jnp.where((c256 < 72) & (c256 % 24 == r32), 1.0, 0.0)
    tail = jnp.where((c256 >= 128) & (r32 >= 24) & (r32 < 27), 1.0, 0.0)
    spread = (rep + tail).astype(BF)
    row = iota((8, PB), 0)

    def place(*rows):
        out = jnp.zeros((8, PB), F32)
        for n, r in enumerate(rows):
            out = jnp.where(row == n, r, out)
        return out

    for t in range(3):
        def prep(n, _):
            for m in range(UNROLL):
                b = n * UNROLL + m
                at = pl.ds(pl.multiple_of(b * PB, PB), PB)
                blk = ext[t, :, at]
                p = jnp.where(row < 3, blk * scale, 0.0)
                norm = -0.5 * jnp.sum(p * p, axis=0, keepdims=True)
                temp = blk[3:4]
                volume = blk[4:5] * (2.0 * KERNEL_SCALE)
                half = 0.5 / (1.0 + 0.5 * jnp.tanh(temp))
                packed = groups3(place(half, volume * temp, volume))
                vt[t * NB + b] = place(
                    packed[0][1:2], packed[1][1:2], packed[2][1:2], packed[0][2:3], packed[1][2:3], packed[2][2:3])
                ah = place(packed[0][0:1], packed[1][0:1], packed[2][0:1])
                sj = groups3(jnp.where(row == 3, norm, jnp.where(row == 4, 1.0, p)))
                both = dot(jnp.concatenate(sj + [ah], 0).astype(BF), spread, 0, 0)
                jt[t * NB + b] = both[:, 0:128].astype(BF)
                aj[t * NB + b] = both[:, 128:256]
                if t == 1:
                    hrow[b] = jnp.broadcast_to(half, (8, PB))
                    i0, i1, i2 = groups3(jnp.where(row == 3, 1.0, jnp.where(row == 4, norm, p)))
                    z = jnp.zeros((128 - 72, PB), F32)
                    it[b] = jnp.concatenate([i0, i0, i0, i1, i1, i1, i2, i2, i2, z], 0).astype(BF)
            return 0

        lax.fori_loop(0, NB // UNROLL, prep, 0)


WIN = NB + 1 + 5


def live_weights(nbr, cnt, device):
    local = nbr[...] - (device - 1) * NB
    eq = iota((NB, NB), 0) == iota((NB, NB), 1)
    count = jnp.sum(jnp.where(eq, jnp.broadcast_to(cnt[...], (NB, NB)).astype(F32), 0.0), axis=1, keepdims=True)
    w = jnp.zeros((NB, 128), F32)
    at = iota((NB, 128), 1)
    for s in range(KN):
        live = jnp.where(count > s, 1.0, 0.0)
        w = w + jnp.where(at == local[:, s:s + 1], live, 0.0)
    return w


def heat_blocks(wb, pair_r, vt, jt, it, aj, hrow, acc, start, stop, turns):
    def block(b, _):
        half = hrow[b, 0:1, :]
        itb = it[b]
        others = [b + e + NB * ((b + e) // NB) for e in range(NB + 1)]
        ahead = [(b + d) % NB for d in range(turns)]
        others += [NB + o for o in ahead]
        left = []
        for n, o in enumerate(others):
            e = dot(jt[o], itb, 1, 0)
            a = aj[o]
            for h in range(2):
                sl = slice(h * 128, (h + 1) * 128)
                q = (a + half[:, sl]).reshape(PB // 16, 2, 8, 128)
                q0, q1 = q[:, 0], q[:, 1]
                inv = 1.0 / (q0 * q1)
                f = jnp.stack([q1 * inv, q0 * inv], 1).reshape(PB, 128)
                pair_r[n * PB:(n + 1) * PB, sl] = (jnp.exp2(e[:, sl]) * f).astype(BF)
            w = wb[b, pl.ds(o, 1), :]
            left.append(vt[o] * jnp.concatenate([w, w], 1))
        count = len(others) * PB
        acc[b] += dot(jnp.concatenate(left, 1).astype(BF), pair_r[0:count], 1, 0)
        for d in range(1, turns):
            n = NB + 1 + d
            w = wb[ahead[d], pl.ds(NB + b, 1), :]
            back = (vt[NB + b] * jnp.concatenate([w, w], 1)).astype(BF)
            acc[ahead[d]] += dot(back, pair_r[n * PB:(n + 1) * PB], 1, 1)
        return 0

    lax.fori_loop(start, stop, block, 0)


COPIES = 7 + 2 + 4 + 12 + 15 + 8 + 15 + 7


def main_call(nbr, cnt, *args):
    vm = pl.BlockSpec(memory_space=pltpu.VMEM)
    hbm = pl.BlockSpec(memory_space=pltpu.HBM)
    s = lambda *shape: pltpu.VMEM(shape, F32)
    i = lambda *shape: pltpu.VMEM(shape, jnp.int32)
    return pl.pallas_call(
        main_kernel,
        out_shape=[
            jax.ShapeDtypeStruct((GZ, CX, CY), F32),
            jax.ShapeDtypeStruct((1, PD), F32),
        ],
        in_specs=[hbm] * 13,
        out_specs=[vm, vm],
        scratch_shapes=[
            i(NB, KN), i(1, NB), s(3, PD), s(1, PD), s(16, 128), s(1, PD), i(1, NE), i(1, NE), i(1, NE),
            i(1, 256), s(1, 256),
            s(2, GZ + 1, BX, CY), s(GZ + 1, BX, CY), s(2, BX, CY), s(2, BX, CY),
            s(2, BX, 128), s(CX, CY), s(CX, CY), s(2, BX, 128),
            s(2, CX, CY), s(2, 2, BX, CY),
            s(128, 128), s(NF, NS, 128), s(NS, NF, 128), s(NS, NF, 128),
            s(NS, NF, 128), s(NS, NF, 128), s(NF, NS, 128), s(NF, NS, 128),
            pltpu.VMEM((128, NE), BF), s(CAP, NE), pltpu.VMEM((128, NE), BF),
            s(BX, CY), s(BX, CY), s(8, PD), s(3, 8, PD), s(3 * NB, 8, PB), s(NB, 128, 128), pltpu.VMEM((WIN * PB, PB), BF),
            pltpu.VMEM((3 * NB, PB, 128), BF), pltpu.VMEM((NB, 128, PB), BF),
            s(3 * NB, PB, 128), s(NB, 8, PB), s(NB, 8, PB), s(1, PD),
            pltpu.SemaphoreType.DMA((14,)),
            pltpu.SemaphoreType.DMA((COPIES,)),
            pltpu.SemaphoreType.DMA((COPIES,)),
        ],
        compiler_params=pltpu.CompilerParams(
            collective_id=0, has_side_effects=True, vmem_limit_bytes=32 * 2**20),
        name="step",
    )(*(pltpu.with_memory_space_constraint(x, pltpu.HBM) for x in (nbr, cnt) + args))


def body(positions, particle_temp, volume, nbr_blocks, nbr_count, iface_part, iface_owner,
         iface_cell, substrate_temp, conduct, laser_cells, laser_power):
    field, particle_out = main_call(
        nbr_blocks, nbr_count.reshape(1, NB), positions, particle_temp.reshape(1, PD), particle_temp.reshape(16, 128), volume.reshape(1, PD),
        iface_part.reshape(1, NE), iface_owner.reshape(1, NE), iface_cell.reshape(1, NE),
        laser_cells.reshape(1, -1), laser_power.reshape(1, -1), substrate_temp, conduct)
    return particle_out.reshape(PD), field


def solution(mesh):
    in_specs = (
        P(None, ("sph", "fv")),
        P(("sph", "fv")),
        P(("sph", "fv")),
        P(("sph", "fv"), None),
        P(("sph", "fv")),
        P(("sph", "fv")),
        P(("sph", "fv"), None),
        P(("sph", "fv")),
        P(None, "sph", "fv"),
        P(None, "sph", "fv"),
        P(),
        P(),
    )
    out_specs = (P(("sph", "fv")), P(None, "sph", "fv"))
    return jax.shard_map(body, mesh=mesh, in_specs=in_specs, out_specs=out_specs, check_vma=False)
```

```python
import functools

import jax
import jax.numpy as jnp
from jax import lax
from jax.experimental import pallas as pl
from jax.experimental.pallas import tpu as pltpu
from jax.sharding import PartitionSpec as P

SUB = 4
KERNEL_SCALE = 0.5
SPH_STEP = 0.05
CONTACT_GAIN = 1.0
PARTICLE_SHARE = 0.5
SURFACE_GAIN = 0.5
LAMBDA_STEP = 0.1
NS, NF = 16, 8
CX, CY, GZ = 32, 256, 32
BX = 40
PB, NB, KN, CAP = 256, 8, 16, 16
PD, NE = 2048, 1024
MESH = pl.DeviceIdType.MESH
F32, BF = jnp.float32, jnp.bfloat16
LOG2E = 1.4426950408889634


def split2(x):
    a = x.astype(BF)
    return a, (x - a.astype(F32)).astype(BF)


def dot(a, b, ca, cb):
    return lax.dot_general(a, b, (((ca,), (cb,)), ((), ())), preferred_element_type=F32)


def iota(shape, dim):
    return lax.broadcasted_iota(jnp.int32, shape, dim)


def hot(rows, row_index):
    return jnp.where(iota((rows, row_index.shape[1]), 0) == row_index, 1.0, 0.0)


def keep(rows, row_index, value):
    return jnp.where(iota((rows, row_index.shape[1]), 0) == row_index, value, 0.0)


def faces(remote, left, right, into_right, into_left, S, F, sn, sp, fn, fp):
    return [
        remote(left, into_right.at[pl.ds(0, CX)], (S, fp)),
        remote(right, into_left.at[pl.ds(0, CX)], (S, fn)),
        remote(left.at[pl.ds(0, 4)], into_right.at[pl.ds(32, 4)], (sp, fp)),
        remote(left.at[pl.ds(28, 4)], into_right.at[pl.ds(36, 4)], (sn, fp)),
        remote(right.at[pl.ds(0, 4)], into_left.at[pl.ds(32, 4)], (sp, fn)),
        remote(right.at[pl.ds(28, 4)], into_left.at[pl.ds(36, 4)], (sn, fn)),
    ]


GROUP = 4


def main_kernel(
    h_nbr, h_cnt, h_pos, h_temp1, h_temp16, h_vol, h_ipart, h_iown, h_icell, h_lcell, h_lpow, sub, cond,
    outv, pout,
    nbr, cnt, pos, temp1, temp16, vol, ipart, iown, icell, lcell, lpow,
    U, C, su, sc, fs, surf, top, ty, pk_s, pk_r,
    send1, recv1, send2, recv2, rsend1, rret1, rsend2, rret2,
    pt, qt, ohp_lo, fz_ref, kc_ref, pack, ext, vt, wsend, wrecv, wb, pair_r, jt, it, aj, hrow, hacc, hrecv, heat, lsem, ssem, rsem,
):
    S = lax.axis_index("sph")
    F = lax.axis_index("fv")
    sn, sp = (S + 1) % NS, (S + NS - 1) % NS
    fn, fp = (F + 1) % NF, (F + NF - 1) % NF

    barrier = pltpu.get_barrier_semaphore()
    partners = [(S, (F + d) % NF) for d in range(1, NF)]
    partners += [((S + d) % NS, F) for d in range(1, NS)]
    partners += [(sn, fn), (sn, fp), (sp, fn), (sp, fp)]
    for who in partners:
        pl.semaphore_signal(barrier, inc=1, device_id=who, device_id_type=MESH)

    small = [
        pltpu.make_async_copy(a, b, lsem.at[3 + n]) for n, (a, b) in enumerate((
            (h_ipart, ipart), (h_temp16, temp16), (h_iown, iown), (h_icell, icell), (h_pos, pos), (h_temp1, temp1),
            (h_vol, vol), (h_nbr, nbr), (h_cnt, cnt), (h_lcell, lcell), (h_lpow, lpow)))
    ]
    for c in small:
        c.start()

    lc = [
        pltpu.make_async_copy(sub.at[0], surf, lsem.at[0]),
        pltpu.make_async_copy(sub.at[pl.ds(1, GZ - 1)], U.at[0, pl.ds(1, GZ - 1), pl.ds(0, CX)], lsem.at[1]),
        pltpu.make_async_copy(cond, C.at[pl.ds(0, GZ), pl.ds(0, CX)], lsem.at[2]),
    ]
    for c in lc:
        c.start()

    count = [0]

    def remote(src, dst, who):
        i = count[0]
        count[0] += 1
        c = pltpu.make_async_remote_copy(
            src_ref=src, dst_ref=dst, send_sem=ssem.at[i], recv_sem=rsem.at[i],
            device_id=who, device_id_type=MESH)
        c.start()
        return c

    for c in small:
        c.wait()

    pack[...] = jnp.concatenate([pos[...], temp1[...], vol[...], jnp.zeros((3, PD), F32)], 0)

    wsend[...] = live_weights(nbr, cnt, S * NF + F)

    own = iown[...]
    row_of = (own % NF) * NS + own // NF
    part = ipart[...]
    php = hot(16, part // 128).astype(BF)
    plo = hot(128, part % 128)
    ohp_lo[...] = plo.astype(BF)
    tval = sum(dot(t, php, 0, 0) for t in split2(temp16[...]))
    tval = jnp.sum(tval * plo, axis=0, keepdims=True)
    po = hot(128, row_of)
    pb = po.astype(BF)
    pt[...] = pb
    tri = jnp.where(iota((256, 256), 0) < iota((256, 256), 1), 1.0, 0.0).astype(BF)
    ones = jnp.ones((256, 256), BF)
    run = jnp.zeros((128, 256), F32)
    ranks = []
    for k in range(NE // 256):
        pc = pb[:, k * 256:(k + 1) * 256]
        cum = dot(pc, tri, 1, 0) + run
        run = run + dot(pc, ones, 1, 0)
        ranks.append(jnp.sum(cum * po[:, k * 256:(k + 1) * 256], axis=0, keepdims=True))
    rank = jnp.concatenate(ranks, 1)
    q = jnp.where(iota((CAP, NE), 0).astype(F32) == rank, 1.0, 0.0)
    qt[...] = q
    c1 = icell[...] + 1
    chi = (c1 // 256 * 256).astype(F32)
    clo = (c1 % 256).astype(F32)
    v0, v1 = split2(tval)
    zero = jnp.zeros((96, NE), BF)

    def rows(a, b):
        return jnp.concatenate([jnp.concatenate([a, b], 0).astype(BF), zero], 0)

    send1[...] = (
        dot(pb, rows(q * chi, q * v0.astype(F32)), 1, 1)
        + dot(pb, rows(q * clo, q * v1.astype(F32)), 1, 1)
    )

    pl.semaphore_wait(barrier, len(partners))

    ph1 = []
    for d in range(1, NF):
        f = (F + d) % NF
        ph1.append(remote(send1.at[pl.ds(pl.multiple_of(f * NS, NS), NS)], recv1.at[F], (S, f)))
    recv1[pl.ds(F, 1)] = send1[pl.ds(pl.multiple_of(F * NS, NS), NS)].reshape(1, NS, 128)

    nxt = ((S + (F + 1) // NF) % NS, fn)
    prv = ((S + NS - (NF - F) // NF) % NS, fp)
    pcs = [remote(pack, ext.at[1], prv), remote(wsend, wrecv, prv)]
    ext[0] = pack[...]

    halo = []
    for src, dst, lo in ((sub, U.at[0], 1), (cond, C, 0)):
        n = GZ - lo
        halo.append(remote(src.at[pl.ds(lo, n), pl.ds(0, 4)], dst.at[pl.ds(lo, n), pl.ds(32, 4)], (sp, F)))
        halo.append(remote(src.at[pl.ds(lo, n), pl.ds(28, 4)], dst.at[pl.ds(lo, n), pl.ds(36, 4)], (sn, F)))

    for c in lc:
        c.wait()
    U[0, GZ] = jnp.zeros((BX, CY), F32)
    U[1, GZ] = jnp.zeros((BX, CY), F32)
    C[GZ] = jnp.zeros((BX, CY), F32)
    def packed(src, lo, hi):
        n = hi - lo
        l = iota((n, 128), 1)
        halves = []
        for half in range(2):
            acc = jnp.zeros((n, 128), F32)
            for w in range(16):
                z = half * 16 + w
                x = jnp.where(l < 64, src[z, lo:hi, 0:128], src[z, lo:hi, 128:256])
                acc = jnp.where(l // 8 == w, pltpu.roll(x, (8 * w + 4) % 128, 1), acc)
            halves.append(acc)
        return jnp.concatenate(halves, 1)

    for a in range(2):
        pk_s[a] = packed(U.at[0] if a == 0 else C, 0, CX)
        halo += faces(remote, pk_s.at[a], pk_s.at[a], pk_r.at[a, 1], pk_r.at[a, 0], S, F, sn, sp, fn, fp)

    for c in ph1:
        c.wait_recv()
    send2[...] = jnp.swapaxes(recv1[...], 0, 1)
    ph2 = []
    for d in range(1, NS):
        s = (S + d) % NS
        ph2.append(remote(send2.at[s], recv2.at[S], (s, F)))
    recv2[pl.ds(S, 1)] = send2[pl.ds(S, 1)]

    for c in pcs:
        c.wait_recv()
    heat_prep(ext, vt, jt, it, aj, hrow)
    hacc[...] = jnp.zeros((2 * NB, 8, PB), F32)
    sub8 = iota((NB, 16), 0)
    one8 = jnp.ones((NB, 128), BF)
    for t, w in enumerate((wsend[:, NB:NB + 16], wrecv[:, 0:16])):
        for b in range(NB):
            wb[t * NB + b] = dot(jnp.where(sub8 == b, w, 0.0).astype(BF), one8, 0, 0)
    heat_blocks(wb, pair_r, vt, jt, it, aj, hrow, hacc, 0, NB // 2)

    for c in ph2:
        c.wait_recv()
    rt = jnp.transpose(recv2[...].reshape(128, 128))
    cf = jnp.concatenate([rt[s:s + 1, :] for s in range(CAP)], 1)
    tf = jnp.concatenate([rt[CAP + s:CAP + s + 1, :] for s in range(CAP)], 1)
    ci = cf.astype(jnp.int32) - 1
    live = ci >= 0
    hi = jnp.where(live, ci // 256 + (ci % 256) // 128 * CX, -1)
    lo = jnp.where(live, ci % 128, -1)
    sf = surf[...]
    ss = jnp.concatenate(split2(jnp.concatenate([sf[:, 0:128], sf[:, 128:256]], 0)), 0)
    cons = []
    W = 512
    for k in range(2048 // W):
        sl = slice(k * W, (k + 1) * W)
        ob = hot(64, hi[:, sl]).astype(BF)
        g = dot(ss, jnp.concatenate([ob, ob], 0), 0, 0)
        ghost = jnp.sum(keep(128, lo[:, sl], g), axis=0, keepdims=True)
        cons.append(jnp.where(live[:, sl], CONTACT_GAIN * (tf[:, sl] - ghost), 0.0))
    lc_ = lcell[...]
    lx, ly = lc_ // (NF * CY), lc_ % (NF * CY)
    mine = (lx // CX == S) & (ly // CY == F)
    lhi = jnp.where(mine, lx % CX + (ly % CY) // 128 * CX, -1)
    llo = jnp.where(mine, ly % 128, -1)
    fl = jnp.zeros((128, 128), F32)
    parts = [(hi[:, k * W:(k + 1) * W], lo[:, k * W:(k + 1) * W], cons[k]) for k in range(2048 // W)]
    for h, l, value in parts + [(lhi, llo, lpow[...])]:
        ch = jnp.concatenate([keep(64, h, v.astype(F32)) for v in split2(value)], 0).astype(BF)
        fl = fl + dot(ch, hot(128, l).astype(BF), 1, 1)
    fl = fl[0:64] + fl[64:128]
    top[...] = sf + SURFACE_GAIN * jnp.concatenate([fl[0:32], fl[32:64]], 1)
    con = jnp.concatenate(cons, 1)

    th = [
        remote(top.at[pl.ds(0, 4)], U.at[0, 0, pl.ds(32, 4)], (sp, F)),
        remote(top.at[pl.ds(28, 4)], U.at[0, 0, pl.ds(36, 4)], (sn, F)),
    ]
    th += faces(remote, top.at[:, pl.ds(0, 128)], top.at[:, pl.ds(128, 128)], ty.at[1], ty.at[0], S, F, sn, sp, fn, fp)

    back = jnp.concatenate([con[:, s * 128:(s + 1) * 128] for s in range(CAP)] + [jnp.zeros((112, 128), F32)], 0)
    rsend1[...] = jnp.transpose(back).reshape(NS, NF, 128)
    rh1 = []
    for d in range(1, NS):
        s = (S + d) % NS
        rh1.append(remote(rsend1.at[s], rret1.at[S], (s, F)))
    rret1[pl.ds(S, 1)] = rsend1[pl.ds(S, 1)]

    heat_blocks(wb, pair_r, vt, jt, it, aj, hrow, hacc, NB // 2, NB)
    hc = remote(hacc.at[pl.ds(NB, NB)], hrecv, nxt)

    for c in halo:
        c.wait_recv()
    row = iota((BX, CY), 0)
    lane = iota((BX, CY), 1)
    up = (S > 0).astype(F32)
    down = (S < NS - 1).astype(F32)
    rmask = jnp.where(row < 32, 1.0, jnp.where(row < 36, down, up))
    smask = [
        rmask * jnp.where(lane % 8 < 4, (F > 0).astype(F32), 1.0),
        rmask * jnp.where(lane % 8 < 4, 1.0, (F < NF - 1).astype(F32)),
    ]
    xmask = rmask[32:40]

    @pl.when(S == 0)
    def _():
        U[0, 1:GZ, 36:40, :] = jnp.zeros((GZ - 1, 4, CY), F32)
        C[0:GZ, 36:40, :] = jnp.zeros((GZ, 4, CY), F32)

    @pl.when(S == NS - 1)
    def _():
        U[0, 1:GZ, 32:36, :] = jnp.zeros((GZ - 1, 4, CY), F32)
        C[0:GZ, 32:36, :] = jnp.zeros((GZ, 4, CY), F32)

    for c in th:
        c.wait_recv()
    U[0, 0, 0:CX] = top[...]
    U[0, 0, 32:40] = U[0, 0, 32:40] * xmask
    zero_z = lane < 8
    l128 = iota((BX, 128), 1)
    for a in range(2):
        src = U.at[0] if a == 0 else C
        mine_ = jnp.concatenate([pk_s[a], packed(src, 32, 40)], 0)
        for side in range(2):
            first = (pk_r[a, side], mine_) if side == 0 else (mine_, pk_r[a, side])
            v = jnp.where(lane % 8 < 4, first[0], first[1])
            if a == 0:
                o = U[0, 0, :, side * 128:(side + 1) * 128]
                near = (o, ty[side]) if side == 0 else (ty[side], o)
                near = pltpu.roll(jnp.where(l128 < 64, near[0], near[1]), 4, 1)
                v = jnp.where(zero_z, jnp.concatenate([near, near], 1), v)
                su[side] = v * smask[side]
            else:
                sc[side] = v * smask[side]

    G = LAMBDA_STEP * 0.5

    def conductivity(u, c):
        return c * (G + (0.5 * G) * jnp.tanh(u))

    def along_x(u, k):
        fx = (k + pltpu.roll(k, BX - 1, 0)) * (pltpu.roll(u, BX - 1, 0) - u)
        return fx - pltpu.roll(fx, 1, 0)

    lane1 = iota((BX, 128), 1)
    first_lane, last_lane = lane1 == 0, lane1 == 127
    for step in range(SUB):
        a, b = step % 2, 1 - step % 2
        last = step == SUB - 1
        for side in range(2):
            u, c = su[side], sc[side]
            k = conductivity(u, c)
            fy = (k + pltpu.roll(k, CY - 1, 1)) * (pltpu.roll(u, CY - 1, 1) - u)
            if side == 0:
                face = pltpu.roll(fy, 1, 1)
            else:
                face = jnp.where(lane % 8 == 4, face, fy)
                fs[0] = face[:, 0:128]
                fs[1] = face[:, 128:256]
            if not last:
                below = lane >= CY - 8
                un = jnp.where(below, 0.0, pltpu.roll(u, CY - 8, 1))
                kn = jnp.where(below, k, pltpu.roll(k, CY - 8, 1))
                fz = (k + kn) * (un - u)
                fup = jnp.where(lane < 8, 0.0, pltpu.roll(fz, 8, 1))
                net = (fy - pltpu.roll(fy, 1, 1)) + (fz - fup) + along_x(u, k)
                su[side] = (u + net) * smask[side]

        kc_ref[...] = conductivity(U[a, 0], C[0])
        fz_ref[...] = jnp.zeros((BX, CY), F32)

        def layers(n, _):
            z0 = n * GROUP
            k, fz0 = kc_ref[...], fz_ref[...]
            u = U[a, z0]
            for m in range(GROUP):
                z = z0 + m
                un = U[a, z + 1]
                kn = conductivity(un, C[z + 1])
                if m == GROUP - 1:
                    kf = jnp.where(z == GZ - 1, k, kn)
                else:
                    kf = kn
                fz = (k + kf) * (un - u)
                net = along_x(u, k) + (fz - fz0)
                w = z % 16
                kl, kr = k[:, 0:128], k[:, 128:256]
                ul, ur = u[:, 0:128], u[:, 128:256]
                skl, skr = pltpu.roll(kl, 127, 1), pltpu.roll(kr, 127, 1)
                sul, sur = pltpu.roll(ul, 127, 1), pltpu.roll(ur, 127, 1)
                fyl = (kl + jnp.where(last_lane, skr, skl)) * (jnp.where(last_lane, sur, sul) - ul)
                fyr = (kr + skr) * (sur - ur)
                edge = pltpu.roll(fs[z // 16], (124 + 128 - 8 * w) % 128, 1)
                fyr = jnp.where(last_lane, edge, fyr)
                bl, br = pltpu.roll(fyl, 1, 1), pltpu.roll(fyr, 1, 1)
                nl = fyl - jnp.where(first_lane, edge, bl)
                nr = fyr - jnp.where(first_lane, bl, br)
                new = u + (net + jnp.concatenate([nl, nr], 1))
                if last:
                    outv[z] = new[0:CX]
                else:
                    U[b, z, 0:CX] = new[0:CX]
                    U[b, z, 32:40] = new[32:40] * xmask
                u, k, fz0 = un, kn, fz
            kc_ref[...] = k
            fz_ref[...] = fz0
            return 0

        lax.fori_loop(0, GZ // GROUP, layers, 0)

        if step == 1:
            for c in rh1:
                c.wait_recv()
            rsend2[...] = jnp.swapaxes(rret1[...], 0, 1)
            rh2 = []
            for d in range(1, NF):
                f = (F + d) % NF
                rh2.append(remote(rsend2.at[f], rret2.at[F], (S, f)))
            rret2[pl.ds(F, 1)] = rsend2[pl.ds(F, 1)]

    for c in rh2:
        c.wait_recv()
    rr = rret2[...].reshape(128, 128)[:, 0:CAP]
    x = sum(dot(v, pt[...], 0, 0) for v in split2(rr))
    cval = jnp.sum(x * qt[...], axis=0, keepdims=True)
    ph = ipart[...] // 128
    pf = sum(dot(keep(16, ph, v.astype(F32)).astype(BF), ohp_lo[...], 1, 1) for v in split2(cval))
    pflux = jnp.concatenate([pf[r:r + 1, :] for r in range(16)], 1)
    hc.wait_recv()
    for b in range(NB):
        h8 = hacc[b] + hrecv[b]
        warm, amount = h8[0:1] + h8[1:2] + h8[2:3], h8[3:4] + h8[4:5] + h8[5:6]
        at = slice(b * PB, (b + 1) * PB)
        heat[:, at] = warm - temp1[:, at] * amount
    pout[...] = temp1[...] + SPH_STEP * heat[...] - PARTICLE_SHARE * pflux

    for c in [hc] + ph1 + pcs + halo + ph2 + th + rh1 + rh2:
        c.wait_send()


UNROLL = 8


def groups3(x):
    a = x.astype(BF).astype(F32)
    r = x - a
    b = r.astype(BF).astype(F32)
    return [a, b, r - b]


def heat_prep(ext, vt, jt, it, aj, hrow):
    scale = (LOG2E * 2.0 * KERNEL_SCALE) ** 0.5
    r32, c256 = iota((32, 256), 0), iota((32, 256), 1)
    rep = jnp.where((c256 < 72) & (c256 % 24 == r32), 1.0, 0.0)
    tail = jnp.where((c256 >= 128) & (r32 >= 24) & (r32 < 27), 1.0, 0.0)
    spread = (rep + tail).astype(BF)
    row = iota((8, PB), 0)

    def place(*rows):
        out = jnp.zeros((8, PB), F32)
        for n, r in enumerate(rows):
            out = jnp.where(row == n, r, out)
        return out

    for t in range(2):
        def prep(n, _):
            for m in range(UNROLL):
                b = n * UNROLL + m
                at = pl.ds(pl.multiple_of(b * PB, PB), PB)
                blk = ext[t, :, at]
                p = jnp.where(row < 3, blk * scale, 0.0)
                norm = -0.5 * jnp.sum(p * p, axis=0, keepdims=True)
                temp = blk[3:4]
                volume = blk[4:5] * (2.0 * KERNEL_SCALE)
                half = 0.5 / (1.0 + 0.5 * jnp.tanh(temp))
                packed = groups3(place(half, volume * temp, volume))
                vt[t * NB + b] = place(
                    packed[0][1:2], packed[1][1:2], packed[2][1:2], packed[0][2:3], packed[1][2:3], packed[2][2:3])
                ah = place(packed[0][0:1], packed[1][0:1], packed[2][0:1])
                sj = groups3(jnp.where(row == 3, norm, jnp.where(row == 4, 1.0, p)))
                both = dot(jnp.concatenate(sj + [ah], 0).astype(BF), spread, 0, 0)
                jt[t * NB + b] = both[:, 0:128].astype(BF)
                aj[t * NB + b] = both[:, 128:256]
                if t == 0:
                    hrow[b] = jnp.broadcast_to(half, (8, PB))
                    i0, i1, i2 = groups3(jnp.where(row == 3, 1.0, jnp.where(row == 4, norm, p)))
                    z = jnp.zeros((128 - 72, PB), F32)
                    it[b] = jnp.concatenate([i0, i0, i0, i1, i1, i1, i2, i2, i2, z], 0).astype(BF)
            return 0

        lax.fori_loop(0, NB // UNROLL, prep, 0)


def live_weights(nbr, cnt, device):
    local = nbr[...] - (device - 1) * NB
    eq = iota((NB, NB), 0) == iota((NB, NB), 1)
    count = jnp.sum(jnp.where(eq, jnp.broadcast_to(cnt[...], (NB, NB)).astype(F32), 0.0), axis=1, keepdims=True)
    w = jnp.zeros((NB, 128), F32)
    at = iota((NB, 128), 1)
    for s in range(KN):
        live = jnp.where(count > s, 1.0, 0.0)
        w = w + jnp.where(at == local[:, s:s + 1], live, 0.0)
    return w


def heat_blocks(wb, pair_r, vt, jt, it, aj, hrow, acc, start, stop):
    def block(b, _):
        half = hrow[b, 0:1, :]
        itb = it[b]
        left = []
        for n in range(NB + 1):
            o = b + n
            e = dot(jt[o], itb, 1, 0)
            a = aj[o]
            for h in range(2):
                sl = slice(h * 128, (h + 1) * 128)
                q = (a + half[:, sl]).reshape(PB // 16, 2, 8, 128)
                q0, q1 = q[:, 0], q[:, 1]
                inv = 1.0 / (q0 * q1)
                f = jnp.stack([q1 * inv, q0 * inv], 1).reshape(PB, 128)
                pair_r[n * PB:(n + 1) * PB, sl] = (jnp.exp2(e[:, sl]) * f).astype(BF)
            w = wb[b, pl.ds(o, 1), :]
            left.append(vt[o] * jnp.concatenate([w, w], 1))
        acc[b] += dot(jnp.concatenate(left, 1).astype(BF), pair_r[...], 1, 0)
        for n in range(1, NB + 1):
            w = wb[b + n, pl.ds(b, 1), :]
            back = (vt[b] * jnp.concatenate([w, w], 1)).astype(BF)
            acc[b + n] += dot(back, pair_r[n * PB:(n + 1) * PB], 1, 1)
        return 0

    lax.fori_loop(start, stop, block, 0)


COPIES = 7 + 3 + 4 + 12 + 15 + 8 + 15 + 7


def main_call(nbr, cnt, *args):
    vm = pl.BlockSpec(memory_space=pltpu.VMEM)
    hbm = pl.BlockSpec(memory_space=pltpu.HBM)
    s = lambda *shape: pltpu.VMEM(shape, F32)
    i = lambda *shape: pltpu.VMEM(shape, jnp.int32)
    return pl.pallas_call(
        main_kernel,
        out_shape=[
            jax.ShapeDtypeStruct((GZ, CX, CY), F32),
            jax.ShapeDtypeStruct((1, PD), F32),
        ],
        in_specs=[hbm] * 13,
        out_specs=[vm, vm],
        scratch_shapes=[
            i(NB, KN), i(1, NB), s(3, PD), s(1, PD), s(16, 128), s(1, PD), i(1, NE), i(1, NE), i(1, NE),
            i(1, 256), s(1, 256),
            s(2, GZ + 1, BX, CY), s(GZ + 1, BX, CY), s(2, BX, CY), s(2, BX, CY),
            s(2, BX, 128), s(CX, CY), s(CX, CY), s(2, BX, 128),
            s(2, CX, CY), s(2, 2, BX, CY),
            s(128, 128), s(NF, NS, 128), s(NS, NF, 128), s(NS, NF, 128),
            s(NS, NF, 128), s(NS, NF, 128), s(NF, NS, 128), s(NF, NS, 128),
            pltpu.VMEM((128, NE), BF), s(CAP, NE), pltpu.VMEM((128, NE), BF),
            s(BX, CY), s(BX, CY), s(8, PD), s(2, 8, PD), s(2 * NB, 8, PB), s(NB, 128), s(NB, 128), s(2 * NB, 16, 128),
            pltpu.VMEM(((NB + 1) * PB, PB), BF),
            pltpu.VMEM((2 * NB, PB, 128), BF), pltpu.VMEM((NB, 128, PB), BF),
            s(2 * NB, PB, 128), s(NB, 8, PB), s(2 * NB, 8, PB), s(NB, 8, PB), s(1, PD),
            pltpu.SemaphoreType.DMA((14,)),
            pltpu.SemaphoreType.DMA((COPIES,)),
            pltpu.SemaphoreType.DMA((COPIES,)),
        ],
        compiler_params=pltpu.CompilerParams(
            collective_id=0, has_side_effects=True, vmem_limit_bytes=32 * 2**20),
        name="step",
    )(*(pltpu.with_memory_space_constraint(x, pltpu.HBM) for x in (nbr, cnt) + args))


def body(positions, particle_temp, volume, nbr_blocks, nbr_count, iface_part, iface_owner,
         iface_cell, substrate_temp, conduct, laser_cells, laser_power):
    field, particle_out = main_call(
        nbr_blocks, nbr_count.reshape(1, NB), positions, particle_temp.reshape(1, PD), particle_temp.reshape(16, 128), volume.reshape(1, PD),
        iface_part.reshape(1, NE), iface_owner.reshape(1, NE), iface_cell.reshape(1, NE),
        laser_cells.reshape(1, -1), laser_power.reshape(1, -1), substrate_temp, conduct)
    return particle_out.reshape(PD), field


def solution(mesh):
    in_specs = (
        P(None, ("sph", "fv")),
        P(("sph", "fv")),
        P(("sph", "fv")),
        P(("sph", "fv"), None),
        P(("sph", "fv")),
        P(("sph", "fv")),
        P(("sph", "fv"), None),
        P(("sph", "fv")),
        P(None, "sph", "fv"),
        P(None, "sph", "fv"),
        P(),
        P(),
    )
    out_specs = (P(("sph", "fv")), P(None, "sph", "fv"))
    return jax.shard_map(body, mesh=mesh, in_specs=in_specs, out_specs=out_specs, check_vma=False)
```

```python
import functools

import jax
import jax.numpy as jnp
from jax import lax
from jax.experimental import pallas as pl
from jax.experimental.pallas import tpu as pltpu
from jax.sharding import PartitionSpec as P

SUB = 4
KERNEL_SCALE = 0.5
SPH_STEP = 0.05
CONTACT_GAIN = 1.0
PARTICLE_SHARE = 0.5
SURFACE_GAIN = 0.5
LAMBDA_STEP = 0.1
NS, NF = 16, 8
CX, CY, GZ = 32, 256, 32
BX = 40
PB, NB, KN, CAP = 256, 8, 16, 16
PD, NE = 2048, 1024
MESH = pl.DeviceIdType.MESH
F32, BF = jnp.float32, jnp.bfloat16
LOG2E = 1.4426950408889634


def split2(x):
    a = x.astype(BF)
    return a, (x - a.astype(F32)).astype(BF)


def dot(a, b, ca, cb):
    return lax.dot_general(a, b, (((ca,), (cb,)), ((), ())), preferred_element_type=F32)


def iota(shape, dim):
    return lax.broadcasted_iota(jnp.int32, shape, dim)


def hot(rows, row_index):
    return jnp.where(iota((rows, row_index.shape[1]), 0) == row_index, 1.0, 0.0)


def hot16(rows, row_index):
    return keep16(rows, row_index, jnp.ones((), BF))


def keep16(rows, row_index, value):
    at = iota((rows, row_index.shape[1]), 0).astype(BF)
    return jnp.where(at == row_index.astype(F32).astype(BF), value, jnp.zeros((), BF))


def keep(rows, row_index, value):
    return jnp.where(iota((rows, row_index.shape[1]), 0) == row_index, value, 0.0)


def faces(remote, left, right, into_right, into_left, S, F, sn, sp, fn, fp):
    return [
        remote(left, into_right.at[pl.ds(0, CX)], (S, fp)),
        remote(right, into_left.at[pl.ds(0, CX)], (S, fn)),
        remote(left.at[pl.ds(0, 4)], into_right.at[pl.ds(32, 4)], (sp, fp)),
        remote(left.at[pl.ds(28, 4)], into_right.at[pl.ds(36, 4)], (sn, fp)),
        remote(right.at[pl.ds(0, 4)], into_left.at[pl.ds(32, 4)], (sp, fn)),
        remote(right.at[pl.ds(28, 4)], into_left.at[pl.ds(36, 4)], (sn, fn)),
    ]


GROUP = 4


def main_kernel(
    h_nbr, h_cnt, h_pos, h_temp1, h_temp16, h_vol, h_ipart, h_iown, h_icell, h_lcell, h_lpow, sub, cond,
    outv, pout,
    nbr, cnt, pos, temp1, temp16, vol, ipart, iown, icell, lcell, lpow,
    U, C, su, sc, fs, surf, top, ty, pk_s, pk_r,
    send1, recv1, send2, recv2, rsend1, rret1, rsend2, rret2,
    pt, qt, ohp_lo, fz_ref, kc_ref, pack, ext, vt, wsend, wrecv, wb, pair_r, jt, it, aj, hrow, hacc, hrecv, heat, lsem, ssem, rsem,
):
    S = lax.axis_index("sph")
    F = lax.axis_index("fv")
    sn, sp = (S + 1) % NS, (S + NS - 1) % NS
    fn, fp = (F + 1) % NF, (F + NF - 1) % NF

    barrier = pltpu.get_barrier_semaphore()
    partners = [(S, (F + d) % NF) for d in range(1, NF)]
    partners += [((S + d) % NS, F) for d in range(1, NS)]
    partners += [(sn, fn), (sn, fp), (sp, fn), (sp, fp)]
    for who in partners:
        pl.semaphore_signal(barrier, inc=1, device_id=who, device_id_type=MESH)

    small = [
        pltpu.make_async_copy(a, b, lsem.at[3 + n]) for n, (a, b) in enumerate((
            (h_ipart, ipart), (h_temp16, temp16), (h_iown, iown), (h_icell, icell), (h_pos, pos), (h_temp1, temp1),
            (h_vol, vol), (h_nbr, nbr), (h_cnt, cnt), (h_lcell, lcell), (h_lpow, lpow)))
    ]
    for c in small:
        c.start()

    lc = [
        pltpu.make_async_copy(sub.at[0], surf, lsem.at[0]),
        pltpu.make_async_copy(sub.at[pl.ds(1, GZ - 1)], U.at[0, pl.ds(1, GZ - 1), pl.ds(0, CX)], lsem.at[1]),
        pltpu.make_async_copy(cond, C.at[pl.ds(0, GZ), pl.ds(0, CX)], lsem.at[2]),
    ]
    for c in lc:
        c.start()

    count = [0]

    def remote(src, dst, who, i=None):
        if i is None:
            i = count[0]
            count[0] += 1
        c = pltpu.make_async_remote_copy(
            src_ref=src, dst_ref=dst, send_sem=ssem.at[i], recv_sem=rsem.at[i],
            device_id=who, device_id_type=MESH)
        c.start()
        return c

    for c in small:
        c.wait()

    def group():
        count[0] += 1
        return count[0] - 1

    def all_of(src, dst, i):
        return pltpu.make_async_remote_copy(
            src_ref=src, dst_ref=dst, send_sem=ssem.at[i], recv_sem=rsem.at[i],
            device_id=(sn, F), device_id_type=MESH)

    pack[...] = jnp.concatenate([pos[...], temp1[...], vol[...], jnp.zeros((3, PD), F32)], 0)

    wsend[...] = live_weights(nbr, cnt, S * NF + F)

    own = iown[...]
    row_of = (own % NF) * NS + own // NF
    part = ipart[...]
    php = hot16(16, part // 128)
    ohp_lo[...] = hot16(128, part % 128)
    tval = sum(dot(t, php, 0, 0) for t in split2(temp16[...]))
    tval = jnp.sum(keep(128, part % 128, tval), axis=0, keepdims=True)
    pb = hot16(128, row_of)
    pt[...] = pb
    tri = jnp.where(iota((256, 256), 0) < iota((256, 256), 1), 1.0, 0.0).astype(BF)
    ones = jnp.ones((256, 256), BF)
    run = jnp.zeros((128, 256), F32)
    ranks = []
    for k in range(NE // 256):
        pc = pb[:, k * 256:(k + 1) * 256]
        cum = dot(pc, tri, 1, 0) + run
        run = run + dot(pc, ones, 1, 0)
        ranks.append(jnp.sum(keep(128, row_of[:, k * 256:(k + 1) * 256], cum), axis=0, keepdims=True))
    rank = jnp.concatenate(ranks, 1)
    q = jnp.where(iota((CAP, NE), 0).astype(F32) == rank, 1.0, 0.0)
    qt[...] = q
    c1 = icell[...] + 1
    chi = (c1 // 256 * 256).astype(F32)
    clo = (c1 % 256).astype(F32)
    v0, v1 = split2(tval)
    zero = jnp.zeros((96, NE), BF)

    def rows(a, b):
        return jnp.concatenate([jnp.concatenate([a, b], 0).astype(BF), zero], 0)

    send1[...] = (
        dot(pb, rows(q * chi, q * v0.astype(F32)), 1, 1)
        + dot(pb, rows(q * clo, q * v1.astype(F32)), 1, 1)
    )

    pl.semaphore_wait(barrier, len(partners))

    ph1_i = group()
    for d in range(1, NF):
        f = (F + d) % NF
        remote(send1.at[pl.ds(pl.multiple_of(f * NS, NS), NS)], recv1.at[F], (S, f), ph1_i)
    recv1[pl.ds(F, 1)] = send1[pl.ds(pl.multiple_of(F * NS, NS), NS)].reshape(1, NS, 128)

    nxt = ((S + (F + 1) // NF) % NS, fn)
    prv = ((S + NS - (NF - F) // NF) % NS, fp)
    pcs = [remote(pack, ext.at[1], prv), remote(wsend, wrecv, prv)]
    ext[0] = pack[...]

    for c in lc:
        c.wait()
    U[0, GZ] = jnp.zeros((BX, CY), F32)
    U[1, GZ] = jnp.zeros((BX, CY), F32)
    C[GZ] = jnp.zeros((BX, CY), F32)
    def packed(src, lo, hi):
        n = hi - lo
        l = iota((n, 128), 1)
        halves = []
        for half in range(2):
            acc = jnp.zeros((n, 128), F32)
            for w in range(16):
                z = half * 16 + w
                x = jnp.where(l < 64, src[z, lo:hi, 0:128], src[z, lo:hi, 128:256])
                acc = jnp.where(l // 8 == w, pltpu.roll(x, (8 * w + 4) % 128, 1), acc)
            halves.append(acc)
        return jnp.concatenate(halves, 1)

    for a in range(2):
        pk_s[a] = packed(U.at[0] if a == 0 else C, 0, CX)
    heat_prep(ext, vt, jt, it, aj, hrow, (0,))

    ph1 = [all_of(send1.at[pl.ds(0, 7 * NS)], recv1.at[pl.ds(0, NF - 1)], ph1_i)]
    for c in ph1:
        c.wait_recv()
    send2[...] = jnp.swapaxes(recv1[...], 0, 1)
    ph2_i = group()
    for d in range(1, NS):
        s = (S + d) % NS
        remote(send2.at[s], recv2.at[S], (s, F), ph2_i)
    recv2[pl.ds(S, 1)] = send2[pl.ds(S, 1)]

    halo = []
    for src, dst, lo in ((sub, U.at[0], 1), (cond, C, 0)):
        n = GZ - lo
        halo.append(remote(src.at[pl.ds(lo, n), pl.ds(0, 4)], dst.at[pl.ds(lo, n), pl.ds(32, 4)], (sp, F)))
        halo.append(remote(src.at[pl.ds(lo, n), pl.ds(28, 4)], dst.at[pl.ds(lo, n), pl.ds(36, 4)], (sn, F)))
    for a in range(2):
        halo += faces(remote, pk_s.at[a], pk_s.at[a], pk_r.at[a, 1], pk_r.at[a, 0], S, F, sn, sp, fn, fp)

    for c in pcs:
        c.wait_recv()
    heat_prep(ext, vt, jt, it, aj, hrow, (1,))
    hacc[...] = jnp.zeros((2 * NB, 8, PB), F32)
    sub8 = iota((NB, 16), 0)
    one8 = jnp.ones((NB, 128), BF)
    for t, w in enumerate((wsend[:, NB:NB + 16], wrecv[:, 0:16])):
        for b in range(NB):
            wb[t * NB + b] = dot(jnp.where(sub8 == b, w, 0.0).astype(BF), one8, 0, 0)
    heat_blocks(wb, pair_r, vt, jt, it, aj, hrow, hacc, 0, NB // 2)

    ph2 = [all_of(send2.at[pl.ds(0, NS - 1)], recv2.at[pl.ds(0, NS - 1)], ph2_i)]
    for c in ph2:
        c.wait_recv()
    rt = jnp.transpose(recv2[...].reshape(128, 128))
    cf = jnp.concatenate([rt[s:s + 1, :] for s in range(CAP)], 1)
    tf = jnp.concatenate([rt[CAP + s:CAP + s + 1, :] for s in range(CAP)], 1)
    ci = cf.astype(jnp.int32) - 1
    live = ci >= 0
    hi = jnp.where(live, ci // 256 + (ci % 256) // 128 * CX, -1)
    lo = jnp.where(live, ci % 128, -1)
    sf = surf[...]
    ss = jnp.concatenate(split2(jnp.concatenate([sf[:, 0:128], sf[:, 128:256]], 0)), 0)
    cons = []
    W = 512
    for k in range(2048 // W):
        sl = slice(k * W, (k + 1) * W)
        ob = hot16(64, hi[:, sl])
        g = dot(ss, jnp.concatenate([ob, ob], 0), 0, 0)
        ghost = jnp.sum(keep(128, lo[:, sl], g), axis=0, keepdims=True)
        cons.append(jnp.where(live[:, sl], CONTACT_GAIN * (tf[:, sl] - ghost), 0.0))
    lc_ = lcell[...]
    lx, ly = lc_ // (NF * CY), lc_ % (NF * CY)
    mine = (lx // CX == S) & (ly // CY == F)
    lhi = jnp.where(mine, lx % CX + (ly % CY) // 128 * CX, -1)
    llo = jnp.where(mine, ly % 128, -1)
    fl = jnp.zeros((128, 128), F32)
    parts = [(hi[:, k * W:(k + 1) * W], lo[:, k * W:(k + 1) * W], cons[k]) for k in range(2048 // W)]
    for h, l, value in parts + [(lhi, llo, lpow[...])]:
        ch = jnp.concatenate([keep16(64, h, v) for v in split2(value)], 0)
        fl = fl + dot(ch, hot16(128, l), 1, 1)
    fl = fl[0:64] + fl[64:128]
    top[...] = sf + SURFACE_GAIN * jnp.concatenate([fl[0:32], fl[32:64]], 1)
    con = jnp.concatenate(cons, 1)

    th = [
        remote(top.at[pl.ds(0, 4)], U.at[0, 0, pl.ds(32, 4)], (sp, F)),
        remote(top.at[pl.ds(28, 4)], U.at[0, 0, pl.ds(36, 4)], (sn, F)),
    ]
    th += faces(remote, top.at[:, pl.ds(0, 128)], top.at[:, pl.ds(128, 128)], ty.at[1], ty.at[0], S, F, sn, sp, fn, fp)

    back = jnp.concatenate([con[:, s * 128:(s + 1) * 128] for s in range(CAP)] + [jnp.zeros((112, 128), F32)], 0)
    rsend1[...] = jnp.transpose(back).reshape(NS, NF, 128)
    rh1_i = group()
    for d in range(1, NS):
        s = (S + d) % NS
        remote(rsend1.at[s], rret1.at[S], (s, F), rh1_i)
    rret1[pl.ds(S, 1)] = rsend1[pl.ds(S, 1)]

    heat_blocks(wb, pair_r, vt, jt, it, aj, hrow, hacc, NB // 2, NB)
    hc = remote(hacc.at[pl.ds(NB, NB)], hrecv, nxt)

    for c in halo:
        c.wait_recv()
    row = iota((BX, CY), 0)
    lane = iota((BX, CY), 1)
    up = (S > 0).astype(F32)
    down = (S < NS - 1).astype(F32)
    rmask = jnp.where(row < 32, 1.0, jnp.where(row < 36, down, up))
    smask = [
        rmask * jnp.where(lane % 8 < 4, (F > 0).astype(F32), 1.0),
        rmask * jnp.where(lane % 8 < 4, 1.0, (F < NF - 1).astype(F32)),
    ]
    xmask = rmask[32:40]

    @pl.when(S == 0)
    def _():
        U[0, 1:GZ, 36:40, :] = jnp.zeros((GZ - 1, 4, CY), F32)
        C[0:GZ, 36:40, :] = jnp.zeros((GZ, 4, CY), F32)

    @pl.when(S == NS - 1)
    def _():
        U[0, 1:GZ, 32:36, :] = jnp.zeros((GZ - 1, 4, CY), F32)
        C[0:GZ, 32:36, :] = jnp.zeros((GZ, 4, CY), F32)

    for c in th:
        c.wait_recv()
    U[0, 0, 0:CX] = top[...]
    U[0, 0, 32:40] = U[0, 0, 32:40] * xmask
    zero_z = lane < 8
    l128 = iota((BX, 128), 1)
    for a in range(2):
        src = U.at[0] if a == 0 else C
        mine_ = jnp.concatenate([pk_s[a], packed(src, 32, 40)], 0)
        for side in range(2):
            first = (pk_r[a, side], mine_) if side == 0 else (mine_, pk_r[a, side])
            v = jnp.where(lane % 8 < 4, first[0], first[1])
            if a == 0:
                o = U[0, 0, :, side * 128:(side + 1) * 128]
                near = (o, ty[side]) if side == 0 else (ty[side], o)
                near = pltpu.roll(jnp.where(l128 < 64, near[0], near[1]), 4, 1)
                v = jnp.where(zero_z, jnp.concatenate([near, near], 1), v)
                su[side] = v * smask[side]
            else:
                sc[side] = v * smask[side]

    G = LAMBDA_STEP * 0.5

    def conductivity(u, c):
        return c * (G + (0.5 * G) * jnp.tanh(u))

    def along_x(u, k):
        fx = (k + pltpu.roll(k, BX - 1, 0)) * (pltpu.roll(u, BX - 1, 0) - u)
        return fx - pltpu.roll(fx, 1, 0)

    lane1 = iota((BX, 128), 1)
    first_lane, last_lane = lane1 == 0, lane1 == 127
    for step in range(SUB):
        a, b = step % 2, 1 - step % 2
        last = step == SUB - 1
        for side in range(2):
            u, c = su[side], sc[side]
            k = conductivity(u, c)
            fy = (k + pltpu.roll(k, CY - 1, 1)) * (pltpu.roll(u, CY - 1, 1) - u)
            if side == 0:
                face = pltpu.roll(fy, 1, 1)
            else:
                face = jnp.where(lane % 8 == 4, face, fy)
                fs[0] = face[:, 0:128]
                fs[1] = face[:, 128:256]
            if not last:
                below = lane >= CY - 8
                un = jnp.where(below, 0.0, pltpu.roll(u, CY - 8, 1))
                kn = jnp.where(below, k, pltpu.roll(k, CY - 8, 1))
                fz = (k + kn) * (un - u)
                fup = jnp.where(lane < 8, 0.0, pltpu.roll(fz, 8, 1))
                net = (fy - pltpu.roll(fy, 1, 1)) + (fz - fup) + along_x(u, k)
                su[side] = (u + net) * smask[side]

        kc_ref[...] = conductivity(U[a, 0], C[0])
        fz_ref[...] = jnp.zeros((BX, CY), F32)

        def layers(n, _):
            z0 = n * GROUP
            k, fz0 = kc_ref[...], fz_ref[...]
            u = U[a, z0]
            for m in range(GROUP):
                z = z0 + m
                un = U[a, z + 1]
                kn = conductivity(un, C[z + 1])
                if m == GROUP - 1:
                    kf = jnp.where(z == GZ - 1, k, kn)
                else:
                    kf = kn
                fz = (k + kf) * (un - u)
                net = along_x(u, k) + (fz - fz0)
                w = z % 16
                kl, kr = k[:, 0:128], k[:, 128:256]
                ul, ur = u[:, 0:128], u[:, 128:256]
                skl, skr = pltpu.roll(kl, 127, 1), pltpu.roll(kr, 127, 1)
                sul, sur = pltpu.roll(ul, 127, 1), pltpu.roll(ur, 127, 1)
                fyl = (kl + jnp.where(last_lane, skr, skl)) * (jnp.where(last_lane, sur, sul) - ul)
                fyr = (kr + skr) * (sur - ur)
                edge = pltpu.roll(fs[z // 16], (124 + 128 - 8 * w) % 128, 1)
                fyr = jnp.where(last_lane, edge, fyr)
                bl, br = pltpu.roll(fyl, 1, 1), pltpu.roll(fyr, 1, 1)
                nl = fyl - jnp.where(first_lane, edge, bl)
                nr = fyr - jnp.where(first_lane, bl, br)
                new = u + (net + jnp.concatenate([nl, nr], 1))
                if last:
                    outv[z] = new[0:CX]
                else:
                    U[b, z, 0:CX] = new[0:CX]
                    U[b, z, 32:40] = new[32:40] * xmask
                u, k, fz0 = un, kn, fz
            kc_ref[...] = k
            fz_ref[...] = fz0
            return 0

        lax.fori_loop(0, GZ // GROUP, layers, 0)

        if step == 1:
            rh1 = [all_of(rsend1.at[pl.ds(0, NS - 1)], rret1.at[pl.ds(0, NS - 1)], rh1_i)]
            for c in rh1:
                c.wait_recv()
            rsend2[...] = jnp.swapaxes(rret1[...], 0, 1)
            rh2_i = group()
            for d in range(1, NF):
                f = (F + d) % NF
                remote(rsend2.at[f], rret2.at[F], (S, f), rh2_i)
            rret2[pl.ds(F, 1)] = rsend2[pl.ds(F, 1)]

    rh2 = [all_of(rsend2.at[pl.ds(0, NF - 1)], rret2.at[pl.ds(0, NF - 1)], rh2_i)]
    for c in rh2:
        c.wait_recv()
    rr = rret2[...].reshape(128, 128)[:, 0:CAP]
    x = sum(dot(v, pt[...], 0, 0) for v in split2(rr))
    cval = jnp.sum(x * qt[...], axis=0, keepdims=True)
    ph = ipart[...] // 128
    pf = sum(dot(keep16(16, ph, v), ohp_lo[...], 1, 1) for v in split2(cval))
    pflux = jnp.concatenate([pf[r:r + 1, :] for r in range(16)], 1)
    hc.wait_recv()
    for b in range(NB):
        h8 = hacc[b] + hrecv[b]
        warm, amount = h8[0:1] + h8[1:2] + h8[2:3], h8[3:4] + h8[4:5] + h8[5:6]
        at = slice(b * PB, (b + 1) * PB)
        heat[:, at] = warm - temp1[:, at] * amount
    pout[...] = temp1[...] + SPH_STEP * heat[...] - PARTICLE_SHARE * pflux

    for c in [hc] + ph1 + pcs + halo + ph2 + th + rh1 + rh2:
        c.wait_send()


UNROLL = 8


def groups3(x):
    a = x.astype(BF).astype(F32)
    r = x - a
    b = r.astype(BF).astype(F32)
    return [a, b, r - b]


def heat_prep(ext, vt, jt, it, aj, hrow, which):
    scale = (LOG2E * 2.0 * KERNEL_SCALE) ** 0.5
    r32, c256 = iota((32, 256), 0), iota((32, 256), 1)
    rep = jnp.where((c256 < 72) & (c256 % 24 == r32), 1.0, 0.0)
    tail = jnp.where((c256 >= 128) & (r32 >= 24) & (r32 < 27), 1.0, 0.0)
    spread = (rep + tail).astype(BF)
    row = iota((8, PB), 0)

    def place(*rows):
        out = jnp.zeros((8, PB), F32)
        for n, r in enumerate(rows):
            out = jnp.where(row == n, r, out)
        return out

    for t in which:
        def prep(n, _):
            for m in range(UNROLL):
                b = n * UNROLL + m
                at = pl.ds(pl.multiple_of(b * PB, PB), PB)
                blk = ext[t, :, at]
                p = jnp.where(row < 3, blk * scale, 0.0)
                norm = -0.5 * jnp.sum(p * p, axis=0, keepdims=True)
                temp = blk[3:4]
                volume = blk[4:5] * (2.0 * KERNEL_SCALE)
                half = 0.5 / (1.0 + 0.5 * jnp.tanh(temp))
                packed = groups3(place(half, volume * temp, volume))
                vt[t * NB + b] = place(
                    packed[0][1:2], packed[1][1:2], packed[2][1:2], packed[0][2:3], packed[1][2:3], packed[2][2:3])
                ah = place(packed[0][0:1], packed[1][0:1], packed[2][0:1])
                sj = groups3(jnp.where(row == 3, norm, jnp.where(row == 4, 1.0, p)))
                both = dot(jnp.concatenate(sj + [ah], 0).astype(BF), spread, 0, 0)
                jt[t * NB + b] = both[:, 0:128].astype(BF)
                aj[t * NB + b] = both[:, 128:256]
                if t == 0:
                    hrow[b] = jnp.broadcast_to(half, (8, PB))
                    i0, i1, i2 = groups3(jnp.where(row == 3, 1.0, jnp.where(row == 4, norm, p)))
                    z = jnp.zeros((128 - 72, PB), F32)
                    it[b] = jnp.concatenate([i0, i0, i0, i1, i1, i1, i2, i2, i2, z], 0).astype(BF)
            return 0

        lax.fori_loop(0, NB // UNROLL, prep, 0)


def live_weights(nbr, cnt, device):
    local = nbr[...] - (device - 1) * NB
    eq = iota((NB, NB), 0) == iota((NB, NB), 1)
    count = jnp.sum(jnp.where(eq, jnp.broadcast_to(cnt[...], (NB, NB)).astype(F32), 0.0), axis=1, keepdims=True)
    w = jnp.zeros((NB, 128), F32)
    at = iota((NB, 128), 1)
    for s in range(KN):
        live = jnp.where(count > s, 1.0, 0.0)
        w = w + jnp.where(at == local[:, s:s + 1], live, 0.0)
    return w


def heat_blocks(wb, pair_r, vt, jt, it, aj, hrow, acc, start, stop):
    def block(b, _):
        half = hrow[b, 0:1, :]
        itb = it[b]
        left = []
        for n in range(NB + 1):
            o = b + n
            e = dot(jt[o], itb, 1, 0)
            a = aj[o]
            for h in range(2):
                sl = slice(h * 128, (h + 1) * 128)
                q = (a + half[:, sl]).reshape(PB // 16, 2, 8, 128)
                q0, q1 = q[:, 0], q[:, 1]
                inv = 1.0 / (q0 * q1)
                f = jnp.stack([q1 * inv, q0 * inv], 1).reshape(PB, 128)
                pair_r[n * PB:(n + 1) * PB, sl] = (jnp.exp2(e[:, sl]) * f).astype(BF)
            w = wb[b, pl.ds(o, 1), :]
            left.append(vt[o] * jnp.concatenate([w, w], 1))
        acc[b] += dot(jnp.concatenate(left, 1).astype(BF), pair_r[...], 1, 0)
        for n in range(1, NB + 1):
            w = wb[b + n, pl.ds(b, 1), :]
            back = (vt[b] * jnp.concatenate([w, w], 1)).astype(BF)
            acc[b + n] += dot(back, pair_r[n * PB:(n + 1) * PB], 1, 1)
        return 0

    lax.fori_loop(start, stop, block, 0)


COPIES = 4 + 3 + 4 + 12 + 8


def main_call(nbr, cnt, *args):
    vm = pl.BlockSpec(memory_space=pltpu.VMEM)
    hbm = pl.BlockSpec(memory_space=pltpu.HBM)
    s = lambda *shape: pltpu.VMEM(shape, F32)
    i = lambda *shape: pltpu.VMEM(shape, jnp.int32)
    return pl.pallas_call(
        main_kernel,
        out_shape=[
            jax.ShapeDtypeStruct((GZ, CX, CY), F32),
            jax.ShapeDtypeStruct((1, PD), F32),
        ],
        in_specs=[hbm] * 13,
        out_specs=[vm, vm],
        scratch_shapes=[
            i(NB, KN), i(1, NB), s(3, PD), s(1, PD), s(16, 128), s(1, PD), i(1, NE), i(1, NE), i(1, NE),
            i(1, 256), s(1, 256),
            s(2, GZ + 1, BX, CY), s(GZ + 1, BX, CY), s(2, BX, CY), s(2, BX, CY),
            s(2, BX, 128), s(CX, CY), s(CX, CY), s(2, BX, 128),
            s(2, CX, CY), s(2, 2, BX, CY),
            s(128, 128), s(NF, NS, 128), s(NS, NF, 128), s(NS, NF, 128),
            s(NS, NF, 128), s(NS, NF, 128), s(NF, NS, 128), s(NF, NS, 128),
            pltpu.VMEM((128, NE), BF), s(CAP, NE), pltpu.VMEM((128, NE), BF),
            s(BX, CY), s(BX, CY), s(8, PD), s(2, 8, PD), s(2 * NB, 8, PB), s(NB, 128), s(NB, 128), s(2 * NB, 16, 128),
            pltpu.VMEM(((NB + 1) * PB, PB), BF),
            pltpu.VMEM((2 * NB, PB, 128), BF), pltpu.VMEM((NB, 128, PB), BF),
            s(2 * NB, PB, 128), s(NB, 8, PB), s(2 * NB, 8, PB), s(NB, 8, PB), s(1, PD),
            pltpu.SemaphoreType.DMA((14,)),
            pltpu.SemaphoreType.DMA((COPIES,)),
            pltpu.SemaphoreType.DMA((COPIES,)),
        ],
        compiler_params=pltpu.CompilerParams(
            collective_id=0, has_side_effects=True, vmem_limit_bytes=32 * 2**20),
        name="step",
    )(*(pltpu.with_memory_space_constraint(x, pltpu.HBM) for x in (nbr, cnt) + args))


def body(positions, particle_temp, volume, nbr_blocks, nbr_count, iface_part, iface_owner,
         iface_cell, substrate_temp, conduct, laser_cells, laser_power):
    field, particle_out = main_call(
        nbr_blocks, nbr_count.reshape(1, NB), positions, particle_temp.reshape(1, PD), particle_temp.reshape(16, 128), volume.reshape(1, PD),
        iface_part.reshape(1, NE), iface_owner.reshape(1, NE), iface_cell.reshape(1, NE),
        laser_cells.reshape(1, -1), laser_power.reshape(1, -1), substrate_temp, conduct)
    return particle_out.reshape(PD), field


def solution(mesh):
    in_specs = (
        P(None, ("sph", "fv")),
        P(("sph", "fv")),
        P(("sph", "fv")),
        P(("sph", "fv"), None),
        P(("sph", "fv")),
        P(("sph", "fv")),
        P(("sph", "fv"), None),
        P(("sph", "fv")),
        P(None, "sph", "fv"),
        P(None, "sph", "fv"),
        P(),
        P(),
    )
    out_specs = (P(("sph", "fv")), P(None, "sph", "fv"))
    return jax.shard_map(body, mesh=mesh, in_specs=in_specs, out_specs=out_specs, check_vma=False)
```

```python
import functools

import jax
import jax.numpy as jnp
from jax import lax
from jax.experimental import pallas as pl
from jax.experimental.pallas import tpu as pltpu
from jax.sharding import PartitionSpec as P

SUB = 4
KERNEL_SCALE = 0.5
SPH_STEP = 0.05
CONTACT_GAIN = 1.0
PARTICLE_SHARE = 0.5
SURFACE_GAIN = 0.5
LAMBDA_STEP = 0.1
NS, NF = 16, 8
CX, CY, GZ = 32, 256, 32
BX, RX = 40, 48
PB, NB, KN, CAP = 256, 8, 16, 16
PD, NE = 2048, 1024
MESH = pl.DeviceIdType.MESH
F32, BF = jnp.float32, jnp.bfloat16
LOG2E = 1.4426950408889634


def split2(x):
    a = x.astype(BF)
    return a, (x - a.astype(F32)).astype(BF)


def dot(a, b, ca, cb):
    return lax.dot_general(a, b, (((ca,), (cb,)), ((), ())), preferred_element_type=F32)


def iota(shape, dim):
    return lax.broadcasted_iota(jnp.int32, shape, dim)


def hot(rows, row_index):
    return jnp.where(iota((rows, row_index.shape[1]), 0) == row_index, 1.0, 0.0)


def hot16(rows, row_index):
    return keep16(rows, row_index, jnp.ones((), BF))


def keep16(rows, row_index, value):
    at = iota((rows, row_index.shape[1]), 0).astype(BF)
    return jnp.where(at == row_index.astype(F32).astype(BF), value, jnp.zeros((), BF))


def keep(rows, row_index, value):
    return jnp.where(iota((rows, row_index.shape[1]), 0) == row_index, value, 0.0)


def faces(remote, left, right, into_right, into_left, S, F, sn, sp, fn, fp):
    return [
        remote(left, into_right.at[pl.ds(0, CX)], (S, fp)),
        remote(right, into_left.at[pl.ds(0, CX)], (S, fn)),
        remote(left.at[pl.ds(0, 4)], into_right.at[pl.ds(32, 4)], (sp, fp)),
        remote(left.at[pl.ds(28, 4)], into_right.at[pl.ds(36, 4)], (sn, fp)),
        remote(right.at[pl.ds(0, 4)], into_left.at[pl.ds(32, 4)], (sp, fn)),
        remote(right.at[pl.ds(28, 4)], into_left.at[pl.ds(36, 4)], (sn, fn)),
    ]


GROUP = 16


def main_kernel(
    h_nbr, h_cnt, h_pos, h_temp1, h_temp16, h_vol, h_ipart, h_iown, h_icell, h_lcell, h_lpow, sub, cond,
    outv, pout,
    nbr, cnt, pos, temp1, temp16, vol, ipart, iown, icell, lcell, lpow,
    U0, U1, C, su, sc, fs, surf, top, ty, pk_s, pk_r,
    send1, recv1, send2, recv2, rsend1, rret1, rsend2, rret2,
    pt, qt, ohp_lo, fz_ref, ks, fxs, mmat, pack, ext, vt, wsend, wrecv, wb, pair_r, jt, it, aj, hrow, hacc, hrecv, heat, lsem, ssem, rsem,
):
    S = lax.axis_index("sph")
    F = lax.axis_index("fv")
    sn, sp = (S + 1) % NS, (S + NS - 1) % NS
    fn, fp = (F + 1) % NF, (F + NF - 1) % NF

    barrier = pltpu.get_barrier_semaphore()
    partners = [(S, (F + d) % NF) for d in range(1, NF)]
    partners += [((S + d) % NS, F) for d in range(1, NS)]
    partners += [(sn, fn), (sn, fp), (sp, fn), (sp, fp)]
    for who in partners:
        pl.semaphore_signal(barrier, inc=1, device_id=who, device_id_type=MESH)

    small = [
        pltpu.make_async_copy(a, b, lsem.at[3 + n]) for n, (a, b) in enumerate((
            (h_ipart, ipart), (h_temp16, temp16), (h_iown, iown), (h_icell, icell), (h_pos, pos), (h_temp1, temp1),
            (h_vol, vol), (h_nbr, nbr), (h_cnt, cnt), (h_lcell, lcell), (h_lpow, lpow)))
    ]
    for c in small:
        c.start()

    lc = [
        pltpu.make_async_copy(sub.at[0], surf, lsem.at[0]),
    ]
    for t in range(2):
        at = pl.ds(t * 128, 128)
        lc += [
            pltpu.make_async_copy(
                sub.at[pl.ds(1, GZ - 1), :, at], U0.at[pl.ds(1, GZ - 1), t, pl.ds(0, CX)], lsem.at[1 + t]),
            pltpu.make_async_copy(cond.at[:, :, at], C.at[pl.ds(0, GZ), t, pl.ds(0, CX)], lsem.at[14 + t]),
        ]
    for c in lc:
        c.start()

    count = [0]

    def remote(src, dst, who, i=None):
        if i is None:
            i = count[0]
            count[0] += 1
        c = pltpu.make_async_remote_copy(
            src_ref=src, dst_ref=dst, send_sem=ssem.at[i], recv_sem=rsem.at[i],
            device_id=who, device_id_type=MESH)
        c.start()
        return c

    for c in small:
        c.wait()

    def group():
        count[0] += 1
        return count[0] - 1

    def all_of(src, dst, i):
        return pltpu.make_async_remote_copy(
            src_ref=src, dst_ref=dst, send_sem=ssem.at[i], recv_sem=rsem.at[i],
            device_id=(sn, F), device_id_type=MESH)

    pack[...] = jnp.concatenate([pos[...], temp1[...], vol[...], jnp.zeros((3, PD), F32)], 0)

    wsend[...] = live_weights(nbr, cnt, S * NF + F)

    own = iown[...]
    row_of = (own % NF) * NS + own // NF
    part = ipart[...]
    php = hot16(16, part // 128)
    ohp_lo[...] = hot16(128, part % 128)
    tval = sum(dot(t, php, 0, 0) for t in split2(temp16[...]))
    tval = jnp.sum(keep(128, part % 128, tval), axis=0, keepdims=True)
    pb = hot16(128, row_of)
    pt[...] = pb
    tri = jnp.where(iota((256, 256), 0) < iota((256, 256), 1), 1.0, 0.0).astype(BF)
    ones = jnp.ones((256, 256), BF)
    run = jnp.zeros((128, 256), F32)
    ranks = []
    for k in range(NE // 256):
        pc = pb[:, k * 256:(k + 1) * 256]
        cum = dot(pc, tri, 1, 0) + run
        run = run + dot(pc, ones, 1, 0)
        ranks.append(jnp.sum(keep(128, row_of[:, k * 256:(k + 1) * 256], cum), axis=0, keepdims=True))
    rank = jnp.concatenate(ranks, 1)
    q = jnp.where(iota((CAP, NE), 0).astype(F32) == rank, 1.0, 0.0)
    qt[...] = q
    c1 = icell[...] + 1
    chi = (c1 // 256 * 256).astype(F32)
    clo = (c1 % 256).astype(F32)
    v0, v1 = split2(tval)
    zero = jnp.zeros((96, NE), BF)

    def rows(a, b):
        return jnp.concatenate([jnp.concatenate([a, b], 0).astype(BF), zero], 0)

    send1[...] = (
        dot(pb, rows(q * chi, q * v0.astype(F32)), 1, 1)
        + dot(pb, rows(q * clo, q * v1.astype(F32)), 1, 1)
    )

    pl.semaphore_wait(barrier, len(partners))

    ph1_i = group()
    for d in range(1, NF):
        f = (F + d) % NF
        remote(send1.at[pl.ds(pl.multiple_of(f * NS, NS), NS)], recv1.at[F], (S, f), ph1_i)
    recv1[pl.ds(F, 1)] = send1[pl.ds(pl.multiple_of(F * NS, NS), NS)].reshape(1, NS, 128)

    nxt = ((S + (F + 1) // NF) % NS, fn)
    prv = ((S + NS - (NF - F) // NF) % NS, fp)
    pcs = [remote(pack, ext.at[1], prv), remote(wsend, wrecv, prv)]
    ext[0] = pack[...]

    for c in lc:
        c.wait()
    U0[GZ] = jnp.zeros((2, RX, 128), F32)
    U1[GZ] = jnp.zeros((2, RX, 128), F32)
    C[GZ] = jnp.zeros((2, BX, 128), F32)
    def packed(src, lo, hi):
        n = hi - lo
        l = iota((n, 128), 1)
        halves = []
        for half in range(2):
            acc = jnp.zeros((n, 128), F32)
            for w in range(16):
                z = half * 16 + w
                x = jnp.where(l < 64, src[z, 0, lo:hi], src[z, 1, lo:hi])
                acc = jnp.where(l // 8 == w, pltpu.roll(x, (8 * w + 4) % 128, 1), acc)
            halves.append(acc)
        return jnp.concatenate(halves, 1)

    for a in range(2):
        pk_s[a] = packed(U0 if a == 0 else C, 0, CX)
    heat_prep(ext, vt, jt, it, aj, hrow, (0,))

    ph1 = [all_of(send1.at[pl.ds(0, 7 * NS)], recv1.at[pl.ds(0, NF - 1)], ph1_i)]
    for c in ph1:
        c.wait_recv()
    send2[...] = jnp.swapaxes(recv1[...], 0, 1)
    ph2_i = group()
    for d in range(1, NS):
        s = (S + d) % NS
        remote(send2.at[s], recv2.at[S], (s, F), ph2_i)
    recv2[pl.ds(S, 1)] = send2[pl.ds(S, 1)]

    halo = []
    for src, dst, lo in ((sub, U0, 1), (cond, C, 0)):
        layers_ = pl.ds(lo, GZ - lo)
        for t in range(2):
            at = pl.ds(t * 128, 128)
            halo.append(remote(src.at[layers_, pl.ds(0, 4), at], dst.at[layers_, t, pl.ds(32, 4)], (sp, F)))
            halo.append(remote(src.at[layers_, pl.ds(28, 4), at], dst.at[layers_, t, pl.ds(36, 4)], (sn, F)))
    for a in range(2):
        halo += faces(remote, pk_s.at[a], pk_s.at[a], pk_r.at[a, 1], pk_r.at[a, 0], S, F, sn, sp, fn, fp)

    for c in pcs:
        c.wait_recv()
    heat_prep(ext, vt, jt, it, aj, hrow, (1,))
    hacc[...] = jnp.zeros((2 * NB, 8, PB), F32)
    sub8 = iota((NB, 16), 0)
    one8 = jnp.ones((NB, 128), BF)
    for t, w in enumerate((wsend[:, NB:NB + 16], wrecv[:, 0:16])):
        for b in range(NB):
            wb[t * NB + b] = dot(jnp.where(sub8 == b, w, 0.0).astype(BF), one8, 0, 0)
    heat_blocks(wb, pair_r, vt, jt, it, aj, hrow, hacc, 0, NB // 2)

    ph2 = [all_of(send2.at[pl.ds(0, NS - 1)], recv2.at[pl.ds(0, NS - 1)], ph2_i)]
    for c in ph2:
        c.wait_recv()
    rt = jnp.transpose(recv2[...].reshape(128, 128))
    cf = jnp.concatenate([rt[s:s + 1, :] for s in range(CAP)], 1)
    tf = jnp.concatenate([rt[CAP + s:CAP + s + 1, :] for s in range(CAP)], 1)
    ci = cf.astype(jnp.int32) - 1
    live = ci >= 0
    hi = jnp.where(live, ci // 256 + (ci % 256) // 128 * CX, -1)
    lo = jnp.where(live, ci % 128, -1)
    sf = surf[...]
    ss = jnp.concatenate(split2(jnp.concatenate([sf[:, 0:128], sf[:, 128:256]], 0)), 0)
    cons = []
    W = 512
    for k in range(2048 // W):
        sl = slice(k * W, (k + 1) * W)
        ob = hot16(64, hi[:, sl])
        g = dot(ss, jnp.concatenate([ob, ob], 0), 0, 0)
        ghost = jnp.sum(keep(128, lo[:, sl], g), axis=0, keepdims=True)
        cons.append(jnp.where(live[:, sl], CONTACT_GAIN * (tf[:, sl] - ghost), 0.0))
    lc_ = lcell[...]
    lx, ly = lc_ // (NF * CY), lc_ % (NF * CY)
    mine = (lx // CX == S) & (ly // CY == F)
    lhi = jnp.where(mine, lx % CX + (ly % CY) // 128 * CX, -1)
    llo = jnp.where(mine, ly % 128, -1)
    fl = jnp.zeros((128, 128), F32)
    parts = [(hi[:, k * W:(k + 1) * W], lo[:, k * W:(k + 1) * W], cons[k]) for k in range(2048 // W)]
    for h, l, value in parts + [(lhi, llo, lpow[...])]:
        ch = jnp.concatenate([keep16(64, h, v) for v in split2(value)], 0)
        fl = fl + dot(ch, hot16(128, l), 1, 1)
    fl = fl[0:64] + fl[64:128]
    top[0] = sf[:, 0:128] + SURFACE_GAIN * fl[0:32]
    top[1] = sf[:, 128:256] + SURFACE_GAIN * fl[32:64]
    con = jnp.concatenate(cons, 1)

    th = [
        remote(top.at[:, pl.ds(0, 4)], U0.at[0, :, pl.ds(32, 4)], (sp, F)),
        remote(top.at[:, pl.ds(28, 4)], U0.at[0, :, pl.ds(36, 4)], (sn, F)),
    ]
    th += faces(remote, top.at[0], top.at[1], ty.at[1], ty.at[0], S, F, sn, sp, fn, fp)

    back = jnp.concatenate([con[:, s * 128:(s + 1) * 128] for s in range(CAP)] + [jnp.zeros((112, 128), F32)], 0)
    rsend1[...] = jnp.transpose(back).reshape(NS, NF, 128)
    rh1_i = group()
    for d in range(1, NS):
        s = (S + d) % NS
        remote(rsend1.at[s], rret1.at[S], (s, F), rh1_i)
    rret1[pl.ds(S, 1)] = rsend1[pl.ds(S, 1)]

    heat_blocks(wb, pair_r, vt, jt, it, aj, hrow, hacc, NB // 2, NB)
    hc = remote(hacc.at[pl.ds(NB, NB)], hrecv, nxt)

    for c in halo:
        c.wait_recv()
    row = iota((BX, CY), 0)
    lane = iota((BX, CY), 1)
    up = (S > 0).astype(F32)
    down = (S < NS - 1).astype(F32)
    rmask = jnp.where(row < 32, 1.0, jnp.where(row < 36, down, up))
    smask = [
        rmask * jnp.where(lane % 8 < 4, (F > 0).astype(F32), 1.0),
        rmask * jnp.where(lane % 8 < 4, 1.0, (F < NF - 1).astype(F32)),
    ]
    xmask = rmask[32:40, 0:128]

    @pl.when(S == 0)
    def _():
        U0[1:GZ, :, 36:40, :] = jnp.zeros((GZ - 1, 2, 4, 128), F32)
        C[0:GZ, :, 36:40, :] = jnp.zeros((GZ, 2, 4, 128), F32)

    @pl.when(S == NS - 1)
    def _():
        U0[1:GZ, :, 32:36, :] = jnp.zeros((GZ - 1, 2, 4, 128), F32)
        C[0:GZ, :, 32:36, :] = jnp.zeros((GZ, 2, 4, 128), F32)

    for c in th:
        c.wait_recv()
    U0[0, :, 0:CX] = top[...]
    U0[0, :, 32:40] = U0[0, :, 32:40] * xmask
    U0[0:GZ, :, 40:41] = U0[0:GZ, :, 0:1]
    zero_z = lane < 8
    l128 = iota((BX, 128), 1)
    for a in range(2):
        src = U0 if a == 0 else C
        mine_ = jnp.concatenate([pk_s[a], packed(src, 32, 40)], 0)
        for side in range(2):
            first = (pk_r[a, side], mine_) if side == 0 else (mine_, pk_r[a, side])
            v = jnp.where(lane % 8 < 4, first[0], first[1])
            if a == 0:
                o = U0[0, side, 0:BX]
                near = (o, ty[side]) if side == 0 else (ty[side], o)
                near = pltpu.roll(jnp.where(l128 < 64, near[0], near[1]), 4, 1)
                v = jnp.where(zero_z, jnp.concatenate([near, near], 1), v)
                su[side] = v * smask[side]
            else:
                sc[side] = v * smask[side]

    G = LAMBDA_STEP * 0.5
    Us = (U0, U1)

    def conductivity(u, c):
        return c * (G + (0.5 * G) * jnp.tanh(u))

    def along_x(u, k):
        fx = (k + pltpu.roll(k, BX - 1, 0)) * (pltpu.roll(u, BX - 1, 0) - u)
        return fx - pltpu.roll(fx, 1, 0)

    lane1 = iota((BX, 128), 1)
    first_lane, last_lane = lane1 == 0, lane1 == 127
    r256, c256 = iota((CY, CY), 0), iota((CY, CY), 1)
    mmat[...] = (jnp.where(r256 == c256, 1.0, 0.0) - jnp.where(r256 + 1 == c256, 1.0, 0.0)).astype(BF)
    for step in range(SUB):
        a, b = step % 2, 1 - step % 2
        last = step == SUB - 1
        for side in range(2):
            u, c = su[side], sc[side]
            k = conductivity(u, c)
            fy = (k + pltpu.roll(k, CY - 1, 1)) * (pltpu.roll(u, CY - 1, 1) - u)
            if side == 0:
                face = pltpu.roll(fy, 1, 1)
            else:
                face = jnp.where(lane % 8 == 4, face, fy)
                fs[0] = face[:, 0:128]
                fs[1] = face[:, 128:256]
            if not last:
                below = lane >= CY - 8
                un = jnp.where(below, 0.0, pltpu.roll(u, CY - 8, 1))
                kn = jnp.where(below, k, pltpu.roll(k, CY - 8, 1))
                fz = (k + kn) * (un - u)
                fup = jnp.where(lane < 8, 0.0, pltpu.roll(fz, 8, 1))
                net = (fy - pltpu.roll(fy, 1, 1)) + (fz - fup) + along_x(u, k)
                su[side] = (u + net) * smask[side]

        for t in range(2):
            k0 = conductivity(Us[a][0, t, 0:BX], C[0, t])
            ks[0, t, 0:BX] = k0
            ks[0, t, 40:41] = k0[0:1]
        fz_ref[...] = jnp.zeros((2, BX, 128), F32)

        def layers(n, _):
            minus_left = mmat[...]
            z0 = n * GROUP
            both = range(2)
            k = [ks[0, t, 0:BX] for t in both]
            fz0 = [fz_ref[t] for t in both]
            u = [Us[a][z0, t, 0:BX] for t in both]
            for m in range(GROUP):
                z = z0 + m
                un = [Us[a][z + 1, t, 0:BX] for t in both]
                kn = [conductivity(un[t], C[z + 1, t]) for t in both]
                w = z % 16
                edge = pltpu.roll(fs[z // 16], (124 + 128 - 8 * w) % 128, 1)
                sk = [pltpu.roll(v, 127, 1) for v in k]
                su_ = [pltpu.roll(v, 127, 1) for v in u]
                fyl = (k[0] + jnp.where(last_lane, sk[1], sk[0])) * (jnp.where(last_lane, su_[1], su_[0]) - u[0])
                fyr = jnp.where(last_lane, edge, (k[1] + sk[1]) * (su_[1] - u[1]))
                hi = [v.astype(BF) for v in (fyl, fyr)]
                low = [(v - h.astype(F32)).astype(BF) for v, h in zip((fyl, fyr), hi)]
                twice = dot(jnp.concatenate([jnp.concatenate(hi, 1), jnp.concatenate(low, 1)], 0), minus_left, 1, 0)
                ny = twice[0:BX] + twice[BX:2 * BX]
                ny = [ny[:, 0:128] - jnp.where(first_lane, edge, 0.0), ny[:, 128:256]]
                fzs = []
                for t in both:
                    fx = (k[t] + ks[m, t, 1:41]) * (Us[a][z, t, 1:41] - u[t])
                    fxs[m, t, 8:48] = fx
                    fxs[m, t, 7:8] = fx[39:40]
                    kf = jnp.where(z == GZ - 1, k[t], kn[t]) if m == GROUP - 1 else kn[t]
                    fz = (k[t] + kf) * (un[t] - u[t])
                    new = u[t] + ((fx - fxs[m, t, 7:47]) + (fz - fz0[t]) + ny[t])
                    if last:
                        outv[z, :, t * 128:(t + 1) * 128] = new[0:CX]
                    else:
                        Us[b][z, t, 0:CX] = new[0:CX]
                        Us[b][z, t, 32:40] = new[32:40] * xmask
                        Us[b][z, t, 40:41] = new[0:1]
                    fzs.append(fz)
                    slot = (m + 1) % GROUP
                    ks[slot, t, 0:BX] = kn[t]
                    ks[slot, t, 40:41] = kn[t][0:1]
                u, k, fz0 = un, kn, fzs
            for t in both:
                fz_ref[t] = fz0[t]
            return 0

        lax.fori_loop(0, GZ // GROUP, layers, 0)

        if step == 1:
            rh1 = [all_of(rsend1.at[pl.ds(0, NS - 1)], rret1.at[pl.ds(0, NS - 1)], rh1_i)]
            for c in rh1:
                c.wait_recv()
            rsend2[...] = jnp.swapaxes(rret1[...], 0, 1)
            rh2_i = group()
            for d in range(1, NF):
                f = (F + d) % NF
                remote(rsend2.at[f], rret2.at[F], (S, f), rh2_i)
            rret2[pl.ds(F, 1)] = rsend2[pl.ds(F, 1)]

    rh2 = [all_of(rsend2.at[pl.ds(0, NF - 1)], rret2.at[pl.ds(0, NF - 1)], rh2_i)]
    for c in rh2:
        c.wait_recv()
    rr = rret2[...].reshape(128, 128)[:, 0:CAP]
    x = sum(dot(v, pt[...], 0, 0) for v in split2(rr))
    cval = jnp.sum(x * qt[...], axis=0, keepdims=True)
    ph = ipart[...] // 128
    pf = sum(dot(keep16(16, ph, v), ohp_lo[...], 1, 1) for v in split2(cval))
    pflux = jnp.concatenate([pf[r:r + 1, :] for r in range(16)], 1)
    hc.wait_recv()
    for b in range(NB):
        h8 = hacc[b] + hrecv[b]
        warm, amount = h8[0:1] + h8[1:2] + h8[2:3], h8[3:4] + h8[4:5] + h8[5:6]
        at = slice(b * PB, (b + 1) * PB)
        heat[:, at] = warm - temp1[:, at] * amount
    pout[...] = temp1[...] + SPH_STEP * heat[...] - PARTICLE_SHARE * pflux

    for c in [hc] + ph1 + pcs + halo + ph2 + th + rh1 + rh2:
        c.wait_send()


UNROLL = 8


def groups3(x):
    a = x.astype(BF).astype(F32)
    r = x - a
    b = r.astype(BF).astype(F32)
    return [a, b, r - b]


def heat_prep(ext, vt, jt, it, aj, hrow, which):
    scale = (LOG2E * 2.0 * KERNEL_SCALE) ** 0.5
    r32, c256 = iota((32, 256), 0), iota((32, 256), 1)
    rep = jnp.where((c256 < 72) & (c256 % 24 == r32), 1.0, 0.0)
    tail = jnp.where((c256 >= 128) & (r32 >= 24) & (r32 < 27), 1.0, 0.0)
    spread = (rep + tail).astype(BF)
    row = iota((8, PB), 0)

    def place(*rows):
        out = jnp.zeros((8, PB), F32)
        for n, r in enumerate(rows):
            out = jnp.where(row == n, r, out)
        return out

    for t in which:
        def prep(n, _):
            for m in range(UNROLL):
                b = n * UNROLL + m
                at = pl.ds(pl.multiple_of(b * PB, PB), PB)
                blk = ext[t, :, at]
                p = jnp.where(row < 3, blk * scale, 0.0)
                norm = -0.5 * jnp.sum(p * p, axis=0, keepdims=True)
                temp = blk[3:4]
                volume = blk[4:5] * (2.0 * KERNEL_SCALE)
                half = 0.5 / (1.0 + 0.5 * jnp.tanh(temp))
                packed = groups3(place(half, volume * temp, volume))
                vt[t * NB + b] = place(
                    packed[0][1:2], packed[1][1:2], packed[2][1:2], packed[0][2:3], packed[1][2:3], packed[2][2:3])
                ah = place(packed[0][0:1], packed[1][0:1], packed[2][0:1])
                sj = groups3(jnp.where(row == 3, norm, jnp.where(row == 4, 1.0, p)))
                both = dot(jnp.concatenate(sj + [ah], 0).astype(BF), spread, 0, 0)
                jt[t * NB + b] = both[:, 0:128].astype(BF)
                aj[t * NB + b] = both[:, 128:256]
                if t == 0:
                    hrow[b] = jnp.broadcast_to(half, (8, PB))
                    i0, i1, i2 = groups3(jnp.where(row == 3, 1.0, jnp.where(row == 4, norm, p)))
                    z = jnp.zeros((128 - 72, PB), F32)
                    it[b] = jnp.concatenate([i0, i0, i0, i1, i1, i1, i2, i2, i2, z], 0).astype(BF)
            return 0

        lax.fori_loop(0, NB // UNROLL, prep, 0)


def live_weights(nbr, cnt, device):
    local = nbr[...] - (device - 1) * NB
    eq = iota((NB, NB), 0) == iota((NB, NB), 1)
    count = jnp.sum(jnp.where(eq, jnp.broadcast_to(cnt[...], (NB, NB)).astype(F32), 0.0), axis=1, keepdims=True)
    w = jnp.zeros((NB, 128), F32)
    at = iota((NB, 128), 1)
    for s in range(KN):
        live = jnp.where(count > s, 1.0, 0.0)
        w = w + jnp.where(at == local[:, s:s + 1], live, 0.0)
    return w


def heat_blocks(wb, pair_r, vt, jt, it, aj, hrow, acc, start, stop):
    def block(b, _):
        half = hrow[b, 0:1, :]
        itb = it[b]
        left = []
        for n in range(NB + 1):
            o = b + n
            e = dot(jt[o], itb, 1, 0)
            a = aj[o]
            for h in range(2):
                sl = slice(h * 128, (h + 1) * 128)
                q = (a + half[:, sl]).reshape(PB // 16, 2, 8, 128)
                q0, q1 = q[:, 0], q[:, 1]
                inv = 1.0 / (q0 * q1)
                f = jnp.stack([q1 * inv, q0 * inv], 1).reshape(PB, 128)
                pair_r[n * PB:(n + 1) * PB, sl] = (jnp.exp2(e[:, sl]) * f).astype(BF)
            w = wb[b, pl.ds(o, 1), :]
            left.append(vt[o] * jnp.concatenate([w, w], 1))
        acc[b] += dot(jnp.concatenate(left, 1).astype(BF), pair_r[...], 1, 0)
        for n in range(1, NB + 1):
            w = wb[b + n, pl.ds(b, 1), :]
            back = (vt[b] * jnp.concatenate([w, w], 1)).astype(BF)
            acc[b + n] += dot(back, pair_r[n * PB:(n + 1) * PB], 1, 1)
        return 0

    lax.fori_loop(start, stop, block, 0)


COPIES = 4 + 3 + 8 + 12 + 8


def main_call(nbr, cnt, *args):
    vm = pl.BlockSpec(memory_space=pltpu.VMEM)
    hbm = pl.BlockSpec(memory_space=pltpu.HBM)
    s = lambda *shape: pltpu.VMEM(shape, F32)
    i = lambda *shape: pltpu.VMEM(shape, jnp.int32)
    return pl.pallas_call(
        main_kernel,
        out_shape=[
            jax.ShapeDtypeStruct((GZ, CX, CY), F32),
            jax.ShapeDtypeStruct((1, PD), F32),
        ],
        in_specs=[hbm] * 13,
        out_specs=[vm, vm],
        scratch_shapes=[
            i(NB, KN), i(1, NB), s(3, PD), s(1, PD), s(16, 128), s(1, PD), i(1, NE), i(1, NE), i(1, NE),
            i(1, 256), s(1, 256),
            s(GZ + 1, 2, RX, 128), s(GZ + 1, 2, RX, 128), s(GZ + 1, 2, BX, 128), s(2, BX, CY), s(2, BX, CY),
            s(2, BX, 128), s(CX, CY), s(2, CX, 128), s(2, BX, 128),
            s(2, CX, CY), s(2, 2, BX, CY),
            s(128, 128), s(NF, NS, 128), s(NS, NF, 128), s(NS, NF, 128),
            s(NS, NF, 128), s(NS, NF, 128), s(NF, NS, 128), s(NF, NS, 128),
            pltpu.VMEM((128, NE), BF), s(CAP, NE), pltpu.VMEM((128, NE), BF),
            s(2, BX, 128), s(GROUP, 2, RX, 128), s(GROUP, 2, RX, 128), pltpu.VMEM((CY, CY), BF), s(8, PD), s(2, 8, PD), s(2 * NB, 8, PB), s(NB, 128), s(NB, 128), s(2 * NB, 16, 128),
            pltpu.VMEM(((NB + 1) * PB, PB), BF),
            pltpu.VMEM((2 * NB, PB, 128), BF), pltpu.VMEM((NB, 128, PB), BF),
            s(2 * NB, PB, 128), s(NB, 8, PB), s(2 * NB, 8, PB), s(NB, 8, PB), s(1, PD),
            pltpu.SemaphoreType.DMA((16,)),
            pltpu.SemaphoreType.DMA((COPIES,)),
            pltpu.SemaphoreType.DMA((COPIES,)),
        ],
        compiler_params=pltpu.CompilerParams(
            collective_id=0, has_side_effects=True, vmem_limit_bytes=32 * 2**20),
        name="step",
    )(*(pltpu.with_memory_space_constraint(x, pltpu.HBM) for x in (nbr, cnt) + args))


def body(positions, particle_temp, volume, nbr_blocks, nbr_count, iface_part, iface_owner,
         iface_cell, substrate_temp, conduct, laser_cells, laser_power):
    field, particle_out = main_call(
        nbr_blocks, nbr_count.reshape(1, NB), positions, particle_temp.reshape(1, PD), particle_temp.reshape(16, 128), volume.reshape(1, PD),
        iface_part.reshape(1, NE), iface_owner.reshape(1, NE), iface_cell.reshape(1, NE),
        laser_cells.reshape(1, -1), laser_power.reshape(1, -1), substrate_temp, conduct)
    return particle_out.reshape(PD), field


def solution(mesh):
    in_specs = (
        P(None, ("sph", "fv")),
        P(("sph", "fv")),
        P(("sph", "fv")),
        P(("sph", "fv"), None),
        P(("sph", "fv")),
        P(("sph", "fv")),
        P(("sph", "fv"), None),
        P(("sph", "fv")),
        P(None, "sph", "fv"),
        P(None, "sph", "fv"),
        P(),
        P(),
    )
    out_specs = (P(("sph", "fv")), P(None, "sph", "fv"))
    return jax.shard_map(body, mesh=mesh, in_specs=in_specs, out_specs=out_specs, check_vma=False)
```

```python
import functools

import jax
import jax.numpy as jnp
from jax import lax
from jax.experimental import pallas as pl
from jax.experimental.pallas import tpu as pltpu
from jax.sharding import PartitionSpec as P

SUB = 4
KERNEL_SCALE = 0.5
SPH_STEP = 0.05
CONTACT_GAIN = 1.0
PARTICLE_SHARE = 0.5
SURFACE_GAIN = 0.5
LAMBDA_STEP = 0.1
NS, NF = 16, 8
CX, CY, GZ = 32, 256, 32
BX, RX = 40, 48
PB, NB, KN, CAP = 256, 8, 16, 16
PD, NE = 2048, 1024
MESH = pl.DeviceIdType.MESH
F32, BF = jnp.float32, jnp.bfloat16
LOG2E = 1.4426950408889634


def split2(x):
    a = x.astype(BF)
    return a, (x - a.astype(F32)).astype(BF)


def dot(a, b, ca, cb):
    return lax.dot_general(a, b, (((ca,), (cb,)), ((), ())), preferred_element_type=F32)


def iota(shape, dim):
    return lax.broadcasted_iota(jnp.int32, shape, dim)


def hot(rows, row_index):
    return jnp.where(iota((rows, row_index.shape[1]), 0) == row_index, 1.0, 0.0)


def hot16(rows, row_index):
    return keep16(rows, row_index, jnp.ones((), BF))


def keep16(rows, row_index, value):
    at = iota((rows, row_index.shape[1]), 0).astype(BF)
    return jnp.where(at == row_index.astype(F32).astype(BF), value, jnp.zeros((), BF))


def keep(rows, row_index, value):
    return jnp.where(iota((rows, row_index.shape[1]), 0) == row_index, value, 0.0)


def faces(remote, left, right, into_right, into_left, S, F, sn, sp, fn, fp):
    return [
        remote(left, into_right.at[pl.ds(0, CX)], (S, fp)),
        remote(right, into_left.at[pl.ds(0, CX)], (S, fn)),
        remote(left.at[pl.ds(0, 4)], into_right.at[pl.ds(32, 4)], (sp, fp)),
        remote(left.at[pl.ds(28, 4)], into_right.at[pl.ds(36, 4)], (sn, fp)),
        remote(right.at[pl.ds(0, 4)], into_left.at[pl.ds(32, 4)], (sp, fn)),
        remote(right.at[pl.ds(28, 4)], into_left.at[pl.ds(36, 4)], (sn, fn)),
    ]


GROUP = 16


def main_kernel(
    h_nbr, h_cnt, h_pos, h_temp1, h_temp16, h_vol, h_ipart, h_iown, h_icell, h_lcell, h_lpow, sub, cond,
    outv, pout,
    nbr, cnt, pos, temp1, temp16, vol, ipart, iown, icell, lcell, lpow,
    U0, U1, C, su, sc, fs, surf, top, ty, pk_s, pk_r,
    send1, recv1, send2, recv2, rsend1, rret1, rsend2, rret2,
    pt, qt, ohp_lo, fz_ref, ks, fxs, mmat, pack, ext, vt, wsend, wrecv, wb, pair_r, jt, it, aj, hrow, hacc, hrecv, heat, lsem, ssem, rsem,
):
    S = lax.axis_index("sph")
    F = lax.axis_index("fv")
    sn, sp = (S + 1) % NS, (S + NS - 1) % NS
    fn, fp = (F + 1) % NF, (F + NF - 1) % NF

    small = [
        pltpu.make_async_copy(a, b, lsem.at[3 + n]) for n, (a, b) in enumerate((
            (h_ipart, ipart), (h_temp16, temp16), (h_iown, iown), (h_icell, icell), (h_pos, pos), (h_temp1, temp1),
            (h_vol, vol), (h_nbr, nbr), (h_cnt, cnt), (h_lcell, lcell), (h_lpow, lpow)))
    ]
    for c in small:
        c.start()

    lc = [
        pltpu.make_async_copy(sub.at[0], surf, lsem.at[0]),
    ]
    for t in range(2):
        at = pl.ds(t * 128, 128)
        lc += [
            pltpu.make_async_copy(
                sub.at[pl.ds(1, GZ - 1), :, at], U0.at[pl.ds(1, GZ - 1), t, pl.ds(0, CX)], lsem.at[1 + t]),
            pltpu.make_async_copy(cond.at[:, :, at], C.at[pl.ds(0, GZ), t, pl.ds(0, CX)], lsem.at[14 + t]),
        ]
    for c in lc:
        c.start()

    barrier = pltpu.get_barrier_semaphore()
    partners = [(S, (F + d) % NF) for d in range(1, NF)]
    partners += [((S + d) % NS, F) for d in range(1, NS)]
    partners += [(sn, fn), (sn, fp), (sp, fn), (sp, fp)]
    for who in partners:
        pl.semaphore_signal(barrier, inc=1, device_id=who, device_id_type=MESH)

    count = [0]

    def remote(src, dst, who, i=None):
        if i is None:
            i = count[0]
            count[0] += 1
        c = pltpu.make_async_remote_copy(
            src_ref=src, dst_ref=dst, send_sem=ssem.at[i], recv_sem=rsem.at[i],
            device_id=who, device_id_type=MESH)
        c.start()
        return c

    for c in small:
        c.wait()

    def group():
        count[0] += 1
        return count[0] - 1

    def all_of(src, dst, i):
        return pltpu.make_async_remote_copy(
            src_ref=src, dst_ref=dst, send_sem=ssem.at[i], recv_sem=rsem.at[i],
            device_id=(sn, F), device_id_type=MESH)

    pack[...] = jnp.concatenate([pos[...], temp1[...], vol[...], jnp.zeros((3, PD), F32)], 0)

    wsend[...] = live_weights(nbr, cnt, S * NF + F)

    own = iown[...]
    row_of = (own % NF) * NS + own // NF
    part = ipart[...]
    php = hot16(16, part // 128)
    ohp_lo[...] = hot16(128, part % 128)
    tval = sum(dot(t, php, 0, 0) for t in split2(temp16[...]))
    tval = jnp.sum(keep(128, part % 128, tval), axis=0, keepdims=True)
    pb = hot16(128, row_of)
    pt[...] = pb
    tri = jnp.where(iota((256, 256), 0) < iota((256, 256), 1), 1.0, 0.0).astype(BF)
    ones = jnp.ones((256, 256), BF)
    run = jnp.zeros((128, 256), F32)
    ranks = []
    for k in range(NE // 256):
        pc = pb[:, k * 256:(k + 1) * 256]
        cum = dot(pc, tri, 1, 0) + run
        run = run + dot(pc, ones, 1, 0)
        ranks.append(jnp.sum(keep(128, row_of[:, k * 256:(k + 1) * 256], cum), axis=0, keepdims=True))
    rank = jnp.concatenate(ranks, 1)
    q = jnp.where(iota((CAP, NE), 0).astype(F32) == rank, 1.0, 0.0)
    qt[...] = q
    c1 = icell[...] + 1
    chi = (c1 // 256 * 256).astype(F32)
    clo = (c1 % 256).astype(F32)
    v0, v1 = split2(tval)
    zero = jnp.zeros((96, NE), BF)

    def rows(a, b):
        return jnp.concatenate([jnp.concatenate([a, b], 0).astype(BF), zero], 0)

    send1[...] = (
        dot(pb, rows(q * chi, q * v0.astype(F32)), 1, 1)
        + dot(pb, rows(q * clo, q * v1.astype(F32)), 1, 1)
    )

    pl.semaphore_wait(barrier, len(partners))

    ph1_i = group()
    for d in range(1, NF):
        f = (F + d) % NF
        remote(send1.at[pl.ds(pl.multiple_of(f * NS, NS), NS)], recv1.at[F], (S, f), ph1_i)
    recv1[pl.ds(F, 1)] = send1[pl.ds(pl.multiple_of(F * NS, NS), NS)].reshape(1, NS, 128)

    nxt = ((S + (F + 1) // NF) % NS, fn)
    prv = ((S + NS - (NF - F) // NF) % NS, fp)
    pcs = [remote(pack, ext.at[1], prv), remote(wsend, wrecv, prv)]
    ext[0] = pack[...]

    for c in lc:
        c.wait()
    U0[GZ] = jnp.zeros((2, RX, 128), F32)
    U1[GZ] = jnp.zeros((2, RX, 128), F32)
    C[GZ] = jnp.zeros((2, BX, 128), F32)
    def packed(src, lo, hi):
        n = hi - lo
        l = iota((n, 128), 1)
        halves = []
        for half in range(2):
            acc = jnp.zeros((n, 128), F32)
            for w in range(16):
                z = half * 16 + w
                x = jnp.where(l < 64, src[z, 0, lo:hi], src[z, 1, lo:hi])
                acc = jnp.where(l // 8 == w, pltpu.roll(x, (8 * w + 4) % 128, 1), acc)
            halves.append(acc)
        return jnp.concatenate(halves, 1)

    for a in range(2):
        pk_s[a] = packed(U0 if a == 0 else C, 0, CX)
    heat_prep(ext, vt, jt, it, aj, hrow, (0,))
    hacc[...] = jnp.zeros((2 * NB, 8, PB), F32)
    sub8 = iota((NB, 16), 0)
    one8 = jnp.ones((NB, 128), BF)

    def spread_weights(w, base):
        for b in range(NB):
            wb[base + b] = dot(jnp.where(sub8 == b, w, 0.0).astype(BF), one8, 0, 0)

    spread_weights(wsend[:, NB:NB + 16], 0)
    heat_own(wb, pair_r, vt, jt, it, aj, hrow, hacc, 0, NB // 2, 5)

    ph1 = [all_of(send1.at[pl.ds(0, 7 * NS)], recv1.at[pl.ds(0, NF - 1)], ph1_i)]
    for c in ph1:
        c.wait_recv()
    send2[...] = jnp.swapaxes(recv1[...], 0, 1)
    ph2_i = group()
    for d in range(1, NS):
        s = (S + d) % NS
        remote(send2.at[s], recv2.at[S], (s, F), ph2_i)
    recv2[pl.ds(S, 1)] = send2[pl.ds(S, 1)]

    halo = []
    for src, dst, lo in ((sub, U0, 1), (cond, C, 0)):
        layers_ = pl.ds(lo, GZ - lo)
        for t in range(2):
            at = pl.ds(t * 128, 128)
            halo.append(remote(src.at[layers_, pl.ds(0, 4), at], dst.at[layers_, t, pl.ds(32, 4)], (sp, F)))
            halo.append(remote(src.at[layers_, pl.ds(28, 4), at], dst.at[layers_, t, pl.ds(36, 4)], (sn, F)))
    for a in range(2):
        halo += faces(remote, pk_s.at[a], pk_s.at[a], pk_r.at[a, 1], pk_r.at[a, 0], S, F, sn, sp, fn, fp)

    heat_own(wb, pair_r, vt, jt, it, aj, hrow, hacc, NB // 2, NB, 4)
    for c in pcs:
        c.wait_recv()
    heat_prep(ext, vt, jt, it, aj, hrow, (1,))
    spread_weights(wrecv[:, 0:16], NB)
    heat_next(wb, pair_r, vt, jt, it, aj, hrow, hacc, 0, 2)

    ph2 = [all_of(send2.at[pl.ds(0, NS - 1)], recv2.at[pl.ds(0, NS - 1)], ph2_i)]
    for c in ph2:
        c.wait_recv()
    rt = jnp.transpose(recv2[...].reshape(128, 128))
    cf = jnp.concatenate([rt[s:s + 1, :] for s in range(CAP)], 1)
    tf = jnp.concatenate([rt[CAP + s:CAP + s + 1, :] for s in range(CAP)], 1)
    ci = cf.astype(jnp.int32) - 1
    live = ci >= 0
    hi = jnp.where(live, ci // 256 + (ci % 256) // 128 * CX, -1)
    lo = jnp.where(live, ci % 128, -1)
    sf = surf[...]
    ss = jnp.concatenate(split2(jnp.concatenate([sf[:, 0:128], sf[:, 128:256]], 0)), 0)
    cons = []
    W = 512
    for k in range(2048 // W):
        sl = slice(k * W, (k + 1) * W)
        ob = hot16(64, hi[:, sl])
        g = dot(ss, jnp.concatenate([ob, ob], 0), 0, 0)
        ghost = jnp.sum(keep(128, lo[:, sl], g), axis=0, keepdims=True)
        cons.append(jnp.where(live[:, sl], CONTACT_GAIN * (tf[:, sl] - ghost), 0.0))
    lc_ = lcell[...]
    lx, ly = lc_ // (NF * CY), lc_ % (NF * CY)
    mine = (lx // CX == S) & (ly // CY == F)
    lhi = jnp.where(mine, lx % CX + (ly % CY) // 128 * CX, -1)
    llo = jnp.where(mine, ly % 128, -1)
    fl = jnp.zeros((128, 128), F32)
    parts = [(hi[:, k * W:(k + 1) * W], lo[:, k * W:(k + 1) * W], cons[k]) for k in range(2048 // W)]
    for h, l, value in parts + [(lhi, llo, lpow[...])]:
        ch = jnp.concatenate([keep16(64, h, v) for v in split2(value)], 0)
        fl = fl + dot(ch, hot16(128, l), 1, 1)
    fl = fl[0:64] + fl[64:128]
    top[0] = sf[:, 0:128] + SURFACE_GAIN * fl[0:32]
    top[1] = sf[:, 128:256] + SURFACE_GAIN * fl[32:64]
    con = jnp.concatenate(cons, 1)

    th = [
        remote(top.at[:, pl.ds(0, 4)], U0.at[0, :, pl.ds(32, 4)], (sp, F)),
        remote(top.at[:, pl.ds(28, 4)], U0.at[0, :, pl.ds(36, 4)], (sn, F)),
    ]
    th += faces(remote, top.at[0], top.at[1], ty.at[1], ty.at[0], S, F, sn, sp, fn, fp)

    back = jnp.concatenate([con[:, s * 128:(s + 1) * 128] for s in range(CAP)] + [jnp.zeros((112, 128), F32)], 0)
    rsend1[...] = jnp.transpose(back).reshape(NS, NF, 128)
    rh1_i = group()
    for d in range(1, NS):
        s = (S + d) % NS
        remote(rsend1.at[s], rret1.at[S], (s, F), rh1_i)
    rret1[pl.ds(S, 1)] = rsend1[pl.ds(S, 1)]

    heat_next(wb, pair_r, vt, jt, it, aj, hrow, hacc, 2, NB // 2)
    hc = remote(hacc.at[pl.ds(NB, NB)], hrecv, nxt)

    for c in halo:
        c.wait_recv()
    row = iota((BX, CY), 0)
    lane = iota((BX, CY), 1)
    up = (S > 0).astype(F32)
    down = (S < NS - 1).astype(F32)
    rmask = jnp.where(row < 32, 1.0, jnp.where(row < 36, down, up))
    smask = [
        rmask * jnp.where(lane % 8 < 4, (F > 0).astype(F32), 1.0),
        rmask * jnp.where(lane % 8 < 4, 1.0, (F < NF - 1).astype(F32)),
    ]
    xmask = rmask[32:40, 0:128]

    @pl.when(S == 0)
    def _():
        U0[1:GZ, :, 36:40, :] = jnp.zeros((GZ - 1, 2, 4, 128), F32)
        C[0:GZ, :, 36:40, :] = jnp.zeros((GZ, 2, 4, 128), F32)

    @pl.when(S == NS - 1)
    def _():
        U0[1:GZ, :, 32:36, :] = jnp.zeros((GZ - 1, 2, 4, 128), F32)
        C[0:GZ, :, 32:36, :] = jnp.zeros((GZ, 2, 4, 128), F32)

    for c in th:
        c.wait_recv()
    U0[0, :, 0:CX] = top[...]
    U0[0, :, 32:40] = U0[0, :, 32:40] * xmask
    U0[0:GZ, :, 40:41] = U0[0:GZ, :, 0:1]
    zero_z = lane < 8
    l128 = iota((BX, 128), 1)
    for a in range(2):
        src = U0 if a == 0 else C
        mine_ = jnp.concatenate([pk_s[a], packed(src, 32, 40)], 0)
        for side in range(2):
            first = (pk_r[a, side], mine_) if side == 0 else (mine_, pk_r[a, side])
            v = jnp.where(lane % 8 < 4, first[0], first[1])
            if a == 0:
                o = U0[0, side, 0:BX]
                near = (o, ty[side]) if side == 0 else (ty[side], o)
                near = pltpu.roll(jnp.where(l128 < 64, near[0], near[1]), 4, 1)
                v = jnp.where(zero_z, jnp.concatenate([near, near], 1), v)
                su[side] = v * smask[side]
            else:
                sc[side] = v * smask[side]

    G = LAMBDA_STEP * 0.5
    Us = (U0, U1)

    def conductivity(u, c):
        return c * (G + (0.5 * G) * jnp.tanh(u))

    def along_x(u, k):
        fx = (k + pltpu.roll(k, BX - 1, 0)) * (pltpu.roll(u, BX - 1, 0) - u)
        return fx - pltpu.roll(fx, 1, 0)

    lane1 = iota((BX, 128), 1)
    first_lane, last_lane = lane1 == 0, lane1 == 127
    r256, c256 = iota((CY, CY), 0), iota((CY, CY), 1)
    mmat[...] = (jnp.where(r256 == c256, 1.0, 0.0) - jnp.where(r256 + 1 == c256, 1.0, 0.0)).astype(BF)
    for step in range(SUB):
        a, b = step % 2, 1 - step % 2
        last = step == SUB - 1
        for side in range(2):
            u, c = su[side], sc[side]
            k = conductivity(u, c)
            fy = (k + pltpu.roll(k, CY - 1, 1)) * (pltpu.roll(u, CY - 1, 1) - u)
            if side == 0:
                face = pltpu.roll(fy, 1, 1)
            else:
                face = jnp.where(lane % 8 == 4, face, fy)
                fs[0] = face[:, 0:128]
                fs[1] = face[:, 128:256]
            if not last:
                below = lane >= CY - 8
                un = jnp.where(below, 0.0, pltpu.roll(u, CY - 8, 1))
                kn = jnp.where(below, k, pltpu.roll(k, CY - 8, 1))
                fz = (k + kn) * (un - u)
                fup = jnp.where(lane < 8, 0.0, pltpu.roll(fz, 8, 1))
                net = (fy - pltpu.roll(fy, 1, 1)) + (fz - fup) + along_x(u, k)
                su[side] = (u + net) * smask[side]

        for t in range(2):
            k0 = conductivity(Us[a][0, t, 0:BX], C[0, t])
            ks[0, t, 0:BX] = k0
            ks[0, t, 40:41] = k0[0:1]
        fz_ref[...] = jnp.zeros((2, BX, 128), F32)

        def layers(n, _):
            minus_left = mmat[...]
            z0 = n * GROUP
            both = range(2)
            k = [ks[0, t, 0:BX] for t in both]
            fz0 = [fz_ref[t] for t in both]
            u = [Us[a][z0, t, 0:BX] for t in both]
            for m in range(GROUP):
                z = z0 + m
                un = [Us[a][z + 1, t, 0:BX] for t in both]
                kn = [conductivity(un[t], C[z + 1, t]) for t in both]
                w = z % 16
                edge = pltpu.roll(fs[z // 16], (124 + 128 - 8 * w) % 128, 1)
                sk = [pltpu.roll(v, 127, 1) for v in k]
                su_ = [pltpu.roll(v, 127, 1) for v in u]
                fyl = (k[0] + jnp.where(last_lane, sk[1], sk[0])) * (jnp.where(last_lane, su_[1], su_[0]) - u[0])
                fyr = jnp.where(last_lane, edge, (k[1] + sk[1]) * (su_[1] - u[1]))
                hi = [v.astype(BF) for v in (fyl, fyr)]
                low = [(v - h.astype(F32)).astype(BF) for v, h in zip((fyl, fyr), hi)]
                twice = dot(jnp.concatenate([jnp.concatenate(hi, 1), jnp.concatenate(low, 1)], 0), minus_left, 1, 0)
                ny = twice[0:BX] + twice[BX:2 * BX]
                ny = [ny[:, 0:128] - jnp.where(first_lane, edge, 0.0), ny[:, 128:256]]
                fzs = []
                for t in both:
                    fx = (k[t] + ks[m, t, 1:41]) * (Us[a][z, t, 1:41] - u[t])
                    fxs[m, t, 8:48] = fx
                    fxs[m, t, 7:8] = fx[39:40]
                    kf = jnp.where(z == GZ - 1, k[t], kn[t]) if m == GROUP - 1 else kn[t]
                    fz = (k[t] + kf) * (un[t] - u[t])
                    new = u[t] + ((fx - fxs[m, t, 7:47]) + (fz - fz0[t]) + ny[t])
                    if last:
                        outv[z, :, t * 128:(t + 1) * 128] = new[0:CX]
                    else:
                        Us[b][z, t, 0:CX] = new[0:CX]
                        Us[b][z, t, 32:40] = new[32:40] * xmask
                        Us[b][z, t, 40:41] = new[0:1]
                    fzs.append(fz)
                    slot = (m + 1) % GROUP
                    ks[slot, t, 0:BX] = kn[t]
                    ks[slot, t, 40:41] = kn[t][0:1]
                u, k, fz0 = un, kn, fzs
            for t in both:
                fz_ref[t] = fz0[t]
            return 0

        lax.fori_loop(0, GZ // GROUP, layers, 0)

        if step == 1:
            rh1 = [all_of(rsend1.at[pl.ds(0, NS - 1)], rret1.at[pl.ds(0, NS - 1)], rh1_i)]
            for c in rh1:
                c.wait_recv()
            rsend2[...] = jnp.swapaxes(rret1[...], 0, 1)
            rh2_i = group()
            for d in range(1, NF):
                f = (F + d) % NF
                remote(rsend2.at[f], rret2.at[F], (S, f), rh2_i)
            rret2[pl.ds(F, 1)] = rsend2[pl.ds(F, 1)]

    rh2 = [all_of(rsend2.at[pl.ds(0, NF - 1)], rret2.at[pl.ds(0, NF - 1)], rh2_i)]
    for c in rh2:
        c.wait_recv()
    rr = rret2[...].reshape(128, 128)[:, 0:CAP]
    x = sum(dot(v, pt[...], 0, 0) for v in split2(rr))
    cval = jnp.sum(x * qt[...], axis=0, keepdims=True)
    ph = ipart[...] // 128
    pf = sum(dot(keep16(16, ph, v), ohp_lo[...], 1, 1) for v in split2(cval))
    pflux = jnp.concatenate([pf[r:r + 1, :] for r in range(16)], 1)
    hc.wait_recv()
    for b in range(NB):
        h8 = hacc[b] + hrecv[b]
        warm, amount = h8[0:1] + h8[1:2] + h8[2:3], h8[3:4] + h8[4:5] + h8[5:6]
        at = slice(b * PB, (b + 1) * PB)
        heat[:, at] = warm - temp1[:, at] * amount
    pout[...] = temp1[...] + SPH_STEP * heat[...] - PARTICLE_SHARE * pflux

    for c in [hc] + ph1 + pcs + halo + ph2 + th + rh1 + rh2:
        c.wait_send()


UNROLL = 8


def groups3(x):
    a = x.astype(BF).astype(F32)
    r = x - a
    b = r.astype(BF).astype(F32)
    return [a, b, r - b]


def heat_prep(ext, vt, jt, it, aj, hrow, which):
    scale = (LOG2E * 2.0 * KERNEL_SCALE) ** 0.5
    r32, c256 = iota((32, 256), 0), iota((32, 256), 1)
    rep = jnp.where((c256 < 72) & (c256 % 24 == r32), 1.0, 0.0)
    tail = jnp.where((c256 >= 128) & (r32 >= 24) & (r32 < 27), 1.0, 0.0)
    spread = (rep + tail).astype(BF)
    row = iota((8, PB), 0)

    def place(*rows):
        out = jnp.zeros((8, PB), F32)
        for n, r in enumerate(rows):
            out = jnp.where(row == n, r, out)
        return out

    for t in which:
        def prep(n, _):
            for m in range(UNROLL):
                b = n * UNROLL + m
                at = pl.ds(pl.multiple_of(b * PB, PB), PB)
                blk = ext[t, :, at]
                p = jnp.where(row < 3, blk * scale, 0.0)
                norm = -0.5 * jnp.sum(p * p, axis=0, keepdims=True)
                temp = blk[3:4]
                volume = blk[4:5] * (2.0 * KERNEL_SCALE)
                half = 0.5 / (1.0 + 0.5 * jnp.tanh(temp))
                packed = groups3(place(half, volume * temp, volume))
                vt[t * NB + b] = place(
                    packed[0][1:2], packed[1][1:2], packed[2][1:2], packed[0][2:3], packed[1][2:3], packed[2][2:3])
                ah = place(packed[0][0:1], packed[1][0:1], packed[2][0:1])
                sj = groups3(jnp.where(row == 3, norm, jnp.where(row == 4, 1.0, p)))
                both = dot(jnp.concatenate(sj + [ah], 0).astype(BF), spread, 0, 0)
                jt[t * NB + b] = both[:, 0:128].astype(BF)
                aj[t * NB + b] = both[:, 128:256]
                if t == 0:
                    hrow[b] = jnp.broadcast_to(half, (8, PB))
                    i0, i1, i2 = groups3(jnp.where(row == 3, 1.0, jnp.where(row == 4, norm, p)))
                    z = jnp.zeros((128 - 72, PB), F32)
                    it[b] = jnp.concatenate([i0, i0, i0, i1, i1, i1, i2, i2, i2, z], 0).astype(BF)
            return 0

        lax.fori_loop(0, NB // UNROLL, prep, 0)


def live_weights(nbr, cnt, device):
    local = nbr[...] - (device - 1) * NB
    eq = iota((NB, NB), 0) == iota((NB, NB), 1)
    count = jnp.sum(jnp.where(eq, jnp.broadcast_to(cnt[...], (NB, NB)).astype(F32), 0.0), axis=1, keepdims=True)
    w = jnp.zeros((NB, 128), F32)
    at = iota((NB, 128), 1)
    for s in range(KN):
        live = jnp.where(count > s, 1.0, 0.0)
        w = w + jnp.where(at == local[:, s:s + 1], live, 0.0)
    return w


def pair_block(pair_r, n, jt, it, aj, hrow, o, b):
    e = dot(jt[o], it[b], 1, 0)
    a = aj[o]
    half = hrow[b, 0:1, :]
    for h in range(2):
        sl = slice(h * 128, (h + 1) * 128)
        q = (a + half[:, sl]).reshape(PB // 16, 2, 8, 128)
        q0, q1 = q[:, 0], q[:, 1]
        inv = 1.0 / (q0 * q1)
        f = jnp.stack([q1 * inv, q0 * inv], 1).reshape(PB, 128)
        pair_r[n * PB:(n + 1) * PB, sl] = (jnp.exp2(e[:, sl]) * f).astype(BF)


def weighted(wb, vt, to, of):
    w = wb[to, pl.ds(of, 1), :]
    return vt[of] * jnp.concatenate([w, w], 1)


def heat_own(wb, pair_r, vt, jt, it, aj, hrow, acc, start, stop, turns):
    def block(b, _):
        others = [(b + d) % NB for d in range(turns)]
        for n, o in enumerate(others):
            pair_block(pair_r, n, jt, it, aj, hrow, o, b)
        left = jnp.concatenate([weighted(wb, vt, b, o) for o in others], 1).astype(BF)
        acc[b] += dot(left, pair_r[0:turns * PB], 1, 0)
        for n in range(1, turns):
            o = others[n]
            acc[o] += dot(weighted(wb, vt, o, b).astype(BF), pair_r[n * PB:(n + 1) * PB], 1, 1)
        return 0

    lax.fori_loop(start, stop, block, 0)


def heat_next(wb, pair_r, vt, jt, it, aj, hrow, acc, start, stop):
    def block(i, _):
        pairs = []
        for n in range(NB + 1):
            low = (NB + i - n) // NB
            b = low * i + (1 - low) * (NB - 1 - i)
            pairs.append((b, NB + n - (1 - low) * (i + 1)))
        for n, (b, o) in enumerate(pairs):
            pair_block(pair_r, n, jt, it, aj, hrow, o, b)
        for n, (b, o) in enumerate(pairs):
            r = pair_r[n * PB:(n + 1) * PB]
            acc[b] += dot(weighted(wb, vt, b, o).astype(BF), r, 1, 0)
            acc[o] += dot(weighted(wb, vt, o, b).astype(BF), r, 1, 1)
        return 0

    lax.fori_loop(start, stop, block, 0)


COPIES = 4 + 3 + 8 + 12 + 8


def main_call(nbr, cnt, *args):
    vm = pl.BlockSpec(memory_space=pltpu.VMEM)
    hbm = pl.BlockSpec(memory_space=pltpu.HBM)
    s = lambda *shape: pltpu.VMEM(shape, F32)
    i = lambda *shape: pltpu.VMEM(shape, jnp.int32)
    return pl.pallas_call(
        main_kernel,
        out_shape=[
            jax.ShapeDtypeStruct((GZ, CX, CY), F32),
            jax.ShapeDtypeStruct((1, PD), F32),
        ],
        in_specs=[hbm] * 13,
        out_specs=[vm, vm],
        scratch_shapes=[
            i(NB, KN), i(1, NB), s(3, PD), s(1, PD), s(16, 128), s(1, PD), i(1, NE), i(1, NE), i(1, NE),
            i(1, 256), s(1, 256),
            s(GZ + 1, 2, RX, 128), s(GZ + 1, 2, RX, 128), s(GZ + 1, 2, BX, 128), s(2, BX, CY), s(2, BX, CY),
            s(2, BX, 128), s(CX, CY), s(2, CX, 128), s(2, BX, 128),
            s(2, CX, CY), s(2, 2, BX, CY),
            s(128, 128), s(NF, NS, 128), s(NS, NF, 128), s(NS, NF, 128),
            s(NS, NF, 128), s(NS, NF, 128), s(NF, NS, 128), s(NF, NS, 128),
            pltpu.VMEM((128, NE), BF), s(CAP, NE), pltpu.VMEM((128, NE), BF),
            s(2, BX, 128), s(GROUP, 2, RX, 128), s(GROUP, 2, RX, 128), pltpu.VMEM((CY, CY), BF), s(8, PD), s(2, 8, PD), s(2 * NB, 8, PB), s(NB, 128), s(NB, 128), s(2 * NB, 16, 128),
            pltpu.VMEM(((NB + 1) * PB, PB), BF),
            pltpu.VMEM((2 * NB, PB, 128), BF), pltpu.VMEM((NB, 128, PB), BF),
            s(2 * NB, PB, 128), s(NB, 8, PB), s(2 * NB, 8, PB), s(NB, 8, PB), s(1, PD),
            pltpu.SemaphoreType.DMA((16,)),
            pltpu.SemaphoreType.DMA((COPIES,)),
            pltpu.SemaphoreType.DMA((COPIES,)),
        ],
        compiler_params=pltpu.CompilerParams(
            collective_id=0, has_side_effects=True, vmem_limit_bytes=32 * 2**20),
        name="step",
    )(*(pltpu.with_memory_space_constraint(x, pltpu.HBM) for x in (nbr, cnt) + args))


def body(positions, particle_temp, volume, nbr_blocks, nbr_count, iface_part, iface_owner,
         iface_cell, substrate_temp, conduct, laser_cells, laser_power):
    field, particle_out = main_call(
        nbr_blocks, nbr_count.reshape(1, NB), positions, particle_temp.reshape(1, PD), particle_temp.reshape(16, 128), volume.reshape(1, PD),
        iface_part.reshape(1, NE), iface_owner.reshape(1, NE), iface_cell.reshape(1, NE),
        laser_cells.reshape(1, -1), laser_power.reshape(1, -1), substrate_temp, conduct)
    return particle_out.reshape(PD), field


def solution(mesh):
    in_specs = (
        P(None, ("sph", "fv")),
        P(("sph", "fv")),
        P(("sph", "fv")),
        P(("sph", "fv"), None),
        P(("sph", "fv")),
        P(("sph", "fv")),
        P(("sph", "fv"), None),
        P(("sph", "fv")),
        P(None, "sph", "fv"),
        P(None, "sph", "fv"),
        P(),
        P(),
    )
    out_specs = (P(("sph", "fv")), P(None, "sph", "fv"))
    return jax.shard_map(body, mesh=mesh, in_specs=in_specs, out_specs=out_specs, check_vma=False)
```

```python
import functools

import jax
import jax.numpy as jnp
from jax import lax
from jax.experimental import pallas as pl
from jax.experimental.pallas import tpu as pltpu
from jax.sharding import PartitionSpec as P

SUB = 4
KERNEL_SCALE = 0.5
SPH_STEP = 0.05
CONTACT_GAIN = 1.0
PARTICLE_SHARE = 0.5
SURFACE_GAIN = 0.5
LAMBDA_STEP = 0.1
NS, NF = 16, 8
CX, CY, GZ = 32, 256, 32
BX, RX = 40, 48
PB, NB, KN, CAP = 256, 8, 16, 16
PD, NE = 2048, 1024
MESH = pl.DeviceIdType.MESH
F32, BF = jnp.float32, jnp.bfloat16
LOG2E = 1.4426950408889634


def split2(x):
    a = x.astype(BF)
    return a, (x - a.astype(F32)).astype(BF)


def dot(a, b, ca, cb):
    return lax.dot_general(a, b, (((ca,), (cb,)), ((), ())), preferred_element_type=F32)


def iota(shape, dim):
    return lax.broadcasted_iota(jnp.int32, shape, dim)


def hot(rows, row_index):
    return jnp.where(iota((rows, row_index.shape[1]), 0) == row_index, 1.0, 0.0)


def hot16(rows, row_index):
    return keep16(rows, row_index, jnp.ones((), BF))


def keep16(rows, row_index, value):
    at = iota((rows, row_index.shape[1]), 0).astype(BF)
    return jnp.where(at == row_index.astype(F32).astype(BF), value, jnp.zeros((), BF))


def keep(rows, row_index, value):
    return jnp.where(iota((rows, row_index.shape[1]), 0) == row_index, value, 0.0)


def faces(remote, left, right, into_right, into_left, S, F, sn, sp, fn, fp):
    return [
        remote(left, into_right.at[pl.ds(0, CX)], (S, fp)),
        remote(right, into_left.at[pl.ds(0, CX)], (S, fn)),
        remote(left.at[pl.ds(0, 4)], into_right.at[pl.ds(32, 4)], (sp, fp)),
        remote(left.at[pl.ds(28, 4)], into_right.at[pl.ds(36, 4)], (sn, fp)),
        remote(right.at[pl.ds(0, 4)], into_left.at[pl.ds(32, 4)], (sp, fn)),
        remote(right.at[pl.ds(28, 4)], into_left.at[pl.ds(36, 4)], (sn, fn)),
    ]


GROUP = 16


def main_kernel(
    h_nbr, h_cnt, h_pos, h_temp1, h_temp16, h_vol, h_ipart, h_iown, h_icell, h_lcell, h_lpow, sub, cond,
    outv, pout,
    nbr, cnt, pos, temp1, temp16, vol, ipart, iown, icell, lcell, lpow,
    U0, U1, C, su, sc, fs, surf, top, ty, pk_s, pk_r,
    send1, recv1, send2, recv2, rsend1, rret1, rsend2, rret2,
    pt, qt, ohp_lo, fz_ref, ks, fxs, mmat, pack, ext, vt, wsend, wrecv, wb, pair_r, jt, it, aj, hrow, hacc, hrecv, heat, lsem, ssem, rsem,
):
    S = lax.axis_index("sph")
    F = lax.axis_index("fv")
    sn, sp = (S + 1) % NS, (S + NS - 1) % NS
    fn, fp = (F + 1) % NF, (F + NF - 1) % NF

    small = [
        pltpu.make_async_copy(a, b, lsem.at[3 + n]) for n, (a, b) in enumerate((
            (h_ipart, ipart), (h_temp16, temp16), (h_iown, iown), (h_icell, icell), (h_pos, pos), (h_temp1, temp1),
            (h_vol, vol), (h_nbr, nbr), (h_cnt, cnt), (h_lcell, lcell), (h_lpow, lpow)))
    ]
    for c in small:
        c.start()

    lc = [
        pltpu.make_async_copy(sub.at[0], surf, lsem.at[0]),
    ]
    for t in range(2):
        at = pl.ds(t * 128, 128)
        lc += [
            pltpu.make_async_copy(
                sub.at[pl.ds(1, GZ - 1), :, at], U0.at[pl.ds(1, GZ - 1), t, pl.ds(0, CX)], lsem.at[1 + t]),
            pltpu.make_async_copy(cond.at[:, :, at], C.at[pl.ds(0, GZ), t, pl.ds(0, CX)], lsem.at[14 + t]),
        ]
    for c in lc:
        c.start()

    barrier = pltpu.get_barrier_semaphore()
    partners = [(S, (F + d) % NF) for d in range(1, NF)]
    partners += [((S + d) % NS, F) for d in range(1, NS)]
    partners += [(sn, fn), (sn, fp), (sp, fn), (sp, fp)]
    for who in partners:
        pl.semaphore_signal(barrier, inc=1, device_id=who, device_id_type=MESH)

    count = [0]

    def remote(src, dst, who, i=None):
        if i is None:
            i = count[0]
            count[0] += 1
        c = pltpu.make_async_remote_copy(
            src_ref=src, dst_ref=dst, send_sem=ssem.at[i], recv_sem=rsem.at[i],
            device_id=who, device_id_type=MESH)
        c.start()
        return c

    for c in small:
        c.wait()

    def group():
        count[0] += 1
        return count[0] - 1

    def all_of(src, dst, i):
        return pltpu.make_async_remote_copy(
            src_ref=src, dst_ref=dst, send_sem=ssem.at[i], recv_sem=rsem.at[i],
            device_id=(sn, F), device_id_type=MESH)

    pack[...] = jnp.concatenate([pos[...], temp1[...], vol[...], jnp.zeros((3, PD), F32)], 0)

    wsend[...] = live_weights(nbr, cnt, S * NF + F)

    own = iown[...]
    row_of = (own % NF) * NS + own // NF
    part = ipart[...]
    php = hot16(16, part // 128)
    ohp_lo[...] = hot16(128, part % 128)
    tval = sum(dot(t, php, 0, 0) for t in split2(temp16[...]))
    tval = jnp.sum(keep(128, part % 128, tval), axis=0, keepdims=True)
    pb = hot16(128, row_of)
    pt[...] = pb
    tri = jnp.where(iota((256, 256), 0) < iota((256, 256), 1), 1.0, 0.0).astype(BF)
    ones = jnp.ones((256, 256), BF)
    run = jnp.zeros((128, 256), F32)
    ranks = []
    for k in range(NE // 256):
        pc = pb[:, k * 256:(k + 1) * 256]
        cum = dot(pc, tri, 1, 0) + run
        run = run + dot(pc, ones, 1, 0)
        ranks.append(jnp.sum(keep(128, row_of[:, k * 256:(k + 1) * 256], cum), axis=0, keepdims=True))
    rank = jnp.concatenate(ranks, 1)
    q = jnp.where(iota((CAP, NE), 0).astype(F32) == rank, 1.0, 0.0)
    qt[...] = q
    c1 = icell[...] + 1
    chi = (c1 // 256 * 256).astype(F32)
    clo = (c1 % 256).astype(F32)
    v0, v1 = split2(tval)
    zero = jnp.zeros((96, NE), BF)

    def rows(a, b):
        return jnp.concatenate([jnp.concatenate([a, b], 0).astype(BF), zero], 0)

    send1[...] = (
        dot(pb, rows(q * chi, q * v0.astype(F32)), 1, 1)
        + dot(pb, rows(q * clo, q * v1.astype(F32)), 1, 1)
    )

    pl.semaphore_wait(barrier, len(partners))

    ph1_i = group()
    for d in range(1, NF):
        f = (F + d) % NF
        remote(send1.at[pl.ds(pl.multiple_of(f * NS, NS), NS)], recv1.at[F], (S, f), ph1_i)
    recv1[pl.ds(F, 1)] = send1[pl.ds(pl.multiple_of(F * NS, NS), NS)].reshape(1, NS, 128)

    nxt = ((S + (F + 1) // NF) % NS, fn)
    prv = ((S + NS - (NF - F) // NF) % NS, fp)
    pcs = [remote(pack, ext.at[1], prv), remote(wsend, wrecv, prv)]
    ext[0] = pack[...]

    for c in lc:
        c.wait()
    U0[GZ] = jnp.zeros((2, RX, 128), F32)
    U1[GZ] = jnp.zeros((2, RX, 128), F32)
    C[GZ] = jnp.zeros((2, BX, 128), F32)
    def packed(src, lo, hi):
        n = hi - lo
        l = iota((n, 128), 1)
        halves = []
        for half in range(2):
            acc = jnp.zeros((n, 128), F32)
            for w in range(16):
                z = half * 16 + w
                x = jnp.where(l < 64, src[z, 0, lo:hi], src[z, 1, lo:hi])
                acc = jnp.where(l // 8 == w, pltpu.roll(x, (8 * w + 4) % 128, 1), acc)
            halves.append(acc)
        return jnp.concatenate(halves, 1)

    for a in range(2):
        pk_s[a] = packed(U0 if a == 0 else C, 0, CX)
    heat_prep(ext, vt, jt, it, aj, hrow, (0,))
    hacc[...] = jnp.zeros((2 * NB, 8, PB), F32)
    sub8 = iota((NB, 16), 0)
    one8 = jnp.ones((NB, 128), BF)

    def spread_weights(w, base):
        for b in range(NB):
            wb[base + b] = dot(jnp.where(sub8 == b, w, 0.0).astype(BF), one8, 0, 0)

    spread_weights(wsend[:, NB:NB + 16], 0)
    heat_own(wb, pair_r, vt, jt, it, aj, hrow, hacc, 0, NB // 2, 5)

    ph1 = [all_of(send1.at[pl.ds(0, 7 * NS)], recv1.at[pl.ds(0, NF - 1)], ph1_i)]
    for c in ph1:
        c.wait_recv()
    send2[...] = jnp.swapaxes(recv1[...], 0, 1)
    ph2_i = group()
    for d in range(1, NS):
        s = (S + d) % NS
        remote(send2.at[s], recv2.at[S], (s, F), ph2_i)
    recv2[pl.ds(S, 1)] = send2[pl.ds(S, 1)]

    halo = []
    for src, dst, lo in ((sub, U0, 1), (cond, C, 0)):
        layers_ = pl.ds(lo, GZ - lo)
        for t in range(2):
            at = pl.ds(t * 128, 128)
            halo.append(remote(src.at[layers_, pl.ds(0, 4), at], dst.at[layers_, t, pl.ds(32, 4)], (sp, F)))
            halo.append(remote(src.at[layers_, pl.ds(28, 4), at], dst.at[layers_, t, pl.ds(36, 4)], (sn, F)))
    for a in range(2):
        halo += faces(remote, pk_s.at[a], pk_s.at[a], pk_r.at[a, 1], pk_r.at[a, 0], S, F, sn, sp, fn, fp)

    heat_own(wb, pair_r, vt, jt, it, aj, hrow, hacc, NB // 2, NB, 4)
    for c in pcs:
        c.wait_recv()
    heat_prep(ext, vt, jt, it, aj, hrow, (1,))
    spread_weights(wrecv[:, 0:16], NB)
    heat_next(wb, pair_r, vt, jt, it, aj, hrow, hacc, 0, 2)

    ph2 = [all_of(send2.at[pl.ds(0, NS - 1)], recv2.at[pl.ds(0, NS - 1)], ph2_i)]
    for c in ph2:
        c.wait_recv()
    rt = jnp.transpose(recv2[...].reshape(128, 128))
    cf = jnp.concatenate([rt[s:s + 1, :] for s in range(CAP)], 1)
    tf = jnp.concatenate([rt[CAP + s:CAP + s + 1, :] for s in range(CAP)], 1)
    ci = cf.astype(jnp.int32) - 1
    live = ci >= 0
    hi = jnp.where(live, ci // 256 + (ci % 256) // 128 * CX, -1)
    lo = jnp.where(live, ci % 128, -1)
    sf = surf[...]
    ss = jnp.concatenate(split2(jnp.concatenate([sf[:, 0:128], sf[:, 128:256]], 0)), 0)
    cons = []
    W = 512
    for k in range(2048 // W):
        sl = slice(k * W, (k + 1) * W)
        ob = hot16(64, hi[:, sl])
        g = dot(ss, jnp.concatenate([ob, ob], 0), 0, 0)
        ghost = jnp.sum(keep(128, lo[:, sl], g), axis=0, keepdims=True)
        cons.append(jnp.where(live[:, sl], CONTACT_GAIN * (tf[:, sl] - ghost), 0.0))
    lc_ = lcell[...]
    lx, ly = lc_ // (NF * CY), lc_ % (NF * CY)
    mine = (lx // CX == S) & (ly // CY == F)
    lhi = jnp.where(mine, lx % CX + (ly % CY) // 128 * CX, -1)
    llo = jnp.where(mine, ly % 128, -1)
    fl = jnp.zeros((128, 128), F32)
    parts = [(hi[:, k * W:(k + 1) * W], lo[:, k * W:(k + 1) * W], cons[k]) for k in range(2048 // W)]
    for h, l, value in parts + [(lhi, llo, lpow[...])]:
        ch = jnp.concatenate([keep16(64, h, v) for v in split2(value)], 0)
        fl = fl + dot(ch, hot16(128, l), 1, 1)
    fl = fl[0:64] + fl[64:128]
    top[0] = sf[:, 0:128] + SURFACE_GAIN * fl[0:32]
    top[1] = sf[:, 128:256] + SURFACE_GAIN * fl[32:64]
    con = jnp.concatenate(cons, 1)

    th = [
        remote(top.at[:, pl.ds(0, 4)], U0.at[0, :, pl.ds(32, 4)], (sp, F)),
        remote(top.at[:, pl.ds(28, 4)], U0.at[0, :, pl.ds(36, 4)], (sn, F)),
    ]
    th += faces(remote, top.at[0], top.at[1], ty.at[1], ty.at[0], S, F, sn, sp, fn, fp)

    back = jnp.concatenate([con[:, s * 128:(s + 1) * 128] for s in range(CAP)] + [jnp.zeros((112, 128), F32)], 0)
    rsend1[...] = jnp.transpose(back).reshape(NS, NF, 128)
    rh1_i = group()
    for d in range(1, NS):
        s = (S + d) % NS
        remote(rsend1.at[s], rret1.at[S], (s, F), rh1_i)
    rret1[pl.ds(S, 1)] = rsend1[pl.ds(S, 1)]

    heat_next(wb, pair_r, vt, jt, it, aj, hrow, hacc, 2, NB // 2)
    hc = remote(hacc.at[pl.ds(NB, NB)], hrecv, nxt)

    for c in halo:
        c.wait_recv()
    row = iota((BX, CY), 0)
    lane = iota((BX, CY), 1)
    up = (S > 0).astype(F32)
    down = (S < NS - 1).astype(F32)
    rmask = jnp.where(row < 32, 1.0, jnp.where(row < 36, down, up))
    smask = [
        rmask * jnp.where(lane % 8 < 4, (F > 0).astype(F32), 1.0),
        rmask * jnp.where(lane % 8 < 4, 1.0, (F < NF - 1).astype(F32)),
    ]
    xmask = rmask[32:40, 0:128]

    @pl.when(S == 0)
    def _():
        U0[1:GZ, :, 36:40, :] = jnp.zeros((GZ - 1, 2, 4, 128), F32)
        C[0:GZ, :, 36:40, :] = jnp.zeros((GZ, 2, 4, 128), F32)

    @pl.when(S == NS - 1)
    def _():
        U0[1:GZ, :, 32:36, :] = jnp.zeros((GZ - 1, 2, 4, 128), F32)
        C[0:GZ, :, 32:36, :] = jnp.zeros((GZ, 2, 4, 128), F32)

    for c in th:
        c.wait_recv()
    U0[0, :, 0:CX] = top[...]
    U0[0, :, 32:40] = U0[0, :, 32:40] * xmask
    U0[0:GZ, :, 40:41] = U0[0:GZ, :, 0:1]
    zero_z = lane < 8
    l128 = iota((BX, 128), 1)
    for a in range(2):
        src = U0 if a == 0 else C
        mine_ = jnp.concatenate([pk_s[a], packed(src, 32, 40)], 0)
        for side in range(2):
            first = (pk_r[a, side], mine_) if side == 0 else (mine_, pk_r[a, side])
            v = jnp.where(lane % 8 < 4, first[0], first[1])
            if a == 0:
                o = U0[0, side, 0:BX]
                near = (o, ty[side]) if side == 0 else (ty[side], o)
                near = pltpu.roll(jnp.where(l128 < 64, near[0], near[1]), 4, 1)
                v = jnp.where(zero_z, jnp.concatenate([near, near], 1), v)
                su[side] = v * smask[side]
            else:
                sc[side] = v * smask[side]

    G = LAMBDA_STEP * 0.5
    Us = (U0, U1)

    def conductivity(u, c):
        return c * (G + (0.5 * G) * jnp.tanh(u))

    def along_x(u, k):
        fx = (k + pltpu.roll(k, BX - 1, 0)) * (pltpu.roll(u, BX - 1, 0) - u)
        return fx - pltpu.roll(fx, 1, 0)

    lane1 = iota((BX, 128), 1)
    first_lane, last_lane = lane1 == 0, lane1 == 127
    r256, c256 = iota((CY, CY), 0), iota((CY, CY), 1)
    mmat[...] = (jnp.where(r256 == c256, 1.0, 0.0) - jnp.where(r256 + 1 == c256, 1.0, 0.0)).astype(BF)
    for step in range(SUB):
        a, b = step % 2, 1 - step % 2
        last = step == SUB - 1
        for side in range(2):
            u, c = su[side], sc[side]
            k = conductivity(u, c)
            fy = (k + pltpu.roll(k, CY - 1, 1)) * (pltpu.roll(u, CY - 1, 1) - u)
            if side == 0:
                face = pltpu.roll(fy, 1, 1)
            else:
                face = jnp.where(lane % 8 == 4, face, fy)
                fs[0] = face[:, 0:128]
                fs[1] = face[:, 128:256]
            if not last:
                below = lane >= CY - 8
                un = jnp.where(below, 0.0, pltpu.roll(u, CY - 8, 1))
                kn = jnp.where(below, k, pltpu.roll(k, CY - 8, 1))
                fz = (k + kn) * (un - u)
                fup = jnp.where(lane < 8, 0.0, pltpu.roll(fz, 8, 1))
                net = (fy - pltpu.roll(fy, 1, 1)) + (fz - fup) + along_x(u, k)
                su[side] = (u + net) * smask[side]

        for t in range(2):
            k0 = conductivity(Us[a][0, t, 0:BX], C[0, t])
            ks[0, t, 0:BX] = k0
            ks[0, t, 40:41] = k0[0:1]
        fz_ref[...] = jnp.zeros((2, BX, 128), F32)

        def layers(n, _):
            minus_left = mmat[...]
            z0 = n * GROUP
            both = range(2)
            k = [ks[0, t, 0:BX] for t in both]
            fz0 = [fz_ref[t] for t in both]
            u = [Us[a][z0, t, 0:BX] for t in both]
            for m in range(GROUP):
                z = z0 + m
                un = [Us[a][z + 1, t, 0:BX] for t in both]
                kn = [conductivity(un[t], C[z + 1, t]) for t in both]
                w = z % 16
                edge = pltpu.roll(fs[z // 16], (124 + 128 - 8 * w) % 128, 1)
                sk = [pltpu.roll(v, 127, 1) for v in k]
                su_ = [pltpu.roll(v, 127, 1) for v in u]
                fyl = (k[0] + jnp.where(last_lane, sk[1], sk[0])) * (jnp.where(last_lane, su_[1], su_[0]) - u[0])
                fyr = jnp.where(last_lane, edge, (k[1] + sk[1]) * (su_[1] - u[1]))
                hi = [v.astype(BF) for v in (fyl, fyr)]
                low = [(v - h.astype(F32)).astype(BF) for v, h in zip((fyl, fyr), hi)]
                twice = dot(jnp.concatenate([jnp.concatenate(hi, 1), jnp.concatenate(low, 1)], 0), minus_left, 1, 0)
                ny = twice[0:BX] + twice[BX:2 * BX]
                ny = [ny[:, 0:128] - jnp.where(first_lane, edge, 0.0), ny[:, 128:256]]
                fzs = []
                for t in both:
                    fx = (k[t] + ks[m, t, 1:41]) * (Us[a][z, t, 1:41] - u[t])
                    fxs[m, t, 8:48] = fx
                    fxs[m, t, 7:8] = fx[39:40]
                    kf = jnp.where(z == GZ - 1, k[t], kn[t]) if m == GROUP - 1 else kn[t]
                    fz = (k[t] + kf) * (un[t] - u[t])
                    new = u[t] + ((fx - fxs[m, t, 7:47]) + (fz - fz0[t]) + ny[t])
                    if last:
                        outv[z, :, t * 128:(t + 1) * 128] = new[0:CX]
                    else:
                        Us[b][z, t, 0:CX] = new[0:CX]
                        Us[b][z, t, 32:40] = new[32:40] * xmask
                        Us[b][z, t, 40:41] = new[0:1]
                    fzs.append(fz)
                    slot = (m + 1) % GROUP
                    ks[slot, t, 0:BX] = kn[t]
                    ks[slot, t, 40:41] = kn[t][0:1]
                u, k, fz0 = un, kn, fzs
            for t in both:
                fz_ref[t] = fz0[t]
            return 0

        lax.fori_loop(0, GZ // GROUP, layers, 0)

        if step == 1:
            rh1 = [all_of(rsend1.at[pl.ds(0, NS - 1)], rret1.at[pl.ds(0, NS - 1)], rh1_i)]
            for c in rh1:
                c.wait_recv()
            rsend2[...] = jnp.swapaxes(rret1[...], 0, 1)
            rh2_i = group()
            for d in range(1, NF):
                f = (F + d) % NF
                remote(rsend2.at[f], rret2.at[F], (S, f), rh2_i)
            rret2[pl.ds(F, 1)] = rsend2[pl.ds(F, 1)]

    rh2 = [all_of(rsend2.at[pl.ds(0, NF - 1)], rret2.at[pl.ds(0, NF - 1)], rh2_i)]
    for c in rh2:
        c.wait_recv()
    rr = rret2[...].reshape(128, 128)[:, 0:CAP]
    x = sum(dot(v, pt[...], 0, 0) for v in split2(rr))
    cval = jnp.sum(x * qt[...], axis=0, keepdims=True)
    ph = ipart[...] // 128
    pf = sum(dot(keep16(16, ph, v), ohp_lo[...], 1, 1) for v in split2(cval))
    pflux = jnp.concatenate([pf[r:r + 1, :] for r in range(16)], 1)
    hc.wait_recv()
    for b in range(NB):
        h8 = hacc[b] + hrecv[b]
        warm, amount = h8[0:1] + h8[1:2] + h8[2:3], h8[3:4] + h8[4:5] + h8[5:6]
        at = slice(b * PB, (b + 1) * PB)
        heat[:, at] = warm - temp1[:, at] * amount
    pout[...] = temp1[...] + SPH_STEP * heat[...] - PARTICLE_SHARE * pflux

    for c in [hc] + ph1 + pcs + halo + ph2 + th + rh1 + rh2:
        c.wait_send()


UNROLL = 8


def groups3(x):
    a = x.astype(BF).astype(F32)
    r = x - a
    b = r.astype(BF).astype(F32)
    return [a, b, r - b]


def heat_prep(ext, vt, jt, it, aj, hrow, which):
    scale = (LOG2E * 2.0 * KERNEL_SCALE) ** 0.5
    r32, c256 = iota((32, 256), 0), iota((32, 256), 1)
    rep = jnp.where((c256 < 72) & (c256 % 24 == r32), 1.0, 0.0)
    tail = jnp.where((c256 >= 128) & (r32 >= 24) & (r32 < 27), 1.0, 0.0)
    spread = (rep + tail).astype(BF)
    row = iota((8, PB), 0)

    def place(*rows):
        out = jnp.zeros((8, PB), F32)
        for n, r in enumerate(rows):
            out = jnp.where(row == n, r, out)
        return out

    for t in which:
        def prep(n, _):
            for m in range(UNROLL):
                b = n * UNROLL + m
                at = pl.ds(pl.multiple_of(b * PB, PB), PB)
                blk = ext[t, :, at]
                p = jnp.where(row < 3, blk * scale, 0.0)
                norm = -0.5 * jnp.sum(p * p, axis=0, keepdims=True)
                temp = blk[3:4]
                volume = blk[4:5] * (2.0 * KERNEL_SCALE)
                half = 0.5 / (1.0 + 0.5 * jnp.tanh(temp))
                packed = groups3(place(half, volume * temp, volume))
                vt[t * NB + b] = place(
                    packed[0][1:2], packed[1][1:2], packed[2][1:2], packed[0][2:3], packed[1][2:3], packed[2][2:3])
                ah = place(packed[0][0:1], packed[1][0:1], packed[2][0:1])
                sj = groups3(jnp.where(row == 3, norm, jnp.where(row == 4, 1.0, p)))
                both = dot(jnp.concatenate(sj + [ah], 0).astype(BF), spread, 0, 0)
                jt[t * NB + b] = both[:, 0:128].astype(BF)
                aj[t * NB + b] = both[:, 128:256]
                if t == 0:
                    hrow[b] = jnp.broadcast_to(half, (8, PB))
                    i0, i1, i2 = groups3(jnp.where(row == 3, 1.0, jnp.where(row == 4, norm, p)))
                    z = jnp.zeros((128 - 72, PB), F32)
                    it[b] = jnp.concatenate([i0, i0, i0, i1, i1, i1, i2, i2, i2, z], 0).astype(BF)
            return 0

        lax.fori_loop(0, NB // UNROLL, prep, 0)


def live_weights(nbr, cnt, device):
    local = nbr[...] - (device - 1) * NB
    eq = iota((NB, NB), 0) == iota((NB, NB), 1)
    count = jnp.sum(jnp.where(eq, jnp.broadcast_to(cnt[...], (NB, NB)).astype(F32), 0.0), axis=1, keepdims=True)
    w = jnp.zeros((NB, 128), F32)
    at = iota((NB, 128), 1)
    for s in range(KN):
        live = jnp.where(count > s, 1.0, 0.0)
        w = w + jnp.where(at == local[:, s:s + 1], live, 0.0)
    return w


def pair_block(pair_r, n, jt, it, aj, hrow, o, b):
    e = dot(jt[o], it[b], 1, 0)
    a = aj[o]
    half = hrow[b, 0:1, :]
    for h in range(2):
        sl = slice(h * 128, (h + 1) * 128)
        q = (a + half[:, sl]).reshape(PB // 16, 2, 8, 128)
        q0, q1 = q[:, 0], q[:, 1]
        inv = 1.0 / (q0 * q1)
        f = jnp.stack([q1 * inv, q0 * inv], 1).reshape(PB, 128)
        pair_r[n * PB:(n + 1) * PB, sl] = (jnp.exp2(e[:, sl]) * f).astype(BF)


def weighted(wb, vt, to, of):
    w = wb[to, pl.ds(of, 1), :]
    return vt[of] * jnp.concatenate([w, w], 1)


def heat_own(wb, pair_r, vt, jt, it, aj, hrow, acc, start, stop, turns):
    def two_blocks(g, _):
        mine = [start + 2 * g, start + 2 * g + 1]
        others = [[(b + d) % NB for d in range(turns)] for b in mine]
        for q, b in enumerate(mine):
            for n, o in enumerate(others[q]):
                pair_block(pair_r, q * turns + n, jt, it, aj, hrow, o, b)
        for q, b in enumerate(mine):
            left = jnp.concatenate([weighted(wb, vt, b, o) for o in others[q]], 1).astype(BF)
            acc[b] += dot(left, pair_r[q * turns * PB:(q + 1) * turns * PB], 1, 0)
            for n in range(1, turns):
                o, at = others[q][n], q * turns + n
                acc[o] += dot(weighted(wb, vt, o, b).astype(BF), pair_r[at * PB:(at + 1) * PB], 1, 1)
        return 0

    lax.fori_loop(0, (stop - start) // 2, two_blocks, 0)


def heat_next(wb, pair_r, vt, jt, it, aj, hrow, acc, start, stop):
    pairs = []
    for i in range(start, stop):
        pairs += [(i, NB + o) for o in range(i + 1)]
        pairs += [(NB - 1 - i, NB + o) for o in range(NB - i)]
    for n, (b, o) in enumerate(pairs):
        pair_block(pair_r, n, jt, it, aj, hrow, o, b)
    first = 0
    for i in range(start, stop):
        for b in (i, NB - 1 - i):
            last = first + b + 1
            left = jnp.concatenate([weighted(wb, vt, b, NB + o) for o in range(b + 1)], 1).astype(BF)
            acc[b] += dot(left, pair_r[first * PB:last * PB], 1, 0)
            first = last
    for n, (b, o) in enumerate(pairs):
        acc[o] += dot(weighted(wb, vt, o, b).astype(BF), pair_r[n * PB:(n + 1) * PB], 1, 1)


COPIES = 4 + 3 + 8 + 12 + 8


def main_call(nbr, cnt, *args):
    vm = pl.BlockSpec(memory_space=pltpu.VMEM)
    hbm = pl.BlockSpec(memory_space=pltpu.HBM)
    s = lambda *shape: pltpu.VMEM(shape, F32)
    i = lambda *shape: pltpu.VMEM(shape, jnp.int32)
    return pl.pallas_call(
        main_kernel,
        out_shape=[
            jax.ShapeDtypeStruct((GZ, CX, CY), F32),
            jax.ShapeDtypeStruct((1, PD), F32),
        ],
        in_specs=[hbm] * 13,
        out_specs=[vm, vm],
        scratch_shapes=[
            i(NB, KN), i(1, NB), s(3, PD), s(1, PD), s(16, 128), s(1, PD), i(1, NE), i(1, NE), i(1, NE),
            i(1, 256), s(1, 256),
            s(GZ + 1, 2, RX, 128), s(GZ + 1, 2, RX, 128), s(GZ + 1, 2, BX, 128), s(2, BX, CY), s(2, BX, CY),
            s(2, BX, 128), s(CX, CY), s(2, CX, 128), s(2, BX, 128),
            s(2, CX, CY), s(2, 2, BX, CY),
            s(128, 128), s(NF, NS, 128), s(NS, NF, 128), s(NS, NF, 128),
            s(NS, NF, 128), s(NS, NF, 128), s(NF, NS, 128), s(NF, NS, 128),
            pltpu.VMEM((128, NE), BF), s(CAP, NE), pltpu.VMEM((128, NE), BF),
            s(2, BX, 128), s(GROUP, 2, RX, 128), s(GROUP, 2, RX, 128), pltpu.VMEM((CY, CY), BF), s(8, PD), s(2, 8, PD), s(2 * NB, 8, PB), s(NB, 128), s(NB, 128), s(2 * NB, 16, 128),
            pltpu.VMEM((18 * PB, PB), BF),
            pltpu.VMEM((2 * NB, PB, 128), BF), pltpu.VMEM((NB, 128, PB), BF),
            s(2 * NB, PB, 128), s(NB, 8, PB), s(2 * NB, 8, PB), s(NB, 8, PB), s(1, PD),
            pltpu.SemaphoreType.DMA((16,)),
            pltpu.SemaphoreType.DMA((COPIES,)),
            pltpu.SemaphoreType.DMA((COPIES,)),
        ],
        compiler_params=pltpu.CompilerParams(
            collective_id=0, has_side_effects=True, vmem_limit_bytes=32 * 2**20),
        name="step",
    )(*(pltpu.with_memory_space_constraint(x, pltpu.HBM) for x in (nbr, cnt) + args))


def body(positions, particle_temp, volume, nbr_blocks, nbr_count, iface_part, iface_owner,
         iface_cell, substrate_temp, conduct, laser_cells, laser_power):
    field, particle_out = main_call(
        nbr_blocks, nbr_count.reshape(1, NB), positions, particle_temp.reshape(1, PD), particle_temp.reshape(16, 128), volume.reshape(1, PD),
        iface_part.reshape(1, NE), iface_owner.reshape(1, NE), iface_cell.reshape(1, NE),
        laser_cells.reshape(1, -1), laser_power.reshape(1, -1), substrate_temp, conduct)
    return particle_out.reshape(PD), field


def solution(mesh):
    in_specs = (
        P(None, ("sph", "fv")),
        P(("sph", "fv")),
        P(("sph", "fv")),
        P(("sph", "fv"), None),
        P(("sph", "fv")),
        P(("sph", "fv")),
        P(("sph", "fv"), None),
        P(("sph", "fv")),
        P(None, "sph", "fv"),
        P(None, "sph", "fv"),
        P(),
        P(),
    )
    out_specs = (P(("sph", "fv")), P(None, "sph", "fv"))
    return jax.shard_map(body, mesh=mesh, in_specs=in_specs, out_specs=out_specs, check_vma=False)
```
